32 devices in a mesh: dp: 16 (over z, y, core), tensor: 2 (over x).
Axes of the slice: x: 2, y: 2, z: 4, core: 2. Of those that a mesh axis runs over, the one named last changes fastest.
Arguments:
- video_in: bfloat16 [32, 256, 1152], P('dp', 'tensor'), may hold values from -15 to 15
- condition: float32 [2, 1152], replicated, may hold values from -5 to 5
- adaln_spatial: bfloat16 [1152, 6, 1152], P('dp'), may hold values from -0.1875 to 0.1875
- qkv_spatial: bfloat16 [1152, 3, 1152], P('dp', None, 'tensor'), may hold values from -0.1875 to 0.1875
- proj_spatial: bfloat16 [1152, 1152], P('tensor', 'dp'), may hold values from -1.5 to 1.5
- up_spatial: bfloat16 [1152, 4608], P('dp', 'tensor'), may hold values from -0.1875 to 0.1875
- down_spatial: bfloat16 [4608, 1152], P('tensor', 'dp'), may hold values from -0.09375 to 0.09375
- adaln_temporal: bfloat16 [1152, 6, 1152], P('dp'), may hold values from -0.1875 to 0.1875
- qkv_temporal: bfloat16 [1152, 3, 1152], P('dp', None, 'tensor'), may hold values from -0.1875 to 0.1875
- proj_temporal: bfloat16 [1152, 1152], P('tensor', 'dp'), may hold values from -0.5 to 0.5
- up_temporal: bfloat16 [1152, 4608], P('dp', 'tensor'), may hold values from -0.1875 to 0.1875
- down_temporal: bfloat16 [4608, 1152], P('tensor', 'dp'), may hold values from -0.09375 to 0.09375
- grad_output: float32 [32, 256, 1152], P('dp', 'tensor'), may hold values from -6 to 6
Outputs:
- video_out: bfloat16 [32, 256, 1152], P('dp', 'tensor')
- video_grad: float32 [32, 256, 1152], P('dp', 'tensor')
- condition_grad: float32 [2, 1152], P(None, 'dp')
- adaln_spatial_grad: float32 [1152, 6, 1152], P('dp')
- qkv_spatial_grad: float32 [1152, 3, 1152], P('dp', None, 'tensor')
- proj_spatial_grad: float32 [1152, 1152], P('tensor', 'dp')
- up_spatial_grad: float32 [1152, 4608], P('dp', 'tensor')
- down_spatial_grad: float32 [4608, 1152], P('tensor', 'dp')
- adaln_temporal_grad: float32 [1152, 6, 1152], P('dp')
- qkv_temporal_grad: float32 [1152, 3, 1152], P('dp', None, 'tensor')
- proj_temporal_grad: float32 [1152, 1152], P('tensor', 'dp')
- up_temporal_grad: float32 [1152, 4608], P('dp', 'tensor')
- down_temporal_grad: float32 [4608, 1152], P('tensor', 'dp')
- frame_rms: float32 [8, 16], replicated
- shift_grad: float32 [4, 2, 1152], replicated
The draws below stay inside these ranges and needn't reach their ends.
All inputs are finite; a program needn't handle non-finite values.
Results may differ from the reference program's by a relative error of at most 0.024.
Values may be sent and summed in bfloat16 or wider, within the bound.
A program may use at most 256 MiB of HBM per device.

```python
import math
import jax
import jax.numpy as jnp
from jax import lax

D = 1152
HEADS = 16
HEAD_DIM = 72
FF = 4608
PATCHES = 256
FRAMES = 16
CLIPS = 2
FRAME_ROWS = 32
SLAB = 128


def draw_video_in(key, part):
    row_index = jnp.arange(FRAME_ROWS, dtype=jnp.int32)[:, None, None]
    place_index = jnp.arange(PATCHES, dtype=jnp.int32)[None, :, None]
    frame_pos = (row_index // CLIPS).astype(jnp.float32) / (FRAMES - 1)
    place_pos = (place_index % SLAB).astype(jnp.float32) / max(SLAB - 1, 1)
    noise_field = jnp.clip(jax.random.normal(key, (FRAME_ROWS, PATCHES, D), jnp.float32), -5.0, 5.0)
    row_scale = jnp.exp(math.log(3.0) * (frame_pos - 0.5)) * jnp.exp(math.log(3.0) * (place_pos - 0.5))
    return (noise_field * row_scale).astype(jnp.bfloat16)


def block_scale(stream_key, shape, cuts, low, top_value):
    factor_of = 1.0
    for position, parts in cuts:
        draws = jax.random.uniform(jax.random.fold_in(jax.random.fold_in(stream_key, 6), position), (parts,), jnp.float32, low / len(cuts), top_value / len(cuts))
        factor_of = factor_of * jnp.repeat(jnp.exp(draws), shape[position] // parts).reshape((-1,) + (1,) * (len(shape) - 1 - position))
    return factor_of


def noise(own_key, extent, width, most, cuts=(), kind=jnp.bfloat16):
    loudness = block_scale(own_key, extent, cuts, -0.22, 0.18) if cuts else 1.0
    entries = jax.random.normal(own_key, extent, jnp.float32) * width * loudness
    return jnp.minimum(jnp.maximum(entries, -most), most).astype(kind)


def setup_inputs(seed: int = 0) -> dict:
    key_of = jax.random.split(jax.random.key(seed), 14)
    video_in = draw_video_in(jax.random.fold_in(key_of[13], 71), 0)
    condition = noise(key_of[1], (CLIPS, D), 1.0, 5.0, (), jnp.float32)
    adaln_spatial = noise(key_of[2], (D, 6, D), D ** -0.5, 0.1875, ((0, 16),))
    qkv_spatial = noise(key_of[3], (D, 3, D), D ** -0.5, 0.1875, ((0, 16), (2, 2)))
    proj_spatial = noise(key_of[4], (D, D), (D // 64) ** -0.5, 1.5, ((0, 2), (1, 16)))
    up_spatial = noise(key_of[5], (D, FF), D ** -0.5, 0.1875, ((0, 16), (1, 2)))
    down_spatial = noise(key_of[6], (FF, D), FF ** -0.5, 0.09375, ((0, 2), (1, 16)))
    adaln_temporal = noise(key_of[7], (D, 6, D), D ** -0.5, 0.1875, ((0, 16),))
    qkv_temporal = noise(key_of[8], (D, 3, D), D ** -0.5, 0.1875, ((0, 16), (2, 2)))
    proj_temporal = noise(key_of[9], (D, D), (D // 8) ** -0.5, 0.5, ((0, 2), (1, 16)))
    up_temporal = noise(key_of[10], (D, FF), D ** -0.5, 0.1875, ((0, 16), (1, 2)))
    down_temporal = noise(key_of[11], (FF, D), FF ** -0.5, 0.09375, ((0, 2), (1, 16)))
    grad_output = noise(key_of[12], (FRAME_ROWS, PATCHES, D), 1.0, 6.0, ((0, 16), (1, 2)), jnp.float32)
    return dict(video_in=video_in, condition=condition, adaln_spatial=adaln_spatial, qkv_spatial=qkv_spatial, proj_spatial=proj_spatial, up_spatial=up_spatial, down_spatial=down_spatial, adaln_temporal=adaln_temporal, qkv_temporal=qkv_temporal, proj_temporal=proj_temporal, up_temporal=up_temporal, down_temporal=down_temporal, grad_output=grad_output)


highest = lax.Precision.HIGHEST
epsilon = 1e-06

@jax.custom_vjp
def low(v):
    return lax.optimization_barrier(v.astype(jnp.bfloat16)).astype(jnp.float32)

@jax.custom_vjp
def low_back(v):
    return v

def low_keep(v):
    return (low(v), None)

def low_pass(kept, grad):
    return (grad,)

def back_keep(v):
    return (v, None)

def back_low(kept, grad):
    return (low(grad),)
low.defvjp(low_keep, low_pass)
low_back.defvjp(back_keep, back_low)

def layer_norm(stream):
    average = lax.optimization_barrier(jnp.mean(stream, axis=-1, keepdims=True))
    centered = stream - average
    return centered * lax.rsqrt(lax.optimization_barrier(jnp.mean(centered * centered, axis=-1, keepdims=True)) + epsilon)

def modulation(conditioning, adaln_w):
    silu_cond = low(jax.nn.silu(conditioning))
    flat = jnp.dot(silu_cond, adaln_w.reshape(adaln_w.shape[0], -1), precision=highest)
    return flat.reshape(conditioning.shape[0], 6, -1)

def spatial_block(block_in):
    queries, key_rows, values = block_in
    raw_scores = jnp.einsum('fqhe,fkhe->fhqk', queries, key_rows, precision=highest)
    scores = low_back(raw_scores) * HEAD_DIM ** (-0.5)
    attn_probs = low(jax.nn.softmax(scores, axis=-1))
    return jnp.einsum('fhqk,fkhe->fqhe', attn_probs, values, precision=highest)

def spatial_mix(queries, key_rows, values):
    block_shape = (-1, FRAMES, PATCHES, HEADS, HEAD_DIM)
    result = lax.map(jax.checkpoint(spatial_block), (queries.reshape(block_shape), key_rows.reshape(block_shape), values.reshape(block_shape)))
    return result.reshape(queries.shape)

def temporal_block(block_in):
    queries, key_rows, values = block_in
    raw_scores = jnp.einsum('fphe,gphe->phfg', queries, key_rows, precision=highest)
    scores = low_back(raw_scores) * HEAD_DIM ** (-0.5)
    attn_probs = low(jax.nn.softmax(scores, axis=-1))
    return jnp.einsum('phfg,gphe->fphe', attn_probs, values, precision=highest)

def temporal_mix(queries, key_rows, values):
    swapped = tuple((jnp.swapaxes(entry, 0, 1) for entry in (queries, key_rows, values)))
    result = lax.map(jax.checkpoint(temporal_block), swapped)
    return jnp.swapaxes(result, 0, 1)

def run_layer(stream, conditioning, layer_weights, mixer_fn, shift_probe):
    adaln_w, qkv_w, proj_w, up_w, down_w = layer_weights
    modul = modulation(conditioning, adaln_w)
    pieces = [modul[None, :, None, index, :] for index in range(6)]
    shift_attn = pieces[0] + shift_probe[0][None, :, None, :]
    shift_mlp = pieces[3] + shift_probe[1][None, :, None, :]
    hidden = low(layer_norm(stream) * (1.0 + pieces[1]) + shift_attn)
    mixed_qkv = low(low_back(jnp.einsum('fcpd,dkx->fcpkx', hidden, qkv_w, precision=highest)))
    head_shape = stream.shape[:3] + (HEADS, HEAD_DIM)
    queries = mixed_qkv[..., 0, :].reshape(head_shape)
    key_rows = mixed_qkv[..., 1, :].reshape(head_shape)
    values = mixed_qkv[..., 2, :].reshape(head_shape)
    attended = low(low_back(mixer_fn(queries, key_rows, values).reshape(stream.shape)))
    branch = low_back(jnp.einsum('fcpd,de->fcpe', attended, proj_w, precision=highest))
    gated_attn = pieces[2] * branch
    stream_attn = stream + gated_attn
    hidden_mlp = low(layer_norm(stream_attn) * (1.0 + pieces[4]) + shift_mlp)
    up_values = low_back(jnp.einsum('fcpd,dh->fcph', hidden_mlp, up_w, precision=highest))
    active = low(jax.nn.gelu(up_values, approximate=True))
    branch_mlp = low_back(jnp.einsum('fcph,hd->fcpd', active, down_w, precision=highest))
    gated_mlp = pieces[5] * branch_mlp
    stream_mlp = stream_attn + gated_mlp
    return (stream_mlp, (stream_attn, stream_mlp, gated_attn, gated_mlp))

def forward(video_data, conditioning, *params):
    shift_probe = params[10]
    stream = video_data.reshape(FRAMES, CLIPS, PATCHES, D)
    stream, first_set = run_layer(stream, conditioning, params[:5], spatial_mix, shift_probe[0:2])
    stream, second_set = run_layer(stream, conditioning, params[5:10], temporal_mix, shift_probe[2:4])
    tracked = first_set[:2] + second_set[:2] + first_set[2:] + second_set[2:]
    squares = jnp.stack([lax.optimization_barrier(jnp.sum(entry * entry, axis=(1, 2, 3))) for entry in tracked])
    return (stream.reshape(FRAME_ROWS, PATCHES, D), squares)

def reference(video_in, condition, adaln_spatial, qkv_spatial, proj_spatial, up_spatial, down_spatial, adaln_temporal, qkv_temporal, proj_temporal, up_temporal, down_temporal, grad_output):
    weight_list = [weight_arg.astype(jnp.float32) for weight_arg in (adaln_spatial, qkv_spatial, proj_spatial, up_spatial, down_spatial, adaln_temporal, qkv_temporal, proj_temporal, up_temporal, down_temporal)]
    video_data = video_in.astype(jnp.float32)
    conditioning = condition.astype(jnp.float32)
    shift_probe = jnp.zeros((4, CLIPS, D), jnp.float32)
    output, pullback, squares = jax.vjp(forward, video_data, conditioning, *weight_list, shift_probe, has_aux=True)
    gradients = pullback(grad_output.astype(jnp.float32))
    frame_rms = jnp.sqrt(squares / (CLIPS * PATCHES * D))
    return (output.astype(jnp.bfloat16), gradients[0], gradients[1], gradients[2], gradients[3], gradients[4], gradients[5], gradients[6], gradients[7], gradients[8], gradients[9], gradients[10], gradients[11], frame_rms, gradients[12])
```

```python
import jax
import jax.numpy as jnp
from jax import lax
from jax.sharding import PartitionSpec as P

HEAD_DIM = 72
PATCHES = 256
FRAMES = 16

highest = lax.Precision.HIGHEST
epsilon = 1e-06
bf16 = jnp.bfloat16
f32 = jnp.float32


def dot(a, b):
    return jnp.dot(a, b, preferred_element_type=f32)


def dot_nt(a, b):
    return lax.dot_general(a, b, (((1,), (1,)), ((), ())), preferred_element_type=f32)


def dot_tn(a, b):
    return lax.dot_general(a, b, (((0,), (0,)), ((), ())), preferred_element_type=f32)


def layer_norm(stream):
    average = jnp.mean(stream, axis=-1, keepdims=True)
    centered = stream - average
    inverse = lax.rsqrt(jnp.mean(centered * centered, axis=-1, keepdims=True) + epsilon)
    return (centered * inverse, inverse)


def gelu_tanh(pre_act):
    return jax.nn.gelu(pre_act, approximate=True)


def swap(value, axis, stride, size):
    return lax.ppermute(value, axis, [(i, i ^ stride) for i in range(size)])


def all_sum(value, axes):
    for axis in axes:
        size = lax.axis_size(axis)
        if size & (size - 1):
            value = lax.psum(value, axis)
            continue
        stride = 1
        while stride < size:
            value = value + swap(value, axis, stride, size)
            stride *= 2
    return value


def gather_tokens(local):
    size = lax.axis_size("tensor")
    if size == 2:
        other = swap(local, "tensor", 1, 2)
        return [local, other]
    return list(lax.all_gather(local, "tensor", axis=0, tiled=False))


def scatter_tokens(parts):
    size = lax.axis_size("tensor")
    if size == 2:
        return parts[0] + swap(parts[1].astype(bf16), "tensor", 1, 2).astype(f32)
    stacked = jnp.stack([part.astype(bf16) for part in parts])
    return lax.psum_scatter(stacked, "tensor", scatter_dimension=0, tiled=False).astype(f32)


def split_heads(values, lead):
    heads = values.shape[-1] // (3 * HEAD_DIM)
    view = values.reshape(lead + (3, heads, HEAD_DIM))
    axis = len(lead)
    return [lax.index_in_dim(view, i, axis, keepdims=False) for i in range(3)]


spatial_forms = ("aqhe,akhe->ahqk", "ahqk,akhe->aqhe", "ahqk,aqhe->akhe")
temporal_forms = ("fshe,gshe->shfg", "shfg,gshe->fshe", "shfg,fshe->gshe")


def attend(qkv, forms):
    queries, keys, values = qkv
    scores = jnp.einsum(forms[0], queries, keys, preferred_element_type=f32) * HEAD_DIM ** (-0.5)
    top = jnp.max(scores, axis=-1, keepdims=True)
    unnormed = jnp.exp(scores - top)
    total = jnp.sum(unnormed, axis=-1, keepdims=True)
    probs = (unnormed / total).astype(bf16)
    out = jnp.einsum(forms[1], probs, values, preferred_element_type=f32).astype(bf16)
    return out, top + jnp.log(total)


def attend_back(qkv, log_total, grad_out, forms):
    queries, keys, values = qkv
    scale = HEAD_DIM ** (-0.5)
    scores = jnp.einsum(forms[0], queries, keys, preferred_element_type=f32) * scale
    probs = jnp.exp(scores - log_total)
    grad_probs = jnp.einsum(forms[0], grad_out, values, preferred_element_type=f32)
    grad_scores = probs * (grad_probs - jnp.sum(probs * grad_probs, axis=-1, keepdims=True))
    grad_scaled = (grad_scores * scale).astype(bf16)
    grad_q = jnp.einsum(forms[1], grad_scaled, keys, preferred_element_type=f32)
    grad_k = jnp.einsum(forms[2], grad_scaled, queries, preferred_element_type=f32)
    grad_v = jnp.einsum(forms[2], probs.astype(bf16), grad_out, preferred_element_type=f32)
    return [grad.astype(bf16) for grad in (grad_q, grad_k, grad_v)]


class Layer:
    def __init__(self, rows, tokens, clips, spatial, first_row):
        self.rows, self.tokens, self.clips, self.spatial = rows, tokens, clips, spatial
        self.first_row = first_row

    def by_row(self, table):
        if self.rows % self.clips == 0:
            width = table.shape[-1]
            spread = jnp.broadcast_to(table[None], (self.rows // self.clips, self.clips, width))
            return spread.reshape(self.rows, 1, width)
        start = lax.rem(self.first_row, self.clips)
        return lax.dynamic_slice_in_dim(table, start, self.rows, 0)[:, None, :]

    def by_clip(self, sums):
        width = sums.shape[-1]
        if self.rows % self.clips == 0:
            return jnp.sum(sums.reshape(self.rows // self.clips, self.clips, width), axis=0)
        start = lax.rem(self.first_row, self.clips)
        empty = jnp.zeros((self.clips, width), f32)
        return lax.dynamic_update_slice_in_dim(empty, sums, start, 0)

    def by_frame(self, entries):
        per_row = jnp.sum(entries * entries, axis=(1, 2))
        frames = max(self.rows // self.clips, 1)
        sums = jnp.sum(per_row.reshape(frames, -1), axis=1)
        if frames == FRAMES:
            return sums
        start = self.first_row // self.clips
        return lax.dynamic_update_slice_in_dim(jnp.zeros((FRAMES,), f32), sums, start, 0)

    def modulated(self, stream, mod, offset):
        normed = layer_norm(stream)[0]
        scale = 1.0 + self.by_row(mod[:, offset + 1])
        return (normed * scale + self.by_row(mod[:, offset])).astype(bf16)

    def flat(self, value):
        return value.reshape(self.rows * self.tokens, value.shape[-1])

    def full(self, value):
        return value.reshape(self.rows, self.tokens, value.shape[-1])

    def sequences(self, parts):
        if self.spatial:
            joined = jnp.stack([self.full(part) for part in parts], axis=1)
            joined = joined.reshape(self.rows, -1, joined.shape[-1])
            return [split_heads(joined, joined.shape[:2])]
        return [
            split_heads(part, (FRAMES, part.shape[0] // FRAMES)) for part in parts
        ]

    def parts(self, groups, count):
        if self.spatial:
            (value,) = groups
            value = value.reshape(self.rows, count, self.tokens, -1)
            return [self.flat(value[:, i]) for i in range(count)]
        return [value.reshape(self.rows * self.tokens, -1) for value in groups]

    def forms(self):
        return spatial_forms if self.spatial else temporal_forms

    def attention(self, stream, mod, weights):
        inner = weights.shape[1] // 4
        hidden = [self.flat(h) for h in gather_tokens(self.modulated(stream, mod, 0))]
        w_qkv, w_proj = weights[:, : 3 * inner], weights[:, 3 * inner :]
        qkv = [dot(h, w_qkv).astype(bf16) for h in hidden]
        groups = self.sequences(qkv)
        results = [attend(group, self.forms()) for group in groups]
        attended = self.parts([r[0] for r in results], len(hidden))
        partial = [self.full(dot_nt(a, w_proj)) for a in attended]
        branch = scatter_tokens(partial)
        gated = self.by_row(mod[:, 2]) * branch
        logs = [r[1] for r in results]
        return stream + gated, gated, (stream, branch, hidden, groups, attended, logs, w_qkv, w_proj)

    def mlp(self, stream, mod, weights):
        inner = weights.shape[1] // 2
        hidden = [self.flat(h) for h in gather_tokens(self.modulated(stream, mod, 3))]
        w_up, w_down = weights[:, :inner], weights[:, inner:]
        pre = [dot(h, w_up) for h in hidden]
        active = [gelu_tanh(p).astype(bf16) for p in pre]
        branch = scatter_tokens([self.full(dot_nt(a, w_down)) for a in active])
        gated = self.by_row(mod[:, 5]) * branch
        return stream + gated, gated, (stream, branch, hidden, pre, active, w_up, w_down)

    def branch_back(self, grad, mod, offset, branch):
        grad_branch = (grad * self.by_row(mod[:, offset + 2])).astype(bf16)
        grad_gate = self.by_clip(jnp.sum(grad * branch, axis=1))
        return [self.flat(g) for g in gather_tokens(grad_branch)], grad_gate

    def norm_back(self, grad, grad_hidden, stream, mod, offset):
        normed, inverse = layer_norm(stream)
        grad_normed = grad_hidden * (1.0 + self.by_row(mod[:, offset + 1]))
        centered = grad_normed - jnp.mean(grad_normed, axis=-1, keepdims=True)
        grad_in = inverse * (
            centered - normed * jnp.mean(grad_normed * normed, axis=-1, keepdims=True)
        )
        shift = self.by_clip(jnp.sum(grad_hidden, axis=1))
        scale = self.by_clip(jnp.sum(grad_hidden * normed, axis=1))
        return grad + grad_in, shift, scale

    def mlp_back(self, grad, mod, stored):
        stream, branch, hidden, pre, active, w_up, w_down = stored
        grad_branch, gate = self.branch_back(grad, mod, 3, branch)
        grad_pre = [
            jax.vjp(gelu_tanh, p)[1](dot(g, w_down))[0].astype(bf16)
            for p, g in zip(pre, grad_branch)
        ]
        grad_hidden = scatter_tokens([self.full(dot_nt(g, w_up)) for g in grad_pre])
        joined = [jnp.concatenate(v) for v in (hidden, grad_pre, grad_branch, active)]
        grad_w = jnp.concatenate(
            [dot_tn(joined[0], joined[1]).astype(bf16), dot_tn(joined[2], joined[3]).astype(bf16)],
            axis=1,
        )
        grad, shift, scale = self.norm_back(grad, grad_hidden, stream, mod, 3)
        return grad, jnp.stack([shift, scale, gate], axis=1), grad_w

    def attention_back(self, grad, mod, stored):
        stream, branch, hidden, groups, attended, logs, w_qkv, w_proj = stored
        grad_branch, gate = self.branch_back(grad, mod, 0, branch)
        grad_att = [dot(g, w_proj).astype(bf16) for g in grad_branch]
        heads = grad_att[0].shape[1] // HEAD_DIM
        if self.spatial:
            view = jnp.stack([self.full(g) for g in grad_att], axis=1)
            views = [view.reshape(self.rows, -1, heads, HEAD_DIM)]
        else:
            views = [g.reshape(FRAMES, -1, heads, HEAD_DIM) for g in grad_att]
        grads = [
            attend_back(group, log, view, self.forms())
            for group, log, view in zip(groups, logs, views)
        ]
        three = [self.parts([g[i] for g in grads], len(hidden)) for i in range(3)]
        grad_qkv = [jnp.concatenate([t[i] for t in three], axis=1) for i in range(len(hidden))]
        grad_hidden = scatter_tokens([self.full(dot_nt(g, w_qkv)) for g in grad_qkv])
        joined = [jnp.concatenate(v) for v in (hidden, grad_qkv, grad_branch, attended)]
        grad_w = jnp.concatenate(
            [dot_tn(joined[0], joined[1]).astype(bf16), dot_tn(joined[2], joined[3]).astype(bf16)],
            axis=1,
        )
        grad, shift, scale = self.norm_back(grad, grad_hidden, stream, mod, 0)
        return grad, jnp.stack([shift, scale, gate], axis=1), grad_w


def to_places(stream):
    return lax.all_to_all(
        stream.astype(bf16), "dp", split_axis=1, concat_axis=0, tiled=True
    ).astype(f32)


def to_frames(stream):
    return lax.all_to_all(stream.astype(bf16), "dp", split_axis=0, concat_axis=1, tiled=True)


def gather_weights(first, second):
    packed = jnp.concatenate([first.reshape(first.shape[0], -1), second.T], axis=1)
    return lax.all_gather(packed, "dp", axis=0, tiled=True)


def scatter_grads(grad_w, first, second):
    local = lax.psum_scatter(grad_w, "dp", scatter_dimension=0, tiled=True).astype(f32)
    cut = local.shape[1] - second.shape[0]
    return local[:, :cut].reshape(first.shape), local[:, cut:].T


def body(
    video_in,
    condition,
    adaln_spatial,
    qkv_spatial,
    proj_spatial,
    up_spatial,
    down_spatial,
    adaln_temporal,
    qkv_temporal,
    proj_temporal,
    up_temporal,
    down_temporal,
    grad_output,
):
    rows, tokens, width = video_in.shape
    clips = condition.shape[0]
    dp, me = lax.axis_size("dp"), lax.axis_index("dp")
    spatial = Layer(rows, tokens, clips, True, me * rows)
    temporal = Layer(rows * dp, tokens // dp, clips, False, 0)

    w_attn_s = gather_weights(qkv_spatial, proj_spatial)
    w_mlp_s = gather_weights(up_spatial, down_spatial)
    w_attn_t = gather_weights(qkv_temporal, proj_temporal)
    w_mlp_t = gather_weights(up_temporal, down_temporal)

    share = adaln_spatial.shape[0]
    cond_rows = lax.dynamic_slice_in_dim(condition, me * share, share, 1)
    silu_rows, silu_pull = jax.vjp(jax.nn.silu, cond_rows)
    silu_low = silu_rows.astype(bf16)
    flat_s = adaln_spatial.reshape(share, -1)
    flat_t = adaln_temporal.reshape(share, -1)
    mods = all_sum(jnp.stack([dot(silu_low, flat_s), dot(silu_low, flat_t)]), ("dp",))
    mod_s = mods[0].reshape(clips, 6, width)
    mod_t = mods[1].reshape(clips, 6, width)

    stream0 = video_in.astype(f32)
    s1, g1, kept1 = spatial.attention(stream0, mod_s, w_attn_s)
    s2, g2, kept2 = spatial.mlp(s1, mod_s, w_mlp_s)
    placed = to_places(s2)
    s3, g3, kept3 = temporal.attention(placed, mod_t, w_attn_t)
    s4, g4, kept4 = temporal.mlp(s3, mod_t, w_mlp_t)
    video_out = to_frames(s4)
    squares = jnp.stack(
        [spatial.by_frame(v) for v in (s1, s2)]
        + [temporal.by_frame(v) for v in (s3, s4)]
        + [spatial.by_frame(v) for v in (g1, g2)]
        + [temporal.by_frame(v) for v in (g3, g4)]
    )
    squares = all_sum(squares, ("dp", "tensor"))
    frame_rms = jnp.sqrt(squares / (clips * PATCHES * width))

    grad = to_places(grad_output)
    grad, dmod4, gw4 = temporal.mlp_back(grad, mod_t, kept4)
    grad_up_t, grad_down_t = scatter_grads(gw4, up_temporal, down_temporal)
    dmod4 = all_sum(dmod4, ("dp", "tensor"))
    grad, dmod3, gw3 = temporal.attention_back(grad, mod_t, kept3)
    grad_qkv_t, grad_proj_t = scatter_grads(gw3, qkv_temporal, proj_temporal)
    dmod3 = all_sum(dmod3, ("dp", "tensor"))
    grad = to_frames(grad).astype(f32)
    grad, dmod2, gw2 = spatial.mlp_back(grad, mod_s, kept2)
    grad_up_s, grad_down_s = scatter_grads(gw2, up_spatial, down_spatial)
    dmod2 = all_sum(dmod2, ("dp", "tensor"))
    grad, dmod1, gw1 = spatial.attention_back(grad, mod_s, kept1)
    grad_qkv_s, grad_proj_s = scatter_grads(gw1, qkv_spatial, proj_spatial)
    dmod1 = all_sum(dmod1, ("dp", "tensor"))

    shift_grad = jnp.stack([d[:, 0] for d in (dmod1, dmod2, dmod3, dmod4)])
    silu_wide = silu_low.astype(f32)

    def adaln_back(flat, dmod_attn, dmod_mlp, shape):
        dmod = jnp.concatenate([dmod_attn, dmod_mlp], axis=1).reshape(clips, -1)
        grad_w = jnp.sum(silu_wide[:, :, None] * dmod[:, None, :], axis=0).reshape(shape)
        back = lax.dot_general(
            dmod, flat.astype(f32), (((1,), (1,)), ((), ())), precision=highest
        )
        return grad_w, back

    adaln_t_grad, back_t = adaln_back(flat_t, dmod3, dmod4, adaln_temporal.shape)
    adaln_s_grad, back_s = adaln_back(flat_s, dmod1, dmod2, adaln_spatial.shape)
    condition_grad = silu_pull(back_s + back_t)[0]
    return (
        video_out,
        grad,
        condition_grad,
        adaln_s_grad,
        grad_qkv_s,
        grad_proj_s,
        grad_up_s,
        grad_down_s,
        adaln_t_grad,
        grad_qkv_t,
        grad_proj_t,
        grad_up_t,
        grad_down_t,
        frame_rms,
        shift_grad,
    )


def solution(mesh):
    return jax.shard_map(
        body,
        mesh=mesh,
        in_specs=(
            P("dp", "tensor", None),
            P(),
            P("dp", None, None),
            P("dp", None, "tensor"),
            P("tensor", "dp"),
            P("dp", "tensor"),
            P("tensor", "dp"),
            P("dp", None, None),
            P("dp", None, "tensor"),
            P("tensor", "dp"),
            P("dp", "tensor"),
            P("tensor", "dp"),
            P("dp", "tensor", None),
        ),
        out_specs=(
            P("dp", "tensor", None),
            P("dp", "tensor", None),
            P(None, "dp"),
            P("dp", None, None),
            P("dp", None, "tensor"),
            P("tensor", "dp"),
            P("dp", "tensor"),
            P("tensor", "dp"),
            P("dp", None, None),
            P("dp", None, "tensor"),
            P("tensor", "dp"),
            P("dp", "tensor"),
            P("tensor", "dp"),
            P(),
            P(),
        ),
        check_vma=False,
    )
```

```python
import functools

import jax
import jax.numpy as jnp
from jax import lax
from jax.experimental import pallas as pl
from jax.experimental.pallas import tpu as pltpu
from jax.sharding import PartitionSpec as P

HEAD_DIM = 72
PATCHES = 256
FRAMES = 16

highest = lax.Precision.HIGHEST
epsilon = 1e-06
bf16 = jnp.bfloat16
f32 = jnp.float32
MESH = pl.DeviceIdType.MESH


def dot(a, b):
    return jnp.dot(a, b, preferred_element_type=f32)


def dot_nt(a, b):
    return lax.dot_general(a, b, (((1,), (1,)), ((), ())), preferred_element_type=f32)


def dot_tn(a, b):
    return lax.dot_general(a, b, (((0,), (0,)), ((), ())), preferred_element_type=f32)


def layer_norm(stream):
    average = jnp.mean(stream, axis=-1, keepdims=True)
    centered = stream - average
    inverse = lax.rsqrt(jnp.mean(centered * centered, axis=-1, keepdims=True) + epsilon)
    return (centered * inverse, inverse)


def gelu_tanh(pre_act):
    return jax.nn.gelu(pre_act, approximate=True)


def swap(value, axis, stride, size):
    return lax.ppermute(value, axis, [(i, i ^ stride) for i in range(size)])


def all_sum(value, axes):
    for axis in axes:
        size = lax.axis_size(axis)
        if size & (size - 1):
            value = lax.psum(value, axis)
            continue
        stride = 1
        while stride < size:
            value = value + swap(value, axis, stride, size)
            stride *= 2
    return value


def gather_tokens(local):
    size = lax.axis_size("tensor")
    if size == 2:
        other = swap(local, "tensor", 1, 2)
        return [local, other]
    return list(lax.all_gather(local, "tensor", axis=0, tiled=False))


def scatter_tokens(parts):
    size = lax.axis_size("tensor")
    if size == 2:
        return parts[0] + swap(parts[1].astype(bf16), "tensor", 1, 2).astype(f32)
    stacked = jnp.stack([part.astype(bf16) for part in parts])
    return lax.psum_scatter(stacked, "tensor", scatter_dimension=0, tiled=False).astype(f32)


def softmax_scores(queries, keys, residue):
    scores = dot_nt(queries, keys) * HEAD_DIM ** (-0.5)
    if residue:
        row = lax.broadcasted_iota(jnp.int32, scores.shape, 0)
        col = lax.broadcasted_iota(jnp.int32, scores.shape, 1)
        scores = jnp.where(lax.rem(row, residue) == lax.rem(col, residue), scores, -1e30)
    unnormed = jnp.exp(scores - jnp.max(scores, axis=-1, keepdims=True))
    return unnormed * (1.0 / jnp.sum(unnormed, axis=-1, keepdims=True))


def joined(refs):
    blocks = [ref[0] for ref in refs]
    return blocks[0] if len(blocks) == 1 else jnp.concatenate(blocks, axis=0)


def store_rows(refs, columns, value):
    start = 0
    for ref in refs:
        ref[0, :, columns] = value[start : start + ref.shape[1]]
        start += ref.shape[1]


def attend_kernel(count, residue, *refs):
    ins, outs = refs[:count], refs[count:]
    qkv = joined(ins)
    inner = qkv.shape[1] // 3
    for start in range(0, inner, HEAD_DIM):
        q, k, v = (
            qkv[:, part * inner + start : part * inner + start + HEAD_DIM] for part in range(3)
        )
        probs = softmax_scores(q, k, residue).astype(bf16)
        store_rows(outs, slice(start, start + HEAD_DIM), dot(probs, v).astype(bf16))


def attend_back_kernel(count, residue, *refs):
    ins, grads, outs = refs[:count], refs[count : 2 * count], refs[2 * count :]
    qkv, grad_att = joined(ins), joined(grads)
    inner = grad_att.shape[1]
    for start in range(0, inner, HEAD_DIM):
        q, k, v = (
            qkv[:, part * inner + start : part * inner + start + HEAD_DIM] for part in range(3)
        )
        grad_out = grad_att[:, start : start + HEAD_DIM]
        probs = softmax_scores(q, k, residue)
        grad_probs = dot_nt(grad_out, v)
        mean = jnp.sum(probs * grad_probs, axis=-1, keepdims=True)
        grad_scaled = (probs * (grad_probs - mean) * HEAD_DIM ** (-0.5)).astype(bf16)
        results = (
            dot(grad_scaled, k),
            dot_tn(grad_scaled, q),
            dot_tn(probs.astype(bf16), grad_out),
        )
        for part, value in enumerate(results):
            left = part * inner + start
            store_rows(outs, slice(left, left + HEAD_DIM), value.astype(bf16))


def attend_call(kernel, residue, operands, widths):
    count = len(operands[0])
    rows, tokens = operands[0][0].shape[:2]
    spec = lambda width: pl.BlockSpec((1, tokens, width), lambda r: (r, 0, 0))
    flat = [value for group in operands for value in group]
    length = count * tokens
    heads = widths // HEAD_DIM
    return pl.pallas_call(
        functools.partial(kernel, count, residue),
        grid=(rows,),
        in_specs=[spec(value.shape[2]) for value in flat],
        out_specs=[spec(widths) for _ in range(count)],
        out_shape=[jax.ShapeDtypeStruct((rows, tokens, widths), bf16) for _ in range(count)],
        cost_estimate=pl.CostEstimate(
            flops=rows * heads * length * length * HEAD_DIM * 4,
            bytes_accessed=sum(v.size * 2 for v in flat),
            transcendentals=rows * heads * length * length,
        ),
        compiler_params=pltpu.CompilerParams(vmem_limit_bytes=48 << 20),
    )(*flat)


def weight_grad_kernel(count, *refs):
    ins, outs = refs[: 4 * count], refs[4 * count :]
    left = 0
    for pair in range(2):
        base = 2 * pair * count
        out = outs[pair % len(outs)]
        left = left if len(outs) == 1 else 0
        rows = jnp.concatenate([ref[...] for ref in ins[base : base + count]], axis=0)
        cols = ins[base + count : base + 2 * count]
        width = cols[0].shape[1]
        step = width if width % 1152 else 1152
        for start in range(0, width, step):
            right = jnp.concatenate([ref[:, start : start + step] for ref in cols], axis=0)
            out[:, left + start : left + start + step] = dot_tn(rows, right).astype(bf16)
        left += width


def weight_grad(first, second, split):
    count, width = len(first[0]), first[0][0].shape[1]
    block = 384 if width % 384 == 0 else width
    ins, specs = [], []
    for rows, cols in (first, second):
        ins += rows + cols
        specs += [pl.BlockSpec((r.shape[0], block), lambda i: (0, i)) for r in rows]
        specs += [pl.BlockSpec(c.shape, lambda i: (0, 0)) for c in cols]
    wide = [first[1][0].shape[1], second[1][0].shape[1]]
    total = sum(wide)
    wide = wide if split else [total]
    tokens = count * first[0][0].shape[0]
    return pl.pallas_call(
        functools.partial(weight_grad_kernel, count),
        grid=(width // block,),
        in_specs=specs,
        out_specs=[pl.BlockSpec((block, w), lambda i: (i, 0)) for w in wide],
        out_shape=[jax.ShapeDtypeStruct((width, w), bf16) for w in wide],
        cost_estimate=pl.CostEstimate(
            flops=2 * tokens * width * total,
            bytes_accessed=2 * width * total + 2 * tokens * (2 * width + total),
            transcendentals=0,
        ),
        compiler_params=pltpu.CompilerParams(vmem_limit_bytes=48 << 20),
    )(*ins)


def tie(*values):
    return lax.optimization_barrier(values)


class GradScatter:
    def __init__(self, grad_w, order):
        self.size, me = lax.axis_size("dp"), lax.axis_index("dp")
        ring = self.size // 4
        self.value = grad_w.reshape(ring, 2, 2, -1, grad_w.shape[1])
        self.at = (me // 4, (me // 2) % 2, me % 2)
        self.order = list(order)
        self.wait = None
        self.begin()

    def pick(self, axis, index):
        return lax.dynamic_slice_in_dim(self.value, index, 1, axis)

    def begin(self):
        axis = self.order[0]
        count, at = self.value.shape[axis], self.at[axis]
        if axis:
            self.wait = swap(self.pick(axis, 1 - at), "dp", 3 - axis, self.size)
        else:
            self.left = count - 1
            self.hop(self.pick(0, lax.rem(at + count - 1, count)))

    def hop(self, total):
        links = [(i, (i + 4) % self.size) for i in range(self.size)]
        self.wait = lax.ppermute(total, "dp", links)

    def step(self, value=None):
        if not self.order:
            return value
        if value is not None:
            value, self.wait = tie(value, self.wait)
        axis = self.order[0]
        at = self.at[axis]
        if axis == 0:
            self.left -= 1
            at = lax.rem(at + self.left, self.value.shape[0])
        total = self.pick(axis, at).astype(f32) + self.wait.astype(f32)
        if axis == 0 and self.left:
            self.hop(total.astype(bf16))
            return value
        self.order.pop(0)
        self.value = total
        if self.order:
            self.value = total.astype(bf16)
            self.begin()
        return value

    def finish(self):
        while self.order:
            self.step()
        return self.value.reshape(-1, self.value.shape[-1])


class AllSum:
    def __init__(self, value):
        self.value = value
        self.pairs = [
            (axis, 1 << bit)
            for axis in ("tensor", "dp")
            for bit in range(lax.axis_size(axis).bit_length() - 1)
        ]
        self.begin()

    def begin(self):
        axis, stride = self.pairs[0]
        self.wait = swap(self.value, axis, stride, lax.axis_size(axis))

    def step(self, value=None):
        if not self.pairs:
            return value
        if value is not None:
            value, self.wait = tie(value, self.wait)
        self.value = self.value + self.wait
        self.pairs.pop(0)
        if self.pairs:
            self.begin()
        return value

    def finish(self):
        while self.pairs:
            self.step()
        return self.value


def all_sum_kernel(pairs, value, out, slots, landed, send_sem, recv_sem):
    barrier = pltpu.get_barrier_semaphore()
    partners = [{axis: lax.axis_index(axis) ^ stride} for axis, stride in pairs]
    for partner in partners:
        pl.semaphore_signal(barrier, inc=1, device_id=partner, device_id_type=MESH)
    pl.semaphore_wait(barrier, len(partners))
    slots[0] = value[...]
    for k, partner in enumerate(partners):
        copy = pltpu.make_async_remote_copy(
            src_ref=slots.at[k],
            dst_ref=landed.at[k],
            send_sem=send_sem.at[k],
            recv_sem=recv_sem.at[k],
            device_id=partner,
            device_id_type=MESH,
        )
        copy.start()
        copy.wait()
        slots[k + 1] = slots[k] + landed[k]
    out[...] = slots[len(partners)]


def all_sum_now(value):
    pairs = [
        (axis, 1 << bit)
        for axis in ("tensor", "dp")
        for bit in range(lax.axis_size(axis).bit_length() - 1)
    ]
    count = len(pairs)
    return pl.pallas_call(
        functools.partial(all_sum_kernel, pairs),
        in_specs=[pl.BlockSpec(memory_space=pltpu.VMEM)],
        out_specs=pl.BlockSpec(memory_space=pltpu.VMEM),
        out_shape=jax.ShapeDtypeStruct(value.shape, f32),
        scratch_shapes=[
            pltpu.VMEM((count + 1,) + value.shape, f32),
            pltpu.VMEM((count,) + value.shape, f32),
            pltpu.SemaphoreType.DMA((count,)),
            pltpu.SemaphoreType.DMA((count,)),
        ],
        compiler_params=pltpu.CompilerParams(collective_id=0, has_side_effects=True),
    )(value)


class Layer:
    def __init__(self, rows, tokens, clips, spatial, first_row):
        self.rows, self.tokens, self.clips, self.spatial = rows, tokens, clips, spatial
        self.first_row = first_row

    def by_row(self, table):
        if self.rows % self.clips == 0:
            width = table.shape[-1]
            spread = jnp.broadcast_to(table[None], (self.rows // self.clips, self.clips, width))
            return spread.reshape(self.rows, 1, width)
        start = lax.rem(self.first_row, self.clips)
        return lax.dynamic_slice_in_dim(table, start, self.rows, 0)[:, None, :]

    def by_clip(self, sums):
        width = sums.shape[-1]
        if self.rows % self.clips == 0:
            return jnp.sum(sums.reshape(self.rows // self.clips, self.clips, width), axis=0)
        start = lax.rem(self.first_row, self.clips)
        empty = jnp.zeros((self.clips, width), f32)
        return lax.dynamic_update_slice_in_dim(empty, sums, start, 0)

    def by_frame(self, entries):
        per_row = jnp.sum(entries * entries, axis=(1, 2))
        frames = max(self.rows // self.clips, 1)
        sums = jnp.sum(per_row.reshape(frames, -1), axis=1)
        if frames == FRAMES:
            return sums
        start = self.first_row // self.clips
        return lax.dynamic_update_slice_in_dim(jnp.zeros((FRAMES,), f32), sums, start, 0)

    def modulated(self, stream, mod, offset):
        normed = layer_norm(stream)[0]
        scale = 1.0 + self.by_row(mod[:, offset + 1])
        return (normed * scale + self.by_row(mod[:, offset])).astype(bf16)

    def flat(self, value):
        return value.reshape(self.rows * self.tokens, value.shape[-1])

    def full(self, value):
        return value.reshape(self.rows, self.tokens, value.shape[-1])

    def attend(self, kernel, operands, widths):
        if self.spatial:
            views = [[self.full(value) for value in group] for group in operands]
            return [self.flat(v) for v in attend_call(kernel, 0, views, widths)]
        count = self.rows * self.tokens
        out = []
        for i in range(len(operands[0])):
            views = [[group[i][None]] for group in operands]
            out.append(attend_call(kernel, count // FRAMES, views, widths)[0][0])
        return out

    def attention(self, stream, mod, weights):
        inner = weights.shape[1] // 4
        hidden = [self.flat(h) for h in gather_tokens(self.modulated(stream, mod, 0))]
        w_qkv, w_proj = weights[:, : 3 * inner], weights[:, 3 * inner :]
        qkv = [dot(h, w_qkv).astype(bf16) for h in hidden]
        attended = self.attend(attend_kernel, [qkv], inner)
        partial = [self.full(dot_nt(a, w_proj)) for a in attended]
        branch = scatter_tokens(partial)
        gated = self.by_row(mod[:, 2]) * branch
        return stream + gated, gated, (stream, branch, hidden, qkv, attended, w_qkv, w_proj)

    def mlp(self, stream, mod, weights):
        inner = weights.shape[1] // 2
        hidden = [self.flat(h) for h in gather_tokens(self.modulated(stream, mod, 3))]
        w_up, w_down = weights[:, :inner], weights[:, inner:]
        pre = [dot(h, w_up) for h in hidden]
        active = [gelu_tanh(p).astype(bf16) for p in pre]
        branch = scatter_tokens([self.full(dot_nt(a, w_down)) for a in active])
        gated = self.by_row(mod[:, 5]) * branch
        return stream + gated, gated, (stream, branch, hidden, pre, active, w_up, w_down)

    def branch_back(self, grad, mod, offset, branch):
        grad_branch = (grad * self.by_row(mod[:, offset + 2])).astype(bf16)
        grad_gate = self.by_clip(jnp.sum(grad * branch, axis=1))
        return [self.flat(g) for g in gather_tokens(grad_branch)], grad_gate

    def norm_back(self, grad, grad_hidden, stream, mod, offset):
        normed, inverse = layer_norm(stream)
        grad_normed = grad_hidden * (1.0 + self.by_row(mod[:, offset + 1]))
        centered = grad_normed - jnp.mean(grad_normed, axis=-1, keepdims=True)
        grad_in = inverse * (
            centered - normed * jnp.mean(grad_normed * normed, axis=-1, keepdims=True)
        )
        shift = self.by_clip(jnp.sum(grad_hidden, axis=1))
        scale = self.by_clip(jnp.sum(grad_hidden * normed, axis=1))
        return grad + grad_in, shift, scale

    def mlp_back(self, grad, mod, stored, split, pump):
        stream, branch, hidden, pre, active, w_up, w_down = stored
        grad_branch, gate = self.branch_back(grad, mod, 3, branch)
        grad_branch[-1] = pump(grad_branch[-1])
        grad_pre = [
            jax.vjp(gelu_tanh, p)[1](dot(g, w_down))[0].astype(bf16)
            for p, g in zip(pre, grad_branch)
        ]
        grad_pre[-1] = pump(grad_pre[-1])
        grad_hidden = scatter_tokens([self.full(dot_nt(g, w_up)) for g in grad_pre])
        grad_w = weight_grad((hidden, grad_pre), (grad_branch, active), split)
        grad_hidden, *grad_w = tie(grad_hidden, *grad_w)
        grad_hidden = pump(grad_hidden)
        grad, shift, scale = self.norm_back(grad, grad_hidden, stream, mod, 3)
        return grad, jnp.stack([shift, scale, gate], axis=1), grad_w

    def attention_back(self, grad, mod, stored, split, pump):
        stream, branch, hidden, qkv, attended, w_qkv, w_proj = stored
        grad_branch, gate = self.branch_back(grad, mod, 0, branch)
        grad_branch[-1] = pump(grad_branch[-1])
        grad_att = [dot(g, w_proj).astype(bf16) for g in grad_branch]
        grad_qkv = self.attend(attend_back_kernel, [qkv, grad_att], w_qkv.shape[1])
        grad_qkv[-1] = pump(grad_qkv[-1])
        grad_hidden = scatter_tokens([self.full(dot_nt(g, w_qkv)) for g in grad_qkv])
        grad_w = weight_grad((hidden, grad_qkv), (grad_branch, attended), split)
        grad_hidden, *grad_w = tie(grad_hidden, *grad_w)
        grad_hidden = pump(grad_hidden)
        grad, shift, scale = self.norm_back(grad, grad_hidden, stream, mod, 0)
        return grad, jnp.stack([shift, scale, gate], axis=1), grad_w


def to_places(stream):
    return lax.all_to_all(
        stream.astype(bf16), "dp", split_axis=1, concat_axis=0, tiled=True
    ).astype(f32)


def to_frames(stream):
    return lax.all_to_all(stream.astype(bf16), "dp", split_axis=0, concat_axis=1, tiled=True)


def gather_weights(first, second):
    packed = jnp.concatenate([first.reshape(first.shape[0], -1), second.T], axis=1)
    return lax.all_gather(packed, "dp", axis=0, tiled=True)


def scatter_grads(grad_w, first, second):
    local = lax.psum_scatter(grad_w, "dp", scatter_dimension=0, tiled=True).astype(f32)
    cut = local.shape[1] - second.shape[0]
    return local[:, :cut].reshape(first.shape), local[:, cut:].T


def body(
    video_in,
    condition,
    adaln_spatial,
    qkv_spatial,
    proj_spatial,
    up_spatial,
    down_spatial,
    adaln_temporal,
    qkv_temporal,
    proj_temporal,
    up_temporal,
    down_temporal,
    grad_output,
):
    rows, tokens, width = video_in.shape
    clips = condition.shape[0]
    dp, me = lax.axis_size("dp"), lax.axis_index("dp")
    spatial = Layer(rows, tokens, clips, True, me * rows)
    temporal = Layer(rows * dp, tokens // dp, clips, False, 0)

    w_attn_s = gather_weights(qkv_spatial, proj_spatial)
    w_mlp_s = gather_weights(up_spatial, down_spatial)
    w_attn_t = gather_weights(qkv_temporal, proj_temporal)
    w_mlp_t = gather_weights(up_temporal, down_temporal)

    share = adaln_spatial.shape[0]
    cond_rows = lax.dynamic_slice_in_dim(condition, me * share, share, 1)
    silu_rows, silu_pull = jax.vjp(jax.nn.silu, cond_rows)
    silu_low = silu_rows.astype(bf16)
    flat_s = adaln_spatial.reshape(share, -1)
    flat_t = adaln_temporal.reshape(share, -1)
    mods = all_sum(jnp.stack([dot(silu_low, flat_s), dot(silu_low, flat_t)]), ("dp",))
    mod_s = mods[0].reshape(clips, 6, width)
    mod_t = mods[1].reshape(clips, 6, width)

    stream0 = video_in.astype(f32)
    s1, g1, kept1 = spatial.attention(stream0, mod_s, w_attn_s)
    s2, g2, kept2 = spatial.mlp(s1, mod_s, w_mlp_s)
    placed = to_places(s2)
    s3, g3, kept3 = temporal.attention(placed, mod_t, w_attn_t)
    s4, g4, kept4 = temporal.mlp(s3, mod_t, w_mlp_t)
    video_out = to_frames(s4)
    squares = jnp.stack(
        [spatial.by_frame(v) for v in (s1, s2)]
        + [temporal.by_frame(v) for v in (s3, s4)]
        + [spatial.by_frame(v) for v in (g1, g2)]
        + [temporal.by_frame(v) for v in (g3, g4)]
    )

    keep = lambda value: value
    grad = to_places(grad_output)
    grad, dmod4, (gw4,) = temporal.mlp_back(grad, mod_t, kept4, False, keep)
    grad_up_t, grad_down_t = scatter_grads(gw4, up_temporal, down_temporal)
    grad, dmod3, (gw3,) = temporal.attention_back(grad, mod_t, kept3, False, keep)
    grad_qkv_t, grad_proj_t = scatter_grads(gw3, qkv_temporal, proj_temporal)
    early = AllSum(
        jnp.concatenate([dmod3.reshape(-1), dmod4.reshape(-1), squares.reshape(-1)]).reshape(-1, 128)
    )
    grad = early.step(to_frames(grad).astype(f32))
    grad, dmod2, gw2 = spatial.mlp_back(grad, mod_s, kept2, True, early.step)
    chains = [GradScatter(gw2[0], (2, 1, 0)), GradScatter(gw2[1], (2, 0, 1))]

    def pump(value):
        turn = pump.turn
        pump.turn += 1
        value = early.step(value)
        if turn != 1:
            value = chains[0].step(value)
        return chains[1].step(value)

    pump.turn = 0
    grad, dmod1, gw1 = spatial.attention_back(grad, mod_s, kept1, True, pump)
    chains += [GradScatter(gw1[0], (2, 1, 0)), GradScatter(gw1[1], (2, 0, 1))]
    late = all_sum_now(jnp.concatenate([dmod1.reshape(-1), dmod2.reshape(-1)]).reshape(-1, 128))
    late = late.reshape(2, clips, 3, width)
    dmod1, dmod2 = late[0], late[1]
    cut = clips * 3 * width
    flat_early = early.finish().reshape(-1)
    dmod3 = flat_early[:cut].reshape(clips, 3, width)
    dmod4 = flat_early[cut : 2 * cut].reshape(clips, 3, width)
    squares = flat_early[2 * cut :].reshape(8, FRAMES)
    frame_rms = jnp.sqrt(squares / (clips * PATCHES * width))
    done = [chain.finish() for chain in chains]
    grad_up_s, grad_down_s = done[0], done[1].T
    grad_qkv_s, grad_proj_s = done[2].reshape(qkv_spatial.shape), done[3].T
    shift_grad = jnp.stack([d[:, 0] for d in (dmod1, dmod2, dmod3, dmod4)])
    silu_wide = silu_low.astype(f32)

    def adaln_back(flat, dmod_attn, dmod_mlp, shape):
        dmod = jnp.concatenate([dmod_attn, dmod_mlp], axis=1).reshape(clips, -1)
        grad_w = jnp.sum(silu_wide[:, :, None] * dmod[:, None, :], axis=0).reshape(shape)
        back = lax.dot_general(
            dmod, flat.astype(f32), (((1,), (1,)), ((), ())), precision=highest
        )
        return grad_w, back

    adaln_t_grad, back_t = adaln_back(flat_t, dmod3, dmod4, adaln_temporal.shape)
    adaln_s_grad, back_s = adaln_back(flat_s, dmod1, dmod2, adaln_spatial.shape)
    condition_grad = silu_pull(back_s + back_t)[0]
    return (
        video_out,
        grad,
        condition_grad,
        adaln_s_grad,
        grad_qkv_s,
        grad_proj_s,
        grad_up_s,
        grad_down_s,
        adaln_t_grad,
        grad_qkv_t,
        grad_proj_t,
        grad_up_t,
        grad_down_t,
        frame_rms,
        shift_grad,
    )


def solution(mesh):
    return jax.shard_map(
        body,
        mesh=mesh,
        in_specs=(
            P("dp", "tensor", None),
            P(),
            P("dp", None, None),
            P("dp", None, "tensor"),
            P("tensor", "dp"),
            P("dp", "tensor"),
            P("tensor", "dp"),
            P("dp", None, None),
            P("dp", None, "tensor"),
            P("tensor", "dp"),
            P("dp", "tensor"),
            P("tensor", "dp"),
            P("dp", "tensor", None),
        ),
        out_specs=(
            P("dp", "tensor", None),
            P("dp", "tensor", None),
            P(None, "dp"),
            P("dp", None, None),
            P("dp", None, "tensor"),
            P("tensor", "dp"),
            P("dp", "tensor"),
            P("tensor", "dp"),
            P("dp", None, None),
            P("dp", None, "tensor"),
            P("tensor", "dp"),
            P("dp", "tensor"),
            P("tensor", "dp"),
            P(),
            P(),
        ),
        check_vma=False,
    )
```

```python
import functools

import jax
import jax.numpy as jnp
from jax import lax
from jax.experimental import pallas as pl
from jax.experimental.pallas import tpu as pltpu
from jax.sharding import PartitionSpec as P

HEAD_DIM = 72
PATCHES = 256
FRAMES = 16

highest = lax.Precision.HIGHEST
epsilon = 1e-06
bf16 = jnp.bfloat16
f32 = jnp.float32
MESH = pl.DeviceIdType.MESH


def dot(a, b):
    return jnp.dot(a, b, preferred_element_type=f32)


def dot_nt(a, b):
    return lax.dot_general(a, b, (((1,), (1,)), ((), ())), preferred_element_type=f32)


def dot_tn(a, b):
    return lax.dot_general(a, b, (((0,), (0,)), ((), ())), preferred_element_type=f32)


def layer_norm(stream):
    average = jnp.mean(stream, axis=-1, keepdims=True)
    centered = stream - average
    inverse = lax.rsqrt(jnp.mean(centered * centered, axis=-1, keepdims=True) + epsilon)
    return (centered * inverse, inverse)


def gelu_tanh(pre_act):
    return jax.nn.gelu(pre_act, approximate=True)


def swap(value, axis, stride, size):
    return lax.ppermute(value, axis, [(i, i ^ stride) for i in range(size)])


def all_sum(value, axes):
    for axis in axes:
        size = lax.axis_size(axis)
        if size & (size - 1):
            value = lax.psum(value, axis)
            continue
        stride = 1
        while stride < size:
            value = value + swap(value, axis, stride, size)
            stride *= 2
    return value


def gather_tokens(local):
    size = lax.axis_size("tensor")
    if size == 2:
        other = swap(local, "tensor", 1, 2)
        return [local, other]
    return list(lax.all_gather(local, "tensor", axis=0, tiled=False))


def scatter_tokens(parts):
    size = lax.axis_size("tensor")
    if size == 2:
        return parts[0] + swap(parts[1].astype(bf16), "tensor", 1, 2).astype(f32)
    stacked = jnp.stack([part.astype(bf16) for part in parts])
    return lax.psum_scatter(stacked, "tensor", scatter_dimension=0, tiled=False).astype(f32)


def softmax_scores(queries, keys, residue):
    scores = dot_nt(queries, keys) * HEAD_DIM ** (-0.5)
    if residue:
        row = lax.broadcasted_iota(jnp.int32, scores.shape, 0)
        col = lax.broadcasted_iota(jnp.int32, scores.shape, 1)
        scores = jnp.where(lax.rem(row, residue) == lax.rem(col, residue), scores, -1e30)
    unnormed = jnp.exp(scores - jnp.max(scores, axis=-1, keepdims=True))
    return unnormed * (1.0 / jnp.sum(unnormed, axis=-1, keepdims=True))


def joined(refs):
    blocks = [ref[0] for ref in refs]
    return blocks[0] if len(blocks) == 1 else jnp.concatenate(blocks, axis=0)


def store_rows(refs, columns, value):
    start = 0
    for ref in refs:
        ref[0, :, columns] = value[start : start + ref.shape[1]]
        start += ref.shape[1]


def attend_kernel(count, residue, *refs):
    ins, outs = refs[:count], refs[count:]
    qkv = joined(ins)
    inner = qkv.shape[1] // 3
    for start in range(0, inner, HEAD_DIM):
        q, k, v = (
            qkv[:, part * inner + start : part * inner + start + HEAD_DIM] for part in range(3)
        )
        probs = softmax_scores(q, k, residue).astype(bf16)
        store_rows(outs, slice(start, start + HEAD_DIM), dot(probs, v).astype(bf16))


def attend_back_kernel(count, residue, *refs):
    ins, grads, outs = refs[:count], refs[count : 2 * count], refs[2 * count :]
    qkv, grad_att = joined(ins), joined(grads)
    inner = grad_att.shape[1]
    for start in range(0, inner, HEAD_DIM):
        q, k, v = (
            qkv[:, part * inner + start : part * inner + start + HEAD_DIM] for part in range(3)
        )
        grad_out = grad_att[:, start : start + HEAD_DIM]
        probs = softmax_scores(q, k, residue)
        grad_probs = dot_nt(grad_out, v)
        mean = jnp.sum(probs * grad_probs, axis=-1, keepdims=True)
        grad_scaled = (probs * (grad_probs - mean) * HEAD_DIM ** (-0.5)).astype(bf16)
        results = (
            dot(grad_scaled, k),
            dot_tn(grad_scaled, q),
            dot_tn(probs.astype(bf16), grad_out),
        )
        for part, value in enumerate(results):
            left = part * inner + start
            store_rows(outs, slice(left, left + HEAD_DIM), value.astype(bf16))


def attend_call(kernel, residue, operands, widths):
    count = len(operands[0])
    rows, tokens = operands[0][0].shape[:2]
    spec = lambda width: pl.BlockSpec((1, tokens, width), lambda r: (r, 0, 0))
    flat = [value for group in operands for value in group]
    length = count * tokens
    heads = widths // HEAD_DIM
    return pl.pallas_call(
        functools.partial(kernel, count, residue),
        grid=(rows,),
        in_specs=[spec(value.shape[2]) for value in flat],
        out_specs=[spec(widths) for _ in range(count)],
        out_shape=[jax.ShapeDtypeStruct((rows, tokens, widths), bf16) for _ in range(count)],
        cost_estimate=pl.CostEstimate(
            flops=rows * heads * length * length * HEAD_DIM * 4,
            bytes_accessed=sum(v.size * 2 for v in flat),
            transcendentals=rows * heads * length * length,
        ),
        compiler_params=pltpu.CompilerParams(vmem_limit_bytes=48 << 20),
    )(*flat)


def weight_grad_kernel(count, *refs):
    ins, outs = refs[: 4 * count], refs[4 * count :]
    left = 0
    for pair in range(2):
        base = 2 * pair * count
        out = outs[pair % len(outs)]
        left = left if len(outs) == 1 else 0
        rows = jnp.concatenate([ref[...] for ref in ins[base : base + count]], axis=0)
        cols = ins[base + count : base + 2 * count]
        width = cols[0].shape[1]
        step = width if width % 1152 else 1152
        for start in range(0, width, step):
            right = jnp.concatenate([ref[:, start : start + step] for ref in cols], axis=0)
            out[:, left + start : left + start + step] = dot_tn(rows, right).astype(bf16)
        left += width


def weight_grad(first, second, split):
    count, width = len(first[0]), first[0][0].shape[1]
    block = 384 if width % 384 == 0 else width
    ins, specs = [], []
    for rows, cols in (first, second):
        ins += rows + cols
        specs += [pl.BlockSpec((r.shape[0], block), lambda i: (0, i)) for r in rows]
        specs += [pl.BlockSpec(c.shape, lambda i: (0, 0)) for c in cols]
    wide = [first[1][0].shape[1], second[1][0].shape[1]]
    total = sum(wide)
    wide = wide if split else [total]
    tokens = count * first[0][0].shape[0]
    return pl.pallas_call(
        functools.partial(weight_grad_kernel, count),
        grid=(width // block,),
        in_specs=specs,
        out_specs=[pl.BlockSpec((block, w), lambda i: (i, 0)) for w in wide],
        out_shape=[jax.ShapeDtypeStruct((width, w), bf16) for w in wide],
        cost_estimate=pl.CostEstimate(
            flops=2 * tokens * width * total,
            bytes_accessed=2 * width * total + 2 * tokens * (2 * width + total),
            transcendentals=0,
        ),
        compiler_params=pltpu.CompilerParams(vmem_limit_bytes=48 << 20),
    )(*ins)


def tie(*values):
    return lax.optimization_barrier(values)


class AllSum:
    def __init__(self, value):
        self.value = value
        self.pairs = [
            (axis, 1 << bit)
            for axis in ("tensor", "dp")
            for bit in range(lax.axis_size(axis).bit_length() - 1)
        ]
        self.begin()

    def begin(self):
        axis, stride = self.pairs[0]
        self.wait = swap(self.value, axis, stride, lax.axis_size(axis))

    def step(self, value=None):
        if not self.pairs:
            return value
        if value is not None:
            value, self.wait = tie(value, self.wait)
        self.value = self.value + self.wait
        self.pairs.pop(0)
        if self.pairs:
            self.begin()
        return value

    def finish(self):
        while self.pairs:
            self.step()
        return self.value


def exchange_pairs():
    return [
        (axis, 1 << bit)
        for axis in ("tensor", "dp")
        for bit in range(lax.axis_size(axis).bit_length() - 1)
    ]


class Scatter:
    def __init__(self, grad, out, refs, flipped):
        self.grad, self.out, self.flipped = grad, out, flipped
        self.own, self.core_in, self.y_in, self.ring_in, self.own_sem, self.send_sem, self.recv_sem = refs
        self.ring = grad.shape[0]
        self.stages = self.ring + 2
        self.chunks = self.send_sem.shape[1]
        self.width = grad.shape[-1] // self.chunks
        me, size = lax.axis_index("dp"), 4 * self.ring
        self.me, self.at, self.y, self.core = me, me // 4, lax.rem(me // 2, 2), lax.rem(me, 2)
        self.after, self.before = lax.rem(me + 4, size), lax.rem(me + size - 4, size)
        self.pending = {}
        self.load = None

    @staticmethod
    def scratch(ring, rows, cols):
        chunks = cols // 384 if cols % 384 == 0 else 1
        return [
            pltpu.VMEM((ring, 2, rows, cols), bf16),
            pltpu.VMEM((ring, 2, rows, cols), bf16),
            pltpu.VMEM((ring, rows, cols), bf16),
            pltpu.VMEM((ring - 1, 2, rows, cols), bf16),
            pltpu.SemaphoreType.DMA,
            pltpu.SemaphoreType.DMA((ring + 1, chunks)),
            pltpu.SemaphoreType.DMA((ring + 1, chunks)),
        ]

    def begin(self):
        self.load = pltpu.make_async_copy(self.grad.at[:, :, self.core], self.own, self.own_sem)
        self.load.start()

    def send(self, s, j, source, target, partner):
        copy = pltpu.make_async_remote_copy(
            src_ref=source, dst_ref=target, send_sem=self.send_sem.at[s, j], recv_sem=self.recv_sem.at[s, j],
            device_id={"dp": partner}, device_id_type=MESH,
        )
        copy.start()
        self.pending[s, j] = copy

    def stage(self, s, j):
        cols = pl.ds(j * self.width, self.width)
        ring, y, at = self.ring, self.y, self.at
        if s == 0:
            source = self.grad.at[:, :, 1 - self.core, :, cols]
            return self.send(s, j, source, self.core_in.at[:, :, :, cols], self.me ^ 1)
        if self.load is not None:
            self.load.wait()
            self.load = None
        self.pending[s - 1, j].wait_recv()
        flipped = self.flipped(j)
        if s == 1:
            total = self.own[:, :, :, cols].astype(f32) + self.core_in[:, :, :, cols].astype(f32)
            self.own[:, :, :, cols] = total.astype(bf16)
        if not flipped:
            if s == 1:
                return self.send(s, j, self.own.at[:, 1 - y, :, cols], self.y_in.at[:, :, cols], self.me ^ 2)
            h = s - 2
            if h == 0:
                total = self.own[:, y, :, cols].astype(f32) + self.y_in[:, :, cols].astype(f32)
                self.y_in[:, :, cols] = total.astype(bf16)
                source = self.y_in.at[lax.rem(at + ring - 1, ring), :, cols]
            else:
                total = self.y_in[lax.rem(at + ring - 1 - h, ring), :, cols].astype(f32)
                total = total + self.ring_in[h - 1, 0, :, cols].astype(f32)
                if h == ring - 1:
                    self.out[:, cols] = total
                    return None
                self.ring_in[h - 1, 0, :, cols] = total.astype(bf16)
                source = self.ring_in.at[h - 1, 0, :, cols]
            return self.send(s, j, source, self.ring_in.at[h, 0, :, cols], self.after)
        h = s - 1
        if h == 0:
            source = self.own.at[lax.rem(at + ring - 1, ring), :, :, cols]
            return self.send(s, j, source, self.ring_in.at[h, :, :, cols], self.after)
        if h < ring:
            total = self.own[lax.rem(at + ring - 1 - h, ring), :, :, cols].astype(f32)
            total = total + self.ring_in[h - 1, :, :, cols].astype(f32)
            self.ring_in[h - 1, :, :, cols] = total.astype(bf16)
            if h < ring - 1:
                source = self.ring_in.at[h - 1, :, :, cols]
                return self.send(s, j, source, self.ring_in.at[h, :, :, cols], self.after)
            source = self.ring_in.at[h - 1, 1 - y, :, cols]
            return self.send(s, j, source, self.y_in.at[0, :, cols], self.me ^ 2)
        total = self.ring_in[ring - 2, y, :, cols].astype(f32)
        self.out[:, cols] = total + self.y_in[0, :, cols].astype(f32)
        return None

    def finish(self):
        for copy in self.pending.values():
            copy.wait_send()


class Pipeline:
    def __init__(self, jobs):
        self.jobs = jobs
        self.queue = [(job, j) for job in jobs for j in range(job.chunks)]
        self.flight = []
        for job in jobs:
            job.begin()

    def tick(self):
        for entry in self.flight:
            job, j, s, age = entry
            if age >= max(2 * s - 1, 1):
                job.stage(s, j)
                entry[2] += 1
            entry[3] += 1
        self.flight = [entry for entry in self.flight if entry[2] < entry[0].stages]
        if self.queue:
            job, j = self.queue.pop(0)
            job.stage(0, j)
            self.flight.append([job, j, 1, 1])
        return bool(self.queue or self.flight)

    def finish(self):
        while self.tick():
            pass
        for job in self.jobs:
            job.finish()


class SmallSum:
    def __init__(self, pairs, value, out, refs):
        self.slots, self.landed, self.send_sem, self.recv_sem = refs
        self.value, self.out, self.copies = value, out, []
        self.partners = [{axis: lax.axis_index(axis) ^ stride} for axis, stride in pairs]
        self.k = 0

    @staticmethod
    def scratch(count, shape):
        return [
            pltpu.VMEM((count + 1,) + shape, f32),
            pltpu.VMEM((count,) + shape, f32),
            pltpu.SemaphoreType.DMA((count,)),
            pltpu.SemaphoreType.DMA((count,)),
        ]

    def tick(self):
        k, self.k = self.k, self.k + 1
        if k > len(self.partners):
            return False
        if k == 0:
            self.slots[0] = self.value[...]
        else:
            self.copies[k - 1].wait_recv()
            self.slots[k] = self.slots[k - 1] + self.landed[k - 1]
        if k == len(self.partners):
            self.out[...] = self.slots[k]
            return False
        copy = pltpu.make_async_remote_copy(
            src_ref=self.slots.at[k], dst_ref=self.landed.at[k],
            send_sem=self.send_sem.at[k], recv_sem=self.recv_sem.at[k],
            device_id=self.partners[k], device_id_type=MESH,
        )
        copy.start()
        self.copies.append(copy)
        return True

    def finish(self):
        while self.tick():
            pass
        for copy in self.copies:
            copy.wait_send()


def greet(partners):
    barrier = pltpu.get_barrier_semaphore()
    for partner in partners:
        pl.semaphore_signal(barrier, inc=1, device_id=partner, device_id_type=MESH)
    pl.semaphore_wait(barrier, len(partners))


def tail_kernel(count, pairs, *refs):
    grads, small = refs[:count], refs[count]
    outs, small_out = refs[count + 1 : 2 * count + 1], refs[2 * count + 1]
    scratch = refs[2 * count + 2 :]
    jobs = [
        Scatter(grads[i], outs[i], scratch[7 * i : 7 * i + 7], lambda j: j % 6 == 5)
        for i in range(count)
    ]
    total = SmallSum(pairs, small, small_out, scratch[7 * count :])
    greet(total.partners + [{"dp": jobs[0].after}, {"dp": jobs[0].before}])
    pipeline = Pipeline(jobs)
    total.tick()
    for _ in range(len(pairs)):
        pipeline.tick()
        total.tick()
    pipeline.finish()
    total.finish()


def tail(grads, small):
    ring = lax.axis_size("dp") // 4
    grads = [grad.reshape(ring, 2, 2, -1, grad.shape[1]) for grad in grads]
    pairs = exchange_pairs()
    anywhere, vmem = pl.BlockSpec(memory_space=pl.ANY), pl.BlockSpec(memory_space=pltpu.VMEM)
    scratch = []
    for grad in grads:
        scratch += Scatter.scratch(ring, *grad.shape[3:])
    return pl.pallas_call(
        functools.partial(tail_kernel, len(grads), pairs),
        in_specs=[anywhere] * len(grads) + [vmem],
        out_specs=[vmem] * (len(grads) + 1),
        out_shape=[jax.ShapeDtypeStruct(grad.shape[3:], f32) for grad in grads]
        + [jax.ShapeDtypeStruct(small.shape, f32)],
        scratch_shapes=scratch + SmallSum.scratch(len(pairs), small.shape),
        compiler_params=pltpu.CompilerParams(
            collective_id=0, has_side_effects=True, vmem_limit_bytes=56 << 20
        ),
    )(*grads, small)


class Layer:
    def __init__(self, rows, tokens, clips, spatial, first_row):
        self.rows, self.tokens, self.clips, self.spatial = rows, tokens, clips, spatial
        self.first_row = first_row

    def by_row(self, table):
        if self.rows % self.clips == 0:
            width = table.shape[-1]
            spread = jnp.broadcast_to(table[None], (self.rows // self.clips, self.clips, width))
            return spread.reshape(self.rows, 1, width)
        start = lax.rem(self.first_row, self.clips)
        return lax.dynamic_slice_in_dim(table, start, self.rows, 0)[:, None, :]

    def by_clip(self, sums):
        width = sums.shape[-1]
        if self.rows % self.clips == 0:
            return jnp.sum(sums.reshape(self.rows // self.clips, self.clips, width), axis=0)
        start = lax.rem(self.first_row, self.clips)
        empty = jnp.zeros((self.clips, width), f32)
        return lax.dynamic_update_slice_in_dim(empty, sums, start, 0)

    def by_frame(self, entries):
        per_row = jnp.sum(entries * entries, axis=(1, 2))
        frames = max(self.rows // self.clips, 1)
        sums = jnp.sum(per_row.reshape(frames, -1), axis=1)
        if frames == FRAMES:
            return sums
        start = self.first_row // self.clips
        return lax.dynamic_update_slice_in_dim(jnp.zeros((FRAMES,), f32), sums, start, 0)

    def modulated(self, stream, mod, offset):
        normed = layer_norm(stream)[0]
        scale = 1.0 + self.by_row(mod[:, offset + 1])
        return (normed * scale + self.by_row(mod[:, offset])).astype(bf16)

    def flat(self, value):
        return value.reshape(self.rows * self.tokens, value.shape[-1])

    def full(self, value):
        return value.reshape(self.rows, self.tokens, value.shape[-1])

    def attend(self, kernel, operands, widths):
        if self.spatial:
            views = [[self.full(value) for value in group] for group in operands]
            return [self.flat(v) for v in attend_call(kernel, 0, views, widths)]
        count = self.rows * self.tokens
        out = []
        for i in range(len(operands[0])):
            views = [[group[i][None]] for group in operands]
            out.append(attend_call(kernel, count // FRAMES, views, widths)[0][0])
        return out

    def attention(self, stream, mod, weights, pump, hidden=None):
        inner = weights.shape[1] // 4
        if hidden is None:
            hidden = gather_tokens(self.modulated(stream, mod, 0))
        hidden = [self.flat(h) for h in hidden]
        w_qkv, w_proj = weights[:, : 3 * inner], weights[:, 3 * inner :]
        qkv = [dot(h, w_qkv).astype(bf16) for h in hidden]
        attended = self.attend(attend_kernel, [qkv], inner)
        attended[-1] = pump(attended[-1])
        partial = [self.full(dot_nt(a, w_proj)) for a in attended]
        branch = scatter_tokens(partial)
        branch = pump(branch)
        gated = self.by_row(mod[:, 2]) * branch
        return stream + gated, gated, (stream, branch, hidden, qkv, attended, w_qkv, w_proj)

    def mlp(self, stream, mod, weights, pump):
        inner = weights.shape[1] // 2
        hidden = [self.flat(h) for h in gather_tokens(self.modulated(stream, mod, 3))]
        hidden[-1] = pump(hidden[-1])
        w_up, w_down = weights[:, :inner], weights[:, inner:]
        pre = [dot(h, w_up) for h in hidden]
        active = [gelu_tanh(p).astype(bf16) for p in pre]
        branch = scatter_tokens([self.full(dot_nt(a, w_down)) for a in active])
        branch = pump(branch)
        gated = self.by_row(mod[:, 5]) * branch
        return stream + gated, gated, (stream, branch, hidden, pre, active, w_up, w_down)

    def branch_back(self, grad, mod, offset, branch):
        grad_branch = (grad * self.by_row(mod[:, offset + 2])).astype(bf16)
        grad_gate = self.by_clip(jnp.sum(grad * branch, axis=1))
        return [self.flat(g) for g in gather_tokens(grad_branch)], grad_gate

    def norm_back(self, grad, grad_hidden, stream, mod, offset):
        normed, inverse = layer_norm(stream)
        grad_normed = grad_hidden * (1.0 + self.by_row(mod[:, offset + 1]))
        centered = grad_normed - jnp.mean(grad_normed, axis=-1, keepdims=True)
        grad_in = inverse * (
            centered - normed * jnp.mean(grad_normed * normed, axis=-1, keepdims=True)
        )
        shift = self.by_clip(jnp.sum(grad_hidden, axis=1))
        scale = self.by_clip(jnp.sum(grad_hidden * normed, axis=1))
        return grad + grad_in, shift, scale

    def mlp_back(self, grad, mod, stored, split, pump):
        stream, branch, hidden, pre, active, w_up, w_down = stored
        grad_branch, gate = self.branch_back(grad, mod, 3, branch)
        grad_branch[-1] = pump(grad_branch[-1])
        grad_pre = [
            jax.vjp(gelu_tanh, p)[1](dot(g, w_down))[0].astype(bf16)
            for p, g in zip(pre, grad_branch)
        ]
        grad_pre[-1] = pump(grad_pre[-1])
        grad_hidden = scatter_tokens([self.full(dot_nt(g, w_up)) for g in grad_pre])
        grad_w = weight_grad((hidden, grad_pre), (grad_branch, active), split)
        grad_hidden, *grad_w = tie(grad_hidden, *grad_w)
        grad_hidden = pump(grad_hidden)
        grad, shift, scale = self.norm_back(grad, grad_hidden, stream, mod, 3)
        return grad, jnp.stack([shift, scale, gate], axis=1), grad_w

    def attention_back(self, grad, mod, stored, split, pump):
        stream, branch, hidden, qkv, attended, w_qkv, w_proj = stored
        grad_branch, gate = self.branch_back(grad, mod, 0, branch)
        grad_branch[-1] = pump(grad_branch[-1])
        grad_att = [dot(g, w_proj).astype(bf16) for g in grad_branch]
        grad_qkv = self.attend(attend_back_kernel, [qkv, grad_att], w_qkv.shape[1])
        grad_qkv[-1] = pump(grad_qkv[-1])
        grad_hidden = scatter_tokens([self.full(dot_nt(g, w_qkv)) for g in grad_qkv])
        grad_w = weight_grad((hidden, grad_qkv), (grad_branch, attended), split)
        grad_hidden, *grad_w = tie(grad_hidden, *grad_w)
        grad_hidden = pump(grad_hidden)
        grad, shift, scale = self.norm_back(grad, grad_hidden, stream, mod, 0)
        return grad, jnp.stack([shift, scale, gate], axis=1), grad_w


def to_places(stream):
    return lax.all_to_all(
        stream.astype(bf16), "dp", split_axis=1, concat_axis=0, tiled=True
    ).astype(f32)


def to_frames(stream):
    return lax.all_to_all(stream.astype(bf16), "dp", split_axis=0, concat_axis=1, tiled=True)


def pack(first, second):
    return jnp.concatenate([first.reshape(first.shape[0], -1), second.T], axis=1)


def gather_weights(first, second):
    return lax.all_gather(pack(first, second), "dp", axis=0, tiled=True)


def norm_rows(value):
    centered = value - jnp.mean(value, axis=-1, keepdims=True)
    return centered * lax.rsqrt(jnp.mean(centered * centered, axis=-1, keepdims=True) + epsilon)


def head_kernel(
    ring, clips, pairs, shard, small, video, out, small_out, hidden, other,
    slots, landed_small, own_sem, send_sem, recv_sem, pair_send, pair_recv, x_send, x_recv,
):
    size, me = 4 * ring, lax.axis_index("dp")
    tensor = lax.axis_index("tensor")
    after, before = lax.rem(me + 4, size), lax.rem(me + size - 4, size)
    beside, core = me ^ 2, me ^ 1
    exchange = lax.axis_size("tensor") == 2
    barrier = pltpu.get_barrier_semaphore()
    partners = [{"dp": me ^ stride} for stride in pairs]
    greeted = partners + [{"dp": after}, {"dp": before}]
    if exchange:
        greeted.append({"tensor": 1 - tensor})
    for partner in greeted:
        pl.semaphore_signal(barrier, inc=1, device_id=partner, device_id_type=MESH)
    pl.semaphore_wait(barrier, len(greeted))
    keep = pltpu.make_async_copy(shard, out.at[me], own_sem)
    keep.start()
    sent = []

    def send(source, target, out_sem, in_sem, partner):
        copy = pltpu.make_async_remote_copy(
            src_ref=source, dst_ref=target, send_sem=out_sem, recv_sem=in_sem,
            device_id=partner, device_id_type=MESH,
        )
        copy.start()
        sent.append(copy)
        return copy

    def pass_on(source, place, slot, partner):
        send(source, out.at[place], send_sem.at[slot], recv_sem.at[slot], {"dp": partner})

    def landed(place, slot):
        pltpu.make_async_remote_copy(
            src_ref=out.at[place], dst_ref=out.at[place],
            send_sem=send_sem.at[slot], recv_sem=recv_sem.at[slot],
            device_id={"dp": core}, device_id_type=MESH,
        ).wait_recv()

    flying = []

    def pair_step(k):
        if k == 0:
            slots[0] = small[...]
        else:
            flying[k - 1].wait_recv()
            slots[k] = slots[k - 1] + landed_small[k - 1]
        if k < len(partners):
            flying.append(
                send(slots.at[k], landed_small.at[k], pair_send.at[k], pair_recv.at[k], partners[k])
            )

    pair_step(0)
    step = 1
    for k in range(ring):
        place = lax.rem(me + size - 4 * k, size)
        if k:
            landed(place, k - 1)
        source = shard if k == 0 else out.at[place]
        if k < ring - 1:
            pass_on(source, place, k, after)
        pass_on(source, place, ring + k, beside)
        pass_on(source, place, 2 * ring + k, core)
        if k:
            place = lax.rem((me ^ 2) + size - 4 * (k - 1), size)
            landed(place, ring + k - 1)
            pass_on(out.at[place], place, 3 * ring + k - 1, core)
        if step <= len(partners):
            pair_step(step)
            step += 1
    while step <= len(partners):
        pair_step(step)
        step += 1
    small_out[...] = slots[len(partners)]
    if exchange:
        rows = video.shape[0]
        for r in range(rows):
            clip = r % clips if rows % clips == 0 else lax.rem(me * rows + r, clips)
            shift = slots[len(partners), pl.ds(6 * clip, 1), :]
            scale = slots[len(partners), pl.ds(6 * clip + 1, 1), :]
            normed = norm_rows(video[r].astype(f32))
            hidden[r] = (normed * (1.0 + scale) + shift).astype(bf16)
        swapped = send(hidden, other, x_send, x_recv, {"tensor": 1 - tensor})
    place = lax.rem((me ^ 2) + size - 4 * (ring - 1), size)
    landed(place, 2 * ring - 1)
    pass_on(out.at[place], place, 4 * ring - 1, core)
    for k in range(ring):
        landed(lax.rem(core + size - 4 * k, size), 2 * ring + k)
        landed(lax.rem((core ^ 2) + size - 4 * k, size), 3 * ring + k)
    keep.wait()
    if exchange:
        swapped.wait_recv()
    for copy in sent:
        copy.wait_send()


def head(shard, small, video, clips):
    ring = lax.axis_size("dp") // 4
    rows, cols = shard.shape
    pairs = [1 << bit for bit in range(lax.axis_size("dp").bit_length() - 1)]
    count = len(pairs)
    vmem, anywhere = pl.BlockSpec(memory_space=pltpu.VMEM), pl.BlockSpec(memory_space=pl.ANY)
    full, total, mine, other = pl.pallas_call(
        functools.partial(head_kernel, ring, clips, pairs),
        in_specs=[anywhere, vmem, vmem],
        out_specs=[anywhere, vmem, vmem, vmem],
        out_shape=[
            jax.ShapeDtypeStruct((4 * ring, rows, cols), bf16),
            jax.ShapeDtypeStruct(small.shape, f32),
            jax.ShapeDtypeStruct(video.shape, bf16),
            jax.ShapeDtypeStruct(video.shape, bf16),
        ],
        scratch_shapes=[
            pltpu.VMEM((count + 1,) + small.shape, f32),
            pltpu.VMEM((count,) + small.shape, f32),
            pltpu.SemaphoreType.DMA,
            pltpu.SemaphoreType.DMA((4 * ring,)),
            pltpu.SemaphoreType.DMA((4 * ring,)),
            pltpu.SemaphoreType.DMA((count,)),
            pltpu.SemaphoreType.DMA((count,)),
            pltpu.SemaphoreType.DMA,
            pltpu.SemaphoreType.DMA,
        ],
        cost_estimate=pl.CostEstimate(flops=1 << 35, bytes_accessed=8 * ring * rows * cols, transcendentals=0),
        compiler_params=pltpu.CompilerParams(
            collective_id=1, has_side_effects=True, vmem_limit_bytes=32 << 20
        ),
    )(shard, small, video)
    hidden = [mine, other] if lax.axis_size("tensor") == 2 else None
    return full.reshape(4 * ring * rows, cols), total, hidden


def assemble_kernel(ring, own, *refs):
    hops, beside, core, out, sems = refs[: ring - 1], *refs[ring - 1 :]
    size, me = 4 * ring, lax.axis_index("dp")
    copies = []

    def put(source, place):
        copy = pltpu.make_async_copy(source, out.at[place], sems.at[len(copies)])
        copy.start()
        copies.append(copy)

    for k in range(ring):
        back = lambda device: lax.rem(device + size - 4 * k, size)
        put(own if k == 0 else hops[k - 1], back(me))
        put(beside.at[k], back(me ^ 2))
        put(core.at[k], back(me ^ 1))
        put(core.at[ring + k], back(me ^ 3))
    for copy in copies:
        copy.wait()


class WeightGather:
    def __init__(self, shard):
        self.size = lax.axis_size("dp")
        self.ring = self.size // 4
        self.pieces, self.stage = [shard], 0
        self.begin()

    def begin(self):
        if self.stage < self.ring - 1:
            links = [(i, (i + 4) % self.size) for i in range(self.size)]
            self.wait = lax.ppermute(self.pieces[-1], "dp", links)
        elif self.stage == self.ring - 1:
            self.column = jnp.stack(self.pieces)
            self.wait = swap(self.column, "dp", 2, self.size)
        else:
            self.wait = swap(jnp.concatenate([self.column, self.pieces[-1]]), "dp", 1, self.size)

    def step(self, value=None):
        if self.stage > self.ring:
            return value
        if value is not None:
            value, self.wait = tie(value, self.wait)
        self.pieces.append(self.wait)
        self.stage += 1
        if self.stage <= self.ring:
            self.begin()
        return value

    def finish(self):
        while self.stage <= self.ring:
            self.step()
        rows, cols = self.pieces[0].shape
        anywhere = pl.BlockSpec(memory_space=pl.ANY)
        full = pl.pallas_call(
            functools.partial(assemble_kernel, self.ring),
            in_specs=[anywhere] * (self.ring + 2),
            out_specs=pl.BlockSpec(memory_space=pltpu.VMEM),
            out_shape=jax.ShapeDtypeStruct((self.size, rows, cols), bf16),
            scratch_shapes=[pltpu.SemaphoreType.DMA((self.size,))],
            compiler_params=pltpu.CompilerParams(vmem_limit_bytes=32 << 20),
        )(*self.pieces)
        return full.reshape(self.size * rows, cols)


def scatter_grads(grad_w):
    return lax.psum_scatter(grad_w, "dp", scatter_dimension=0, tiled=True)


def unpack(local, first, second):
    local = local.astype(f32)
    cut = local.shape[1] - second.shape[0]
    return local[:, :cut].reshape(first.shape), local[:, cut:].T


def body(
    video_in,
    condition,
    adaln_spatial,
    qkv_spatial,
    proj_spatial,
    up_spatial,
    down_spatial,
    adaln_temporal,
    qkv_temporal,
    proj_temporal,
    up_temporal,
    down_temporal,
    grad_output,
):
    rows, tokens, width = video_in.shape
    clips = condition.shape[0]
    dp, me = lax.axis_size("dp"), lax.axis_index("dp")
    spatial = Layer(rows, tokens, clips, True, me * rows)
    temporal = Layer(rows * dp, tokens // dp, clips, False, 0)

    w_mlp_s = gather_weights(up_spatial, down_spatial)
    w_mlp_t = gather_weights(up_temporal, down_temporal)

    share = adaln_spatial.shape[0]
    cond_rows = lax.dynamic_slice_in_dim(condition, me * share, share, 1)
    silu_rows, silu_pull = jax.vjp(jax.nn.silu, cond_rows)
    silu_low = silu_rows.astype(bf16)
    flat_s = adaln_spatial.reshape(share, -1)
    flat_t = adaln_temporal.reshape(share, -1)
    mods = jnp.stack([dot(silu_low, flat_s), dot(silu_low, flat_t)]).reshape(-1, width)
    w_attn_s, mods, hidden = head(pack(qkv_spatial, proj_spatial), mods, video_in, clips)

    keep = lambda value: value
    stream0 = video_in.astype(f32)
    shard, mods = tie(pack(qkv_temporal, proj_temporal), mods)
    mod_s, mod_t = mods.reshape(2, clips, 6, width)
    later = WeightGather(shard)
    s1, g1, kept1 = spatial.attention(stream0, mod_s, w_attn_s, later.step, hidden)
    s2, g2, kept2 = spatial.mlp(s1, mod_s, w_mlp_s, later.step)
    placed = later.step(to_places(s2))
    w_attn_t = later.finish()
    placed, grad_output = tie(placed, grad_output)
    grad = to_places(grad_output)
    s3, g3, kept3 = temporal.attention(placed, mod_t, w_attn_t, keep)
    s4, g4, kept4 = temporal.mlp(s3, mod_t, w_mlp_t, keep)
    video_out = to_frames(s4)
    squares = jnp.stack(
        [spatial.by_frame(v) for v in (s1, s2)]
        + [temporal.by_frame(v) for v in (s3, s4)]
        + [spatial.by_frame(v) for v in (g1, g2)]
        + [temporal.by_frame(v) for v in (g3, g4)]
    )

    grad, dmod4, (gw4,) = temporal.mlp_back(grad, mod_t, kept4, False, keep)
    own4 = scatter_grads(gw4)
    grad, dmod3, (gw3,) = temporal.attention_back(grad, mod_t, kept3, False, keep)
    early = AllSum(
        jnp.concatenate([dmod3.reshape(-1), dmod4.reshape(-1), squares.reshape(-1)]).reshape(-1, 128)
    )
    grad = early.step(to_frames(grad).astype(f32))
    grad, dmod2, gw2 = spatial.mlp_back(grad, mod_s, kept2, True, early.step)
    grad, own4, gw3 = tie(grad, own4, gw3)
    own3 = scatter_grads(gw3)
    grad_up_t, grad_down_t = unpack(own4, up_temporal, down_temporal)
    grad_qkv_t, grad_proj_t = unpack(own3, qkv_temporal, proj_temporal)
    grad, dmod1, (gw1,) = spatial.attention_back(grad, mod_s, kept1, False, early.step)
    small = jnp.concatenate([dmod1.reshape(-1), dmod2.reshape(-1)]).reshape(-1, 128)
    grad_up_s, down_s, own1, late = tail([*gw2, gw1], small)
    grad_down_s = down_s.T
    grad_qkv_s, grad_proj_s = unpack(own1, qkv_spatial, proj_spatial)
    late = late.reshape(2, clips, 3, width)
    dmod1, dmod2 = late[0], late[1]
    cut = clips * 3 * width
    flat_early = early.finish().reshape(-1)
    dmod3 = flat_early[:cut].reshape(clips, 3, width)
    dmod4 = flat_early[cut : 2 * cut].reshape(clips, 3, width)
    squares = flat_early[2 * cut :].reshape(8, FRAMES)
    frame_rms = jnp.sqrt(squares / (clips * PATCHES * width))
    shift_grad = jnp.stack([d[:, 0] for d in (dmod1, dmod2, dmod3, dmod4)])
    silu_wide = silu_low.astype(f32)

    def adaln_back(flat, dmod_attn, dmod_mlp, shape):
        dmod = jnp.concatenate([dmod_attn, dmod_mlp], axis=1).reshape(clips, -1)
        grad_w = jnp.sum(silu_wide[:, :, None] * dmod[:, None, :], axis=0).reshape(shape)
        back = lax.dot_general(
            dmod, flat.astype(f32), (((1,), (1,)), ((), ())), precision=highest
        )
        return grad_w, back

    adaln_t_grad, back_t = adaln_back(flat_t, dmod3, dmod4, adaln_temporal.shape)
    adaln_s_grad, back_s = adaln_back(flat_s, dmod1, dmod2, adaln_spatial.shape)
    condition_grad = silu_pull(back_s + back_t)[0]
    return (
        video_out,
        grad,
        condition_grad,
        adaln_s_grad,
        grad_qkv_s,
        grad_proj_s,
        grad_up_s,
        grad_down_s,
        adaln_t_grad,
        grad_qkv_t,
        grad_proj_t,
        grad_up_t,
        grad_down_t,
        frame_rms,
        shift_grad,
    )


def solution(mesh):
    return jax.shard_map(
        body,
        mesh=mesh,
        in_specs=(
            P("dp", "tensor", None),
            P(),
            P("dp", None, None),
            P("dp", None, "tensor"),
            P("tensor", "dp"),
            P("dp", "tensor"),
            P("tensor", "dp"),
            P("dp", None, None),
            P("dp", None, "tensor"),
            P("tensor", "dp"),
            P("dp", "tensor"),
            P("tensor", "dp"),
            P("dp", "tensor", None),
        ),
        out_specs=(
            P("dp", "tensor", None),
            P("dp", "tensor", None),
            P(None, "dp"),
            P("dp", None, None),
            P("dp", None, "tensor"),
            P("tensor", "dp"),
            P("dp", "tensor"),
            P("tensor", "dp"),
            P("dp", None, None),
            P("dp", None, "tensor"),
            P("tensor", "dp"),
            P("dp", "tensor"),
            P("tensor", "dp"),
            P(),
            P(),
        ),
        check_vma=False,
    )
```

```python
import functools

import jax
import jax.numpy as jnp
from jax import lax
from jax.experimental import pallas as pl
from jax.experimental.pallas import tpu as pltpu
from jax.sharding import PartitionSpec as P

HEAD_DIM = 72
PATCHES = 256
FRAMES = 16

highest = lax.Precision.HIGHEST
epsilon = 1e-06
bf16 = jnp.bfloat16
f32 = jnp.float32
MESH = pl.DeviceIdType.MESH


def dot(a, b):
    return jnp.dot(a, b, preferred_element_type=f32)


def dot_nt(a, b):
    return lax.dot_general(a, b, (((1,), (1,)), ((), ())), preferred_element_type=f32)


def dot_tn(a, b):
    return lax.dot_general(a, b, (((0,), (0,)), ((), ())), preferred_element_type=f32)


def layer_norm(stream):
    average = jnp.mean(stream, axis=-1, keepdims=True)
    centered = stream - average
    inverse = lax.rsqrt(jnp.mean(centered * centered, axis=-1, keepdims=True) + epsilon)
    return (centered * inverse, inverse)


def gelu_tanh(pre_act):
    return jax.nn.gelu(pre_act, approximate=True)


def swap(value, axis, stride, size):
    return lax.ppermute(value, axis, [(i, i ^ stride) for i in range(size)])


def all_sum(value, axes):
    for axis in axes:
        size = lax.axis_size(axis)
        if size & (size - 1):
            value = lax.psum(value, axis)
            continue
        stride = 1
        while stride < size:
            value = value + swap(value, axis, stride, size)
            stride *= 2
    return value


def gather_tokens(local):
    size = lax.axis_size("tensor")
    if size == 2:
        other = swap(local, "tensor", 1, 2)
        return [local, other]
    return list(lax.all_gather(local, "tensor", axis=0, tiled=False))


def scatter_tokens(parts):
    size = lax.axis_size("tensor")
    if size == 2:
        return parts[0] + swap(parts[1].astype(bf16), "tensor", 1, 2).astype(f32)
    stacked = jnp.stack([part.astype(bf16) for part in parts])
    return lax.psum_scatter(stacked, "tensor", scatter_dimension=0, tiled=False).astype(f32)


def softmax_scores(queries, keys, residue):
    scores = dot_nt(queries, keys) * HEAD_DIM ** (-0.5)
    if residue:
        row = lax.broadcasted_iota(jnp.int32, scores.shape, 0)
        col = lax.broadcasted_iota(jnp.int32, scores.shape, 1)
        scores = jnp.where(lax.rem(row, residue) == lax.rem(col, residue), scores, -1e30)
    unnormed = jnp.exp(scores - jnp.max(scores, axis=-1, keepdims=True))
    return unnormed * (1.0 / jnp.sum(unnormed, axis=-1, keepdims=True))


def joined(refs):
    blocks = [ref[0] for ref in refs]
    return blocks[0] if len(blocks) == 1 else jnp.concatenate(blocks, axis=0)


def store_rows(refs, columns, value):
    start = 0
    for ref in refs:
        ref[0, :, columns] = value[start : start + ref.shape[1]]
        start += ref.shape[1]


def attend_kernel(count, residue, *refs):
    ins, outs = refs[:count], refs[count:]
    qkv = joined(ins)
    inner = qkv.shape[1] // 3
    for start in range(0, inner, HEAD_DIM):
        q, k, v = (
            qkv[:, part * inner + start : part * inner + start + HEAD_DIM] for part in range(3)
        )
        probs = softmax_scores(q, k, residue).astype(bf16)
        store_rows(outs, slice(start, start + HEAD_DIM), dot(probs, v).astype(bf16))


def attend_back_kernel(count, residue, *refs):
    ins, grads, outs = refs[:count], refs[count : 2 * count], refs[2 * count :]
    qkv, grad_att = joined(ins), joined(grads)
    inner = grad_att.shape[1]
    for start in range(0, inner, HEAD_DIM):
        q, k, v = (
            qkv[:, part * inner + start : part * inner + start + HEAD_DIM] for part in range(3)
        )
        grad_out = grad_att[:, start : start + HEAD_DIM]
        probs = softmax_scores(q, k, residue)
        grad_probs = dot_nt(grad_out, v)
        mean = jnp.sum(probs * grad_probs, axis=-1, keepdims=True)
        grad_scaled = (probs * (grad_probs - mean) * HEAD_DIM ** (-0.5)).astype(bf16)
        results = (
            dot(grad_scaled, k),
            dot_tn(grad_scaled, q),
            dot_tn(probs.astype(bf16), grad_out),
        )
        for part, value in enumerate(results):
            left = part * inner + start
            store_rows(outs, slice(left, left + HEAD_DIM), value.astype(bf16))


def attend_call(kernel, residue, operands, widths):
    count = len(operands[0])
    rows, tokens = operands[0][0].shape[:2]
    spec = lambda width: pl.BlockSpec((1, tokens, width), lambda r: (r, 0, 0))
    flat = [value for group in operands for value in group]
    length = count * tokens
    heads = widths // HEAD_DIM
    return pl.pallas_call(
        functools.partial(kernel, count, residue),
        grid=(rows,),
        in_specs=[spec(value.shape[2]) for value in flat],
        out_specs=[spec(widths) for _ in range(count)],
        out_shape=[jax.ShapeDtypeStruct((rows, tokens, widths), bf16) for _ in range(count)],
        cost_estimate=pl.CostEstimate(
            flops=rows * heads * length * length * HEAD_DIM * 4,
            bytes_accessed=sum(v.size * 2 for v in flat),
            transcendentals=rows * heads * length * length,
        ),
        compiler_params=pltpu.CompilerParams(vmem_limit_bytes=48 << 20),
    )(*flat)


def weight_grad_kernel(count, *refs):
    ins, outs = refs[: 4 * count], refs[4 * count :]
    left = 0
    for pair in range(2):
        base = 2 * pair * count
        out = outs[pair % len(outs)]
        left = left if len(outs) == 1 else 0
        rows = jnp.concatenate([ref[...] for ref in ins[base : base + count]], axis=0)
        cols = ins[base + count : base + 2 * count]
        width = cols[0].shape[1]
        step = width if width % 1152 else 1152
        for start in range(0, width, step):
            right = jnp.concatenate([ref[:, start : start + step] for ref in cols], axis=0)
            out[:, left + start : left + start + step] = dot_tn(rows, right).astype(bf16)
        left += width


def weight_grad(first, second, split):
    count, width = len(first[0]), first[0][0].shape[1]
    block = 384 if width % 384 == 0 else width
    ins, specs = [], []
    for rows, cols in (first, second):
        ins += rows + cols
        specs += [pl.BlockSpec((r.shape[0], block), lambda i: (0, i)) for r in rows]
        specs += [pl.BlockSpec(c.shape, lambda i: (0, 0)) for c in cols]
    wide = [first[1][0].shape[1], second[1][0].shape[1]]
    total = sum(wide)
    wide = wide if split else [total]
    tokens = count * first[0][0].shape[0]
    return pl.pallas_call(
        functools.partial(weight_grad_kernel, count),
        grid=(width // block,),
        in_specs=specs,
        out_specs=[pl.BlockSpec((block, w), lambda i: (i, 0)) for w in wide],
        out_shape=[jax.ShapeDtypeStruct((width, w), bf16) for w in wide],
        cost_estimate=pl.CostEstimate(
            flops=2 * tokens * width * total,
            bytes_accessed=2 * width * total + 2 * tokens * (2 * width + total),
            transcendentals=0,
        ),
        compiler_params=pltpu.CompilerParams(vmem_limit_bytes=48 << 20),
    )(*ins)


def tie(*values):
    return lax.optimization_barrier(values)


class AllSum:
    def __init__(self, value):
        self.value = value
        self.pairs = [
            (axis, 1 << bit)
            for axis in ("tensor", "dp")
            for bit in range(lax.axis_size(axis).bit_length() - 1)
        ]
        self.begin()

    def begin(self):
        axis, stride = self.pairs[0]
        self.wait = swap(self.value, axis, stride, lax.axis_size(axis))

    def step(self, value=None):
        if not self.pairs:
            return value
        if value is not None:
            value, self.wait = tie(value, self.wait)
        self.value = self.value + self.wait
        self.pairs.pop(0)
        if self.pairs:
            self.begin()
        return value

    def finish(self):
        while self.pairs:
            self.step()
        return self.value


def exchange_pairs():
    return [
        (axis, 1 << bit)
        for axis in ("tensor", "dp")
        for bit in range(lax.axis_size(axis).bit_length() - 1)
    ]


class Scatter:
    def __init__(self, grad, out, refs, flipped):
        self.grad, self.out, self.flipped = grad, out, flipped
        self.own, self.own_sem, self.core_in, self.y_in, self.ring_in, self.send_sem, self.recv_sem = refs
        self.ring = grad.shape[0]
        self.stages = self.ring + 2
        self.chunks = self.send_sem.shape[1]
        self.width = grad.shape[-1] // self.chunks
        me, size = lax.axis_index("dp"), 4 * self.ring
        self.me, self.at, self.y, self.core = me, me // 4, lax.rem(me // 2, 2), lax.rem(me, 2)
        self.after, self.before = lax.rem(me + 4, size), lax.rem(me + size - 4, size)
        self.pending = {}
        self.load = None

    @staticmethod
    def scratch(ring, rows, cols, flips=True):
        chunks = cols // 384 if cols % 384 == 0 else 1
        return [
            pltpu.VMEM((ring, 2, rows, cols), bf16),
            pltpu.SemaphoreType.DMA,
            pltpu.VMEM((ring, 2, rows, cols), bf16),
            pltpu.VMEM((ring, rows, cols), bf16),
            pltpu.VMEM((ring - 1, 2 if flips else 1, rows, cols), bf16),
            pltpu.SemaphoreType.DMA((ring + 1, chunks)),
            pltpu.SemaphoreType.DMA((ring + 1, chunks)),
        ]

    def neighbours(self):
        return [{"dp": partner} for partner in (self.after, self.before, self.me ^ 1, self.me ^ 2)]

    def begin(self):
        self.load = pltpu.make_async_copy(self.grad.at[:, :, self.core], self.own, self.own_sem)
        self.load.start()

    def send(self, s, j, source, target, partner):
        copy = pltpu.make_async_remote_copy(
            src_ref=source, dst_ref=target, send_sem=self.send_sem.at[s, j], recv_sem=self.recv_sem.at[s, j],
            device_id={"dp": partner}, device_id_type=MESH,
        )
        copy.start()
        self.pending[s, j] = copy

    def stage(self, s, j):
        cols = pl.ds(j * self.width, self.width)
        ring, y, at = self.ring, self.y, self.at
        if s == 0:
            source = self.grad.at[:, :, 1 - self.core, :, cols]
            return self.send(s, j, source, self.core_in.at[:, :, :, cols], self.me ^ 1)
        if self.load is not None:
            self.load.wait()
            self.load = None
        self.pending[s - 1, j].wait_recv()
        flipped = self.flipped(j)
        if s == 1:
            total = self.own[:, :, :, cols].astype(f32) + self.core_in[:, :, :, cols].astype(f32)
            self.own[:, :, :, cols] = total.astype(bf16)
        if not flipped:
            if s == 1:
                return self.send(s, j, self.own.at[:, 1 - y, :, cols], self.y_in.at[:, :, cols], self.me ^ 2)
            h = s - 2
            if h == 0:
                total = self.own[:, y, :, cols].astype(f32) + self.y_in[:, :, cols].astype(f32)
                self.y_in[:, :, cols] = total.astype(bf16)
                source = self.y_in.at[lax.rem(at + ring - 1, ring), :, cols]
            else:
                total = self.y_in[lax.rem(at + ring - 1 - h, ring), :, cols].astype(f32)
                total = total + self.ring_in[h - 1, 0, :, cols].astype(f32)
                if h == ring - 1:
                    self.out[:, cols] = total
                    return None
                self.ring_in[h - 1, 0, :, cols] = total.astype(bf16)
                source = self.ring_in.at[h - 1, 0, :, cols]
            return self.send(s, j, source, self.ring_in.at[h, 0, :, cols], self.after)
        h = s - 1
        if h == 0:
            source = self.own.at[lax.rem(at + ring - 1, ring), :, :, cols]
            return self.send(s, j, source, self.ring_in.at[h, :, :, cols], self.after)
        if h < ring:
            total = self.own[lax.rem(at + ring - 1 - h, ring), :, :, cols].astype(f32)
            total = total + self.ring_in[h - 1, :, :, cols].astype(f32)
            self.ring_in[h - 1, :, :, cols] = total.astype(bf16)
            if h < ring - 1:
                source = self.ring_in.at[h - 1, :, :, cols]
                return self.send(s, j, source, self.ring_in.at[h, :, :, cols], self.after)
            source = self.ring_in.at[h - 1, 1 - y, :, cols]
            return self.send(s, j, source, self.y_in.at[0, :, cols], self.me ^ 2)
        total = self.ring_in[ring - 2, y, :, cols].astype(f32)
        self.out[:, cols] = total + self.y_in[0, :, cols].astype(f32)
        return None

    def finish(self):
        for copy in self.pending.values():
            copy.wait_send()


class Pipeline:
    def __init__(self):
        self.jobs, self.queue, self.flight = [], [], []

    def add(self, jobs):
        self.jobs = self.jobs + jobs
        self.queue += [(job, j) for job in jobs for j in range(job.chunks)]
        for job in jobs:
            job.begin()

    def tick(self):
        for entry in self.flight:
            job, j, s, age = entry
            if age >= max(2 * s - 1, 1):
                job.stage(s, j)
                entry[2] += 1
            entry[3] += 1
        self.flight = [entry for entry in self.flight if entry[2] < entry[0].stages]
        if self.queue:
            job, j = self.queue.pop(0)
            job.stage(0, j)
            self.flight.append([job, j, 1, 1])
        return bool(self.queue or self.flight)

    def finish(self):
        while self.tick():
            pass
        for job in self.jobs:
            job.finish()


class SmallSum:
    def __init__(self, pairs, value, out, refs):
        self.slots, self.landed, self.send_sem, self.recv_sem = refs
        self.value, self.out, self.copies = value, out, []
        self.partners = [{axis: lax.axis_index(axis) ^ stride} for axis, stride in pairs]
        self.k = 0

    @staticmethod
    def scratch(count, shape):
        return [
            pltpu.VMEM((count + 1,) + shape, f32),
            pltpu.VMEM((count,) + shape, f32),
            pltpu.SemaphoreType.DMA((count,)),
            pltpu.SemaphoreType.DMA((count,)),
        ]

    def tick(self):
        k, self.k = self.k, self.k + 1
        if k > len(self.partners):
            return False
        if k == 0:
            self.slots[0] = self.value[...]
        else:
            self.copies[k - 1].wait_recv()
            self.slots[k] = self.slots[k - 1] + self.landed[k - 1]
        if k == len(self.partners):
            self.out[...] = self.slots[k]
            return False
        copy = pltpu.make_async_remote_copy(
            src_ref=self.slots.at[k], dst_ref=self.landed.at[k],
            send_sem=self.send_sem.at[k], recv_sem=self.recv_sem.at[k],
            device_id=self.partners[k], device_id_type=MESH,
        )
        copy.start()
        self.copies.append(copy)
        return True

    def finish(self):
        while self.tick():
            pass
        for copy in self.copies:
            copy.wait_send()


def greet(partners):
    barrier = pltpu.get_barrier_semaphore()
    for partner in partners:
        pl.semaphore_signal(barrier, inc=1, device_id=partner, device_id_type=MESH)
    pl.semaphore_wait(barrier, len(partners))


class Swap:
    def __init__(self, source, target, sems, k):
        self.copy = pltpu.make_async_remote_copy(
            src_ref=source, dst_ref=target, send_sem=sems.at[0, k], recv_sem=sems.at[1, k],
            device_id={"tensor": 1 - lax.axis_index("tensor")}, device_id_type=MESH,
        )
        self.copy.start()


def spread(value, rows, clips):
    return value.reshape(rows // clips, clips, value.shape[0] // rows, value.shape[1])


def clip_rows(mods, clips, span):
    rows = [mods[6 * c + span : 6 * c + span + 1, :] for c in range(clips)]
    return jnp.stack(rows, axis=0)[None]


def clip_sums(value, rows, clips):
    return jnp.sum(spread(value, rows, clips), axis=(0, 2))


def norm_back_rows(grad, grad_hidden, stream, scale, rows, clips):
    stream = stream.astype(f32)
    centered = stream - jnp.mean(stream, axis=-1, keepdims=True)
    inverse = lax.rsqrt(jnp.mean(centered * centered, axis=-1, keepdims=True) + epsilon)
    normed = centered * inverse
    grad_normed = (spread(grad_hidden, rows, clips) * (1.0 + scale)).reshape(grad_hidden.shape)
    flat = grad_normed - jnp.mean(grad_normed, axis=-1, keepdims=True)
    slope = jnp.mean(grad_normed * normed, axis=-1, keepdims=True)
    grad_in = grad.astype(f32) + inverse * (flat - normed * slope)
    return grad_in, clip_sums(grad_hidden, rows, clips), clip_sums(grad_hidden * normed, rows, clips)


def gradient_blocks(target, value, cols):
    ring, rows = target.shape[0], target.shape[3]
    for k in range(4 * ring):
        target[k // 4, (k // 2) % 2, k % 2, :, cols] = value[k * rows : (k + 1) * rows].astype(bf16)


def attention_back_kernel(rows, clips, spatial, extra, tailing, pairs, *refs):
    grad, branch, stream, mods, hidden0, hidden1, qkv0, qkv1, att0, att1, weights, *refs = refs
    others, refs = refs[:extra], refs[extra:]
    if tailing:
        dmod_in, *refs = refs
    grad_out, *refs = refs
    other_outs, refs = refs[:extra], refs[extra:]
    if tailing:
        own_out, small_out, *refs = refs
    else:
        dmod_out, gw_out, *refs = refs
    w, w_sem, db0, db1, part_out, part_in, keep, ga0, ga1, x_sems, *refs = refs
    dqkv, refs = (refs[:3], refs[3:6]), refs[6:]
    inner = att0.shape[1]
    count = grad.shape[0]
    jobs = []
    for i in range(extra):
        jobs.append(Scatter(others[i], other_outs[i], refs[7 * i : 7 * i + 7], lambda j: j % 6 == 5))
    refs = refs[7 * extra :]
    greeted = [{"tensor": 1 - lax.axis_index("tensor")}]
    if tailing:
        small, gw, *refs = refs
        own_job = Scatter(gw, own_out, refs[:7], lambda j: False)
        total = SmallSum(pairs, small, small_out, refs[7:])
        greeted = total.partners + [{"dp": jobs[0].after}, {"dp": jobs[0].before}]
    elif extra:
        greeted += jobs[0].neighbours()
    greet(greeted)
    load = pltpu.make_async_copy(weights, w, w_sem)
    load.start()
    db0[...] = (
        (spread(grad[...].astype(f32), rows, clips) * clip_rows(mods, clips, 2)).reshape(grad.shape).astype(bf16)
    )
    first = Swap(db0, db1, x_sems, 0)
    pipeline = Pipeline()
    pipeline.add(jobs)
    tick = pipeline.tick
    dgate = clip_sums(grad[...].astype(f32) * branch[...], rows, clips)
    load.wait()
    w_proj = w[:, 3 * inner :]
    ga0[...] = dot(db0[...], w_proj).astype(bf16)
    tick()
    tick()

    def heads(pieces):
        take = lambda refs, cols: (
            refs[pieces[0][0]][pl.ds(*pieces[0][1:]), cols]
            if len(pieces) == 1
            else jnp.concatenate([refs[i][pl.ds(r, n), cols] for i, r, n in pieces], axis=0)
        )
        residue = 0 if spatial else count // FRAMES
        for h, start in enumerate(range(0, inner, HEAD_DIM)):
            q, k, v = (
                take((qkv0, qkv1), slice(p * inner + start, p * inner + start + HEAD_DIM)) for p in range(3)
            )
            cols = slice(start, start + HEAD_DIM)
            grad_out_h = take((ga0, ga1), cols)
            probs = softmax_scores(q, k, residue)
            grad_probs = dot_nt(grad_out_h, v)
            mean = jnp.sum(probs * grad_probs, axis=-1, keepdims=True)
            scaled = (probs * (grad_probs - mean) * HEAD_DIM ** (-0.5)).astype(bf16)
            results = (dot(scaled, k), dot_tn(scaled, q), dot_tn(probs.astype(bf16), grad_out_h))
            for p, value in enumerate(results):
                at = 0
                for i, r, n in pieces:
                    dqkv[i][p][pl.ds(r, n), cols] = value[at : at + n].astype(bf16)
                    at += n
            if h % 4 == 3:
                tick()

    def grad_hidden(i):
        value = dot_nt(dqkv[i][0][...], w[:, :inner])
        value += dot_nt(dqkv[i][1][...], w[:, inner : 2 * inner])
        return value + dot_nt(dqkv[i][2][...], w[:, 2 * inner : 3 * inner])

    if not spatial:
        heads([(0, 0, count)])
    first.copy.wait_recv()
    ga1[...] = dot(db1[...], w_proj).astype(bf16)
    tick()
    if spatial:
        tokens = count // rows
        for r in range(rows):
            heads([(0, r * tokens, tokens), (1, r * tokens, tokens)])
    else:
        heads([(1, 0, count)])
    part_out[...] = grad_hidden(1).astype(bf16)
    second = Swap(part_out, part_in, x_sems, 1)
    tick()
    keep[...] = grad_hidden(0)
    tick()
    both = lambda a, b: jnp.concatenate([a[...], b[...]], axis=0)
    for p in range(4):
        left = both(hidden0, hidden1) if p < 3 else both(db0, db1)
        right = both(dqkv[0][p], dqkv[1][p]) if p < 3 else both(att0, att1)
        value = dot_tn(left, right)
        cols = slice(p * inner, (p + 1) * inner)
        if tailing:
            gradient_blocks(gw, value, cols)
        else:
            gw_out[:, cols] = value.astype(bf16)
        if p % 2:
            tick()
    if tailing:
        pipeline.add([own_job])
    second.copy.wait_recv()
    result, dshift, dscale = norm_back_rows(
        grad[...], keep[...] + part_in[...].astype(f32), stream[...], clip_rows(mods, clips, 1), rows, clips
    )
    grad_out[...] = result
    dmod = (dshift, dscale, dgate)
    if tailing:
        for k, value in enumerate(dmod):
            small[k * clips : (k + 1) * clips] = value
        small[3 * clips :] = dmod_in[...]
        more = total.tick()
        while more:
            pipeline.tick()
            more = total.tick()
        pipeline.finish()
        total.finish()
    else:
        for k, value in enumerate(dmod):
            dmod_out[k * clips : (k + 1) * clips] = value
        pipeline.finish()
    for exchange in (first, second):
        exchange.copy.wait_send()


def attention_back_call(layer, grad, mod, stored, others=(), dmod_in=None):
    stream, branch, hidden, qkv, attended, weights = stored
    rows, clips, count = layer.rows, layer.clips, layer.rows * layer.tokens
    width, inner, ring = weights.shape[0], attended[0].shape[1], lax.axis_size("dp") // 4
    share = width // (4 * ring)
    pairs = exchange_pairs()
    others = [g.reshape(ring, 2, 2, share, g.shape[1]) for g in others]
    vmem, anywhere = pl.BlockSpec(memory_space=pltpu.VMEM), pl.BlockSpec(memory_space=pl.ANY)
    args = [layer.flat(grad), layer.flat(branch), layer.flat(stream), mod.reshape(-1, width)]
    args += [*hidden, *qkv, *attended]
    specs = [vmem] * len(args) + [anywhere] * (1 + len(others))
    args += [weights, *others]
    shape = jax.ShapeDtypeStruct
    outs = [shape((count, width), f32)]
    scratch = [pltpu.VMEM(weights.shape, bf16), pltpu.SemaphoreType.DMA]
    scratch += [pltpu.VMEM((count, width), bf16)] * 4 + [pltpu.VMEM((count, width), f32)]
    scratch += [pltpu.VMEM((count, inner), bf16)] * 2 + [pltpu.SemaphoreType.DMA((2, 2))]
    scratch += [pltpu.VMEM((count, inner), bf16)] * 6
    outs += [shape((share, g.shape[-1]), f32) for g in others]
    for g in others:
        scratch += Scatter.scratch(ring, share, g.shape[-1])
    tailing = dmod_in is not None
    if tailing:
        args.append(dmod_in)
        specs.append(vmem)
        outs.append(shape((share, 4 * inner), f32))
        total = (3 * clips + dmod_in.shape[0], width)
        outs.append(shape(total, f32))
        scratch.append(pltpu.VMEM(total, f32))
        scratch.append(pltpu.VMEM((ring, 2, 2, share, 4 * inner), bf16))
        scratch += Scatter.scratch(ring, share, 4 * inner, False)
        scratch += SmallSum.scratch(len(pairs), total)
    else:
        outs += [shape((3 * clips, width), f32), shape((width, 4 * inner), bf16)]
    return pl.pallas_call(
        functools.partial(attention_back_kernel, rows, clips, layer.spatial, len(others), tailing, pairs),
        in_specs=specs,
        out_specs=[vmem] * len(outs),
        out_shape=outs,
        scratch_shapes=scratch,
        cost_estimate=pl.CostEstimate(flops=1 << 35, bytes_accessed=1 << 25, transcendentals=0),
        compiler_params=pltpu.CompilerParams(
            collective_id=2 + layer.spatial, has_side_effects=True, vmem_limit_bytes=62 << 20
        ),
    )(*args)


class Gather:
    def __init__(self, ring, shard, out, refs):
        self.ring, self.shard, self.out = ring, shard, out
        self.own_sem, self.send_sem, self.recv_sem = refs
        self.me, self.size, self.sent = lax.axis_index("dp"), 4 * ring, []
        self.k = 0

    @staticmethod
    def scratch(ring):
        return [pltpu.SemaphoreType.DMA] + [pltpu.SemaphoreType.DMA((4 * ring,))] * 2

    def neighbours(self):
        me, size = self.me, self.size
        around = (lax.rem(me + 4, size), lax.rem(me + size - 4, size), me ^ 1, me ^ 2)
        return [{"dp": partner} for partner in around]

    def back(self, device, k):
        return lax.rem(device + self.size - 4 * k, self.size)

    def send(self, source, place, slot, partner):
        copy = pltpu.make_async_remote_copy(
            src_ref=source, dst_ref=self.out.at[place],
            send_sem=self.send_sem.at[slot], recv_sem=self.recv_sem.at[slot],
            device_id={"dp": partner}, device_id_type=MESH,
        )
        copy.start()
        self.sent.append(copy)

    def landed(self, place, slot):
        pltpu.make_async_remote_copy(
            src_ref=self.out.at[place], dst_ref=self.out.at[place],
            send_sem=self.send_sem.at[slot], recv_sem=self.recv_sem.at[slot],
            device_id={"dp": self.me ^ 1}, device_id_type=MESH,
        ).wait_recv()

    def step(self):
        k, self.k = self.k, self.k + 1
        ring, me = self.ring, self.me
        if k == 0:
            self.keep = pltpu.make_async_copy(self.shard, self.out.at[me], self.own_sem)
            self.keep.start()
        if k < ring:
            place = self.back(me, k)
            if k:
                self.landed(place, k - 1)
            source = self.out.at[place] if k else self.shard
            if k < ring - 1:
                self.send(source, place, k, lax.rem(me + 4, self.size))
            self.send(source, place, ring + k, me ^ 2)
            self.send(source, place, 2 * ring + k, me ^ 1)
        if 0 < k <= ring:
            place = self.back(me ^ 2, k - 1)
            self.landed(place, ring + k - 1)
            self.send(self.out.at[place], place, 3 * ring + k - 1, me ^ 1)

    def finish(self):
        while self.k <= self.ring:
            self.step()
        for k in range(self.ring):
            self.landed(self.back(self.me ^ 1, k), 2 * self.ring + k)
            self.landed(self.back(self.me ^ 3, k), 3 * self.ring + k)
        self.keep.wait()
        for copy in self.sent:
            copy.wait_send()


class Pieces:
    def __init__(self, rows, clips, count, spatial):
        self.number = rows if spatial else 2
        self.rows, self.clips = rows // self.number, clips
        self.count = count // self.number

    def at(self, i):
        return pl.ds(i * self.count, self.count)

    def times(self, value, mods, span, i, one=0.0):
        if self.rows % self.clips == 0:
            rows = one + clip_rows(mods, self.clips, span)
            return (spread(value, self.rows, self.clips) * rows).reshape(value.shape)
        return value * (one + self.row(mods, span, i))

    def plus(self, value, mods, span, i):
        if self.rows % self.clips == 0:
            rows = clip_rows(mods, self.clips, span)
            return (spread(value, self.rows, self.clips) + rows).reshape(value.shape)
        return value + self.row(mods, span, i)

    def row(self, mods, span, i):
        at = 6 * (i * self.rows % self.clips) + span
        return mods[at : at + 1, :]

    def swap(self, source, target, sems, i, first):
        return Swap(source.at[self.at(i)], target.at[self.at(i)], sems, first + i).copy


def frame_sums(value, rows, clips):
    frames = rows // clips
    view = (value * value).reshape(frames, value.shape[0] // frames, value.shape[1])
    sums = jnp.sum(jnp.sum(view, axis=1), axis=-1, keepdims=True)
    return jnp.broadcast_to(sums, (frames, 128))


def sublayer_end(pieces, stream, mods, span, keep, part_in, swaps, outs):
    stream_out, stream_low, branch_out, squares, rows, clips = outs
    for i, swap_i in enumerate(swaps):
        at = pieces.at(i)
        swap_i.wait_recv()
        branch = keep[at, :] + part_in[at, :].astype(f32)
        branch_out[at, :] = branch
        gated = pieces.times(branch, mods, span, i)
        keep[at, :] = gated
        total = stream[at, :].astype(f32) + gated
        stream_out[at, :] = total
        stream_low[at, :] = total.astype(bf16)
    squares[0] = frame_sums(stream_out[...], rows, clips)
    squares[1] = frame_sums(keep[...], rows, clips)


def attention_kernel(rows, clips, spatial, given, ring, *refs):
    stream, mods, *refs = refs
    if given:
        hidden0, hidden1, *refs = refs
    weights, *refs = refs
    if ring:
        shard, *refs = refs
    stream_out, stream_low, branch_out, squares, qkv0, qkv1, att0, att1, *refs = refs
    if not given:
        hidden0, hidden1, *refs = refs
    if ring:
        gathered, *refs = refs
    w, w_sem, part_out, part_in, keep, x_sems, *refs = refs
    pieces = Pieces(rows, clips, stream.shape[0], spatial)
    inner, count = att0.shape[1], stream.shape[0]
    gather = Gather(ring, shard, gathered, refs) if ring else None
    step = gather.step if ring else (lambda: None)
    greet([{"tensor": 1 - lax.axis_index("tensor")}] + (gather.neighbours() if ring else []))
    load = pltpu.make_async_copy(weights, w, w_sem)
    load.start()
    step()
    arrivals = []
    for i in range(pieces.number if not given else 0):
        normed = norm_rows(stream[pieces.at(i), :].astype(f32))
        value = pieces.plus(pieces.times(normed, mods, 1, i, 1.0), mods, 0, i)
        hidden0[pieces.at(i), :] = value.astype(bf16)
        arrivals.append(pieces.swap(hidden0, hidden1, x_sems, i, 0))
    load.wait()
    w_qkv = w[:, : 3 * inner]
    qkv0[...] = dot(hidden0[...], w_qkv).astype(bf16)
    step()

    def heads(group):
        residue = 0 if spatial else count // FRAMES

        def take(refs, cols):
            values = [refs[i][pl.ds(r, n), cols] for i, r, n in group]
            return values[0] if len(values) == 1 else jnp.concatenate(values, axis=0)

        for start in range(0, inner, HEAD_DIM):
            q, k, v = (
                take((qkv0, qkv1), slice(p * inner + start, p * inner + start + HEAD_DIM)) for p in range(3)
            )
            value = dot(softmax_scores(q, k, residue).astype(bf16), v).astype(bf16)
            at = 0
            for i, r, n in group:
                (att0, att1)[i][pl.ds(r, n), start : start + HEAD_DIM] = value[at : at + n]
                at += n

    swaps = []
    w_proj = w[:, 3 * inner :]
    if spatial:
        tokens = pieces.count
        for r in range(pieces.number):
            if not given:
                arrivals[r].wait_recv()
            at = pieces.at(r)
            qkv1[at, :] = dot(hidden1[at, :], w_qkv).astype(bf16)
            heads([(0, r * tokens, tokens), (1, r * tokens, tokens)])
            part_out[at, :] = dot_nt(att1[at, :], w_proj).astype(bf16)
            swaps.append(pieces.swap(part_out, part_in, x_sems, r, pieces.number))
            step()
    else:
        heads([(0, 0, count)])
        for arrival in arrivals:
            arrival.wait_recv()
        qkv1[...] = dot(hidden1[...], w_qkv).astype(bf16)
        heads([(1, 0, count)])
        for i in range(pieces.number):
            at = pieces.at(i)
            part_out[at, :] = dot_nt(att1[at, :], w_proj).astype(bf16)
            swaps.append(pieces.swap(part_out, part_in, x_sems, i, pieces.number))
    keep[...] = dot_nt(att0[...], w_proj)
    step()
    sublayer_end(
        pieces, stream, mods, 2, keep, part_in, swaps,
        (stream_out, stream_low, branch_out, squares, rows, clips),
    )
    if ring:
        gather.finish()
    for copy in arrivals + swaps:
        copy.wait_send()


def mlp_kernel(rows, clips, spatial, *refs):
    stream, mods, weights, *refs = refs
    stream_out, stream_low, branch_out, squares, hidden0, hidden1, pre0, pre1, act0, act1, *refs = refs
    w, w_sem, part_out, part_in, keep, x_sems = refs
    pieces = Pieces(rows, clips, stream.shape[0], spatial)
    inner = act0.shape[1]
    greet([{"tensor": 1 - lax.axis_index("tensor")}])
    load = pltpu.make_async_copy(weights, w, w_sem)
    load.start()
    arrivals, swaps = [], []
    for i in range(pieces.number):
        normed = norm_rows(stream[pieces.at(i), :].astype(f32))
        value = pieces.plus(pieces.times(normed, mods, 4, i, 1.0), mods, 3, i)
        hidden0[pieces.at(i), :] = value.astype(bf16)
        arrivals.append(pieces.swap(hidden0, hidden1, x_sems, i, 0))
    load.wait()
    block = 768 if inner % 768 == 0 else inner

    def through(hidden, pre, act, at):
        for start in range(0, inner, block):
            cols = slice(start, start + block)
            value = dot(hidden[at, :], w[:, cols])
            pre[at, cols] = value
            act[at, cols] = gelu_tanh(value).astype(bf16)

    w_down = w[:, inner:]
    everything = pl.ds(0, stream.shape[0])
    through(hidden0, pre0, act0, everything)
    for i, arrival in enumerate(arrivals):
        at = pieces.at(i)
        arrival.wait_recv()
        through(hidden1, pre1, act1, at)
        part_out[at, :] = dot_nt(act1[at, :], w_down).astype(bf16)
        swaps.append(pieces.swap(part_out, part_in, x_sems, i, pieces.number))
    keep[...] = dot_nt(act0[...], w_down)
    sublayer_end(
        pieces, stream, mods, 5, keep, part_in, swaps,
        (stream_out, stream_low, branch_out, squares, rows, clips),
    )
    for copy in arrivals + swaps:
        copy.wait_send()


def forward_call(layer, attends, stream, mod, weights, hidden=None, shard=None):
    rows, clips, count = layer.rows, layer.clips, layer.rows * layer.tokens
    width = weights.shape[0]
    inner = weights.shape[1] // (4 if attends else 2)
    number = rows if layer.spatial else 2
    ring = lax.axis_size("dp") // 4 if shard is not None else 0
    vmem, anywhere = pl.BlockSpec(memory_space=pltpu.VMEM), pl.BlockSpec(memory_space=pl.ANY)
    args, specs = [stream, mod.reshape(-1, width)], [vmem, vmem]
    if hidden:
        args, specs = args + list(hidden), specs + [vmem, vmem]
    args, specs = args + [weights], specs + [anywhere]
    shape = jax.ShapeDtypeStruct
    outs = [shape((count, width), kind) for kind in (f32, bf16, f32)]
    outs.append(shape((2, rows // clips, 128), f32))
    if attends:
        outs += [shape((count, 3 * inner), bf16)] * 2 + [shape((count, inner), bf16)] * 2
        if not hidden:
            outs += [shape((count, width), bf16)] * 2
    else:
        outs += [shape((count, width), bf16)] * 2
        outs += [shape((count, inner), f32)] * 2 + [shape((count, inner), bf16)] * 2
    out_specs = [vmem] * len(outs)
    scratch = [pltpu.VMEM(weights.shape, bf16), pltpu.SemaphoreType.DMA]
    scratch += [pltpu.VMEM((count, width), bf16)] * 2 + [pltpu.VMEM((count, width), f32)]
    scratch += [pltpu.SemaphoreType.DMA((2, 2 * number))]
    if ring:
        args, specs = args + [shard], specs + [anywhere]
        outs.append(shape((4 * ring,) + shard.shape, bf16))
        out_specs.append(anywhere)
        scratch += Gather.scratch(ring)
    if attends:
        kernel = functools.partial(attention_kernel, rows, clips, layer.spatial, bool(hidden), ring)
    else:
        kernel = functools.partial(mlp_kernel, rows, clips, layer.spatial)
    return pl.pallas_call(
        kernel,
        in_specs=specs,
        out_specs=out_specs,
        out_shape=outs,
        scratch_shapes=scratch,
        cost_estimate=pl.CostEstimate(flops=1 << 35, bytes_accessed=1 << 25, transcendentals=0),
        compiler_params=pltpu.CompilerParams(
            collective_id=6 + 2 * attends + layer.spatial, has_side_effects=True, vmem_limit_bytes=60 << 20
        ),
    )(*args)


def gelu_slope(value):
    root, cubic = 0.7978845608028654, 0.044715
    square = value * value
    bend = jnp.tanh(root * (value + cubic * square * value))
    return 0.5 * (1.0 + bend) + 0.5 * value * (1.0 - bend * bend) * root * (1.0 + 3.0 * cubic * square)


def mlp_back_kernel(rows, clips, extra, packed, *refs):
    grad, branch, stream, mods, hidden0, hidden1, pre0, pre1, act0, act1, weights, *refs = refs
    others, refs = refs[:extra], refs[extra:]
    grad_out, dmod_out, *refs = refs
    gw_outs, refs = refs[: 2 - packed], refs[2 - packed :]
    other_outs, refs = refs[:extra], refs[extra:]
    w, w_sem, db0, db1, part_out, part_in, keep, dpre0, dpre1, gw, gw_sem, x_sems, *refs = refs
    inner = act0.shape[1]
    jobs = [
        Scatter(others[i], other_outs[i], refs[7 * i : 7 * i + 7], lambda j: False) for i in range(extra)
    ]
    greeted = [{"tensor": 1 - lax.axis_index("tensor")}]
    if extra:
        greeted += jobs[0].neighbours()
    greet(greeted)
    load = pltpu.make_async_copy(weights, w, w_sem)
    load.start()
    db0[...] = (
        (spread(grad[...].astype(f32), rows, clips) * clip_rows(mods, clips, 5)).reshape(grad.shape).astype(bf16)
    )
    first = Swap(db0, db1, x_sems, 0)
    pipeline = Pipeline()
    pipeline.add(jobs)
    tick = pipeline.tick
    dgate = clip_sums(grad[...].astype(f32) * branch[...], rows, clips)
    load.wait()
    block = 768 if inner % 768 == 0 else inner

    def through(db, pre, dpre):
        for start in range(0, inner, block):
            cols = slice(start, start + block)
            dact = dot(db[...], w[:, inner + start : inner + start + block])
            dpre[:, cols] = (dact * gelu_slope(pre[:, cols])).astype(bf16)
        tick()

    tick()
    through(db0, pre0, dpre0)
    first.copy.wait_recv()
    through(db1, pre1, dpre1)
    part_out[...] = dot_nt(dpre1[...], w[:, :inner]).astype(bf16)
    second = Swap(part_out, part_in, x_sems, 1)
    tick()
    keep[...] = dot_nt(dpre0[...], w[:, :inner])
    tick()
    both = lambda a, b, cols: jnp.concatenate([a[:, cols], b[:, cols]], axis=0)
    whole = slice(0, grad.shape[1])
    stored = []
    for p, (left, right) in enumerate((((hidden0, hidden1), (dpre0, dpre1)), ((db0, db1), (act0, act1)))):
        tall = both(*left, whole)
        for start in range(0, inner, block):
            slot = len(stored) % 2
            if len(stored) > 1:
                stored[-2].wait()
            gw[slot] = dot_tn(tall, both(*right, slice(start, start + block))).astype(bf16)
            at = start + inner if packed and p else start
            out = gw_outs[0 if packed else p].at[:, pl.ds(at, block)]
            copy = pltpu.make_async_copy(gw.at[slot], out, gw_sem.at[slot])
            copy.start()
            stored.append(copy)
            if len(stored) % 2:
                tick()
    second.copy.wait_recv()
    result, dshift, dscale = norm_back_rows(
        grad[...], keep[...] + part_in[...].astype(f32), stream[...], clip_rows(mods, clips, 4), rows, clips
    )
    grad_out[...] = result
    for k, value in enumerate((dshift, dscale, dgate)):
        dmod_out[k * clips : (k + 1) * clips] = value
    pipeline.finish()
    for copy in stored[-2:]:
        copy.wait()
    for exchange in (first, second):
        exchange.copy.wait_send()


def mlp_back_call(layer, grad, mod, stored, packed, others=()):
    stream, branch, hidden, pre, active, weights = stored
    rows, clips, count = layer.rows, layer.clips, layer.rows * layer.tokens
    width, inner, ring = weights.shape[0], active[0].shape[1], lax.axis_size("dp") // 4
    share = width // (4 * ring)
    others = [g.reshape(ring, 2, 2, share, g.shape[1]) for g in others]
    vmem, anywhere = pl.BlockSpec(memory_space=pltpu.VMEM), pl.BlockSpec(memory_space=pl.ANY)
    args = [layer.flat(grad), layer.flat(branch), layer.flat(stream), mod.reshape(-1, width)]
    args += [*hidden, *pre, *active]
    specs = [vmem] * len(args) + [anywhere] * (1 + len(others))
    args += [weights, *others]
    shape = jax.ShapeDtypeStruct
    gw = [shape((width, 2 * inner), bf16)] if packed else [shape((width, inner), bf16)] * 2
    outs = [shape((count, width), f32), shape((3 * clips, width), f32)] + gw
    outs += [shape((share, g.shape[-1]), f32) for g in others]
    block = 768 if inner % 768 == 0 else inner
    scratch = [pltpu.VMEM(weights.shape, bf16), pltpu.SemaphoreType.DMA]
    scratch += [pltpu.VMEM((count, width), bf16)] * 4 + [pltpu.VMEM((count, width), f32)]
    scratch += [pltpu.VMEM((count, inner), bf16)] * 2
    scratch += [pltpu.VMEM((2, width, block), bf16), pltpu.SemaphoreType.DMA((2,))]
    scratch += [pltpu.SemaphoreType.DMA((2, 2))]
    for g in others:
        scratch += Scatter.scratch(ring, share, g.shape[-1], False)
    return pl.pallas_call(
        functools.partial(mlp_back_kernel, rows, clips, len(others), packed),
        in_specs=specs,
        out_specs=[vmem, vmem] + [anywhere] * len(gw) + [vmem] * len(others),
        out_shape=outs,
        scratch_shapes=scratch,
        cost_estimate=pl.CostEstimate(flops=1 << 35, bytes_accessed=1 << 25, transcendentals=0),
        compiler_params=pltpu.CompilerParams(
            collective_id=4 + layer.spatial, has_side_effects=True, vmem_limit_bytes=62 << 20
        ),
    )(*args)


def tail_kernel(count, pairs, *refs):
    grads, small = refs[:count], refs[count]
    outs, small_out = refs[count + 1 : 2 * count + 1], refs[2 * count + 1]
    scratch = refs[2 * count + 2 :]
    jobs = [
        Scatter(grads[i], outs[i], scratch[7 * i : 7 * i + 7], lambda j: j % 6 == 5)
        for i in range(count)
    ]
    total = SmallSum(pairs, small, small_out, scratch[7 * count :])
    greet(total.partners + [{"dp": jobs[0].after}, {"dp": jobs[0].before}])
    pipeline = Pipeline()
    total.tick()
    pipeline.add(jobs)
    for _ in range(len(pairs)):
        pipeline.tick()
        total.tick()
    pipeline.finish()
    total.finish()


def tail(grads, small):
    ring = lax.axis_size("dp") // 4
    grads = [grad.reshape(ring, 2, 2, -1, grad.shape[1]) for grad in grads]
    pairs = exchange_pairs()
    anywhere, vmem = pl.BlockSpec(memory_space=pl.ANY), pl.BlockSpec(memory_space=pltpu.VMEM)
    scratch = []
    for grad in grads:
        scratch += Scatter.scratch(ring, *grad.shape[3:])
    return pl.pallas_call(
        functools.partial(tail_kernel, len(grads), pairs),
        in_specs=[anywhere] * len(grads) + [vmem],
        out_specs=[vmem] * (len(grads) + 1),
        out_shape=[jax.ShapeDtypeStruct(grad.shape[3:], f32) for grad in grads]
        + [jax.ShapeDtypeStruct(small.shape, f32)],
        scratch_shapes=scratch + SmallSum.scratch(len(pairs), small.shape),
        compiler_params=pltpu.CompilerParams(
            collective_id=0, has_side_effects=True, vmem_limit_bytes=56 << 20
        ),
    )(*grads, small)


class Layer:
    def __init__(self, rows, tokens, clips, spatial, first_row):
        self.rows, self.tokens, self.clips, self.spatial = rows, tokens, clips, spatial
        self.first_row = first_row

    def by_row(self, table):
        if self.rows % self.clips == 0:
            width = table.shape[-1]
            spread = jnp.broadcast_to(table[None], (self.rows // self.clips, self.clips, width))
            return spread.reshape(self.rows, 1, width)
        start = lax.rem(self.first_row, self.clips)
        return lax.dynamic_slice_in_dim(table, start, self.rows, 0)[:, None, :]

    def by_clip(self, sums):
        width = sums.shape[-1]
        if self.rows % self.clips == 0:
            return jnp.sum(sums.reshape(self.rows // self.clips, self.clips, width), axis=0)
        start = lax.rem(self.first_row, self.clips)
        empty = jnp.zeros((self.clips, width), f32)
        return lax.dynamic_update_slice_in_dim(empty, sums, start, 0)

    def by_frame(self, entries):
        per_row = jnp.sum(entries * entries, axis=(1, 2))
        frames = max(self.rows // self.clips, 1)
        sums = jnp.sum(per_row.reshape(frames, -1), axis=1)
        if frames == FRAMES:
            return sums
        start = self.first_row // self.clips
        return lax.dynamic_update_slice_in_dim(jnp.zeros((FRAMES,), f32), sums, start, 0)

    def modulated(self, stream, mod, offset):
        normed = layer_norm(stream)[0]
        scale = 1.0 + self.by_row(mod[:, offset + 1])
        return (normed * scale + self.by_row(mod[:, offset])).astype(bf16)

    def flat(self, value):
        return value.reshape(self.rows * self.tokens, value.shape[-1])

    def full(self, value):
        return value.reshape(self.rows, self.tokens, value.shape[-1])

    def attend(self, kernel, operands, widths):
        if self.spatial:
            views = [[self.full(value) for value in group] for group in operands]
            return [self.flat(v) for v in attend_call(kernel, 0, views, widths)]
        count = self.rows * self.tokens
        out = []
        for i in range(len(operands[0])):
            views = [[group[i][None]] for group in operands]
            out.append(attend_call(kernel, count // FRAMES, views, widths)[0][0])
        return out

    def attention(self, stream, mod, weights, pump, hidden=None):
        inner = weights.shape[1] // 4
        if hidden is None:
            hidden = gather_tokens(self.modulated(stream, mod, 0))
        hidden = [self.flat(h) for h in hidden]
        w_qkv, w_proj = weights[:, : 3 * inner], weights[:, 3 * inner :]
        qkv = [dot(h, w_qkv).astype(bf16) for h in hidden]
        attended = self.attend(attend_kernel, [qkv], inner)
        attended[-1] = pump(attended[-1])
        partial = [self.full(dot_nt(a, w_proj)) for a in attended]
        branch = scatter_tokens(partial)
        branch = pump(branch)
        gated = self.by_row(mod[:, 2]) * branch
        return stream + gated, gated, (stream, branch, hidden, qkv, attended, w_qkv, w_proj)

    def mlp(self, stream, mod, weights, pump):
        inner = weights.shape[1] // 2
        hidden = [self.flat(h) for h in gather_tokens(self.modulated(stream, mod, 3))]
        hidden[-1] = pump(hidden[-1])
        w_up, w_down = weights[:, :inner], weights[:, inner:]
        pre = [dot(h, w_up) for h in hidden]
        active = [gelu_tanh(p).astype(bf16) for p in pre]
        branch = scatter_tokens([self.full(dot_nt(a, w_down)) for a in active])
        branch = pump(branch)
        gated = self.by_row(mod[:, 5]) * branch
        return stream + gated, gated, (stream, branch, hidden, pre, active, w_up, w_down)

    def branch_back(self, grad, mod, offset, branch):
        grad_branch = (grad * self.by_row(mod[:, offset + 2])).astype(bf16)
        grad_gate = self.by_clip(jnp.sum(grad * branch, axis=1))
        return [self.flat(g) for g in gather_tokens(grad_branch)], grad_gate

    def norm_back(self, grad, grad_hidden, stream, mod, offset):
        normed, inverse = layer_norm(stream)
        grad_normed = grad_hidden * (1.0 + self.by_row(mod[:, offset + 1]))
        centered = grad_normed - jnp.mean(grad_normed, axis=-1, keepdims=True)
        grad_in = inverse * (
            centered - normed * jnp.mean(grad_normed * normed, axis=-1, keepdims=True)
        )
        shift = self.by_clip(jnp.sum(grad_hidden, axis=1))
        scale = self.by_clip(jnp.sum(grad_hidden * normed, axis=1))
        return grad + grad_in, shift, scale

    def mlp_back(self, grad, mod, stored, split, pump):
        stream, branch, hidden, pre, active, w_up, w_down = stored
        grad_branch, gate = self.branch_back(grad, mod, 3, branch)
        grad_branch[-1] = pump(grad_branch[-1])
        grad_pre = [
            jax.vjp(gelu_tanh, p)[1](dot(g, w_down))[0].astype(bf16)
            for p, g in zip(pre, grad_branch)
        ]
        grad_pre[-1] = pump(grad_pre[-1])
        grad_hidden = scatter_tokens([self.full(dot_nt(g, w_up)) for g in grad_pre])
        grad_w = weight_grad((hidden, grad_pre), (grad_branch, active), split)
        grad_hidden, *grad_w = tie(grad_hidden, *grad_w)
        grad_hidden = pump(grad_hidden)
        grad, shift, scale = self.norm_back(grad, grad_hidden, stream, mod, 3)
        return grad, jnp.stack([shift, scale, gate], axis=1), grad_w

    def attention_back(self, grad, mod, stored, split, pump):
        stream, branch, hidden, qkv, attended, w_qkv, w_proj = stored
        grad_branch, gate = self.branch_back(grad, mod, 0, branch)
        grad_branch[-1] = pump(grad_branch[-1])
        grad_att = [dot(g, w_proj).astype(bf16) for g in grad_branch]
        grad_qkv = self.attend(attend_back_kernel, [qkv, grad_att], w_qkv.shape[1])
        grad_qkv[-1] = pump(grad_qkv[-1])
        grad_hidden = scatter_tokens([self.full(dot_nt(g, w_qkv)) for g in grad_qkv])
        grad_w = weight_grad((hidden, grad_qkv), (grad_branch, attended), split)
        grad_hidden, *grad_w = tie(grad_hidden, *grad_w)
        grad_hidden = pump(grad_hidden)
        grad, shift, scale = self.norm_back(grad, grad_hidden, stream, mod, 0)
        return grad, jnp.stack([shift, scale, gate], axis=1), grad_w


def to_places(stream, kind=f32):
    return lax.all_to_all(
        stream.astype(bf16), "dp", split_axis=1, concat_axis=0, tiled=True
    ).astype(kind)


def to_frames(stream):
    return lax.all_to_all(stream.astype(bf16), "dp", split_axis=0, concat_axis=1, tiled=True)


def pack(first, second):
    return jnp.concatenate([first.reshape(first.shape[0], -1), second.T], axis=1)


def gather_weights(first, second):
    return lax.all_gather(pack(first, second), "dp", axis=0, tiled=True)


def norm_rows(value):
    centered = value - jnp.mean(value, axis=-1, keepdims=True)
    return centered * lax.rsqrt(jnp.mean(centered * centered, axis=-1, keepdims=True) + epsilon)


def head_kernel(
    ring, clips, pairs, shard, small, video, out, small_out, hidden, other,
    slots, landed_small, own_sem, send_sem, recv_sem, pair_send, pair_recv, x_send, x_recv,
):
    size, me = 4 * ring, lax.axis_index("dp")
    tensor = lax.axis_index("tensor")
    after, before = lax.rem(me + 4, size), lax.rem(me + size - 4, size)
    beside, core = me ^ 2, me ^ 1
    exchange = lax.axis_size("tensor") == 2
    barrier = pltpu.get_barrier_semaphore()
    partners = [{"dp": me ^ stride} for stride in pairs]
    greeted = partners + [{"dp": after}, {"dp": before}]
    if exchange:
        greeted.append({"tensor": 1 - tensor})
    for partner in greeted:
        pl.semaphore_signal(barrier, inc=1, device_id=partner, device_id_type=MESH)
    pl.semaphore_wait(barrier, len(greeted))
    keep = pltpu.make_async_copy(shard, out.at[me], own_sem)
    keep.start()
    sent = []

    def send(source, target, out_sem, in_sem, partner):
        copy = pltpu.make_async_remote_copy(
            src_ref=source, dst_ref=target, send_sem=out_sem, recv_sem=in_sem,
            device_id=partner, device_id_type=MESH,
        )
        copy.start()
        sent.append(copy)
        return copy

    def pass_on(source, place, slot, partner):
        send(source, out.at[place], send_sem.at[slot], recv_sem.at[slot], {"dp": partner})

    def landed(place, slot):
        pltpu.make_async_remote_copy(
            src_ref=out.at[place], dst_ref=out.at[place],
            send_sem=send_sem.at[slot], recv_sem=recv_sem.at[slot],
            device_id={"dp": core}, device_id_type=MESH,
        ).wait_recv()

    flying = []

    def pair_step(k):
        if k == 0:
            slots[0] = small[...]
        else:
            flying[k - 1].wait_recv()
            slots[k] = slots[k - 1] + landed_small[k - 1]
        if k < len(partners):
            flying.append(
                send(slots.at[k], landed_small.at[k], pair_send.at[k], pair_recv.at[k], partners[k])
            )

    pair_step(0)
    step = 1
    for k in range(ring):
        place = lax.rem(me + size - 4 * k, size)
        if k:
            landed(place, k - 1)
        source = shard if k == 0 else out.at[place]
        if k < ring - 1:
            pass_on(source, place, k, after)
        pass_on(source, place, ring + k, beside)
        pass_on(source, place, 2 * ring + k, core)
        if k:
            place = lax.rem((me ^ 2) + size - 4 * (k - 1), size)
            landed(place, ring + k - 1)
            pass_on(out.at[place], place, 3 * ring + k - 1, core)
        if step <= len(partners):
            pair_step(step)
            step += 1
    while step <= len(partners):
        pair_step(step)
        step += 1
    small_out[...] = slots[len(partners)]
    if exchange:
        rows = video.shape[0]
        for r in range(rows):
            clip = r % clips if rows % clips == 0 else lax.rem(me * rows + r, clips)
            shift = slots[len(partners), pl.ds(6 * clip, 1), :]
            scale = slots[len(partners), pl.ds(6 * clip + 1, 1), :]
            normed = norm_rows(video[r].astype(f32))
            hidden[r] = (normed * (1.0 + scale) + shift).astype(bf16)
        swapped = send(hidden, other, x_send, x_recv, {"tensor": 1 - tensor})
    place = lax.rem((me ^ 2) + size - 4 * (ring - 1), size)
    landed(place, 2 * ring - 1)
    pass_on(out.at[place], place, 4 * ring - 1, core)
    for k in range(ring):
        landed(lax.rem(core + size - 4 * k, size), 2 * ring + k)
        landed(lax.rem((core ^ 2) + size - 4 * k, size), 3 * ring + k)
    keep.wait()
    if exchange:
        swapped.wait_recv()
    for copy in sent:
        copy.wait_send()


def head(shard, small, video, clips):
    ring = lax.axis_size("dp") // 4
    rows, cols = shard.shape
    pairs = [1 << bit for bit in range(lax.axis_size("dp").bit_length() - 1)]
    count = len(pairs)
    vmem, anywhere = pl.BlockSpec(memory_space=pltpu.VMEM), pl.BlockSpec(memory_space=pl.ANY)
    full, total, mine, other = pl.pallas_call(
        functools.partial(head_kernel, ring, clips, pairs),
        in_specs=[anywhere, vmem, vmem],
        out_specs=[anywhere, vmem, vmem, vmem],
        out_shape=[
            jax.ShapeDtypeStruct((4 * ring, rows, cols), bf16),
            jax.ShapeDtypeStruct(small.shape, f32),
            jax.ShapeDtypeStruct(video.shape, bf16),
            jax.ShapeDtypeStruct(video.shape, bf16),
        ],
        scratch_shapes=[
            pltpu.VMEM((count + 1,) + small.shape, f32),
            pltpu.VMEM((count,) + small.shape, f32),
            pltpu.SemaphoreType.DMA,
            pltpu.SemaphoreType.DMA((4 * ring,)),
            pltpu.SemaphoreType.DMA((4 * ring,)),
            pltpu.SemaphoreType.DMA((count,)),
            pltpu.SemaphoreType.DMA((count,)),
            pltpu.SemaphoreType.DMA,
            pltpu.SemaphoreType.DMA,
        ],
        cost_estimate=pl.CostEstimate(flops=1 << 35, bytes_accessed=8 * ring * rows * cols, transcendentals=0),
        compiler_params=pltpu.CompilerParams(
            collective_id=1, has_side_effects=True, vmem_limit_bytes=32 << 20
        ),
    )(shard, small, video)
    hidden = [mine, other] if lax.axis_size("tensor") == 2 else None
    return full.reshape(4 * ring * rows, cols), total, hidden


def assemble_kernel(ring, own, *refs):
    hops, beside, core, out, sems = refs[: ring - 1], *refs[ring - 1 :]
    size, me = 4 * ring, lax.axis_index("dp")
    copies = []

    def put(source, place):
        copy = pltpu.make_async_copy(source, out.at[place], sems.at[len(copies)])
        copy.start()
        copies.append(copy)

    for k in range(ring):
        back = lambda device: lax.rem(device + size - 4 * k, size)
        put(own if k == 0 else hops[k - 1], back(me))
        put(beside.at[k], back(me ^ 2))
        put(core.at[k], back(me ^ 1))
        put(core.at[ring + k], back(me ^ 3))
    for copy in copies:
        copy.wait()


class WeightGather:
    def __init__(self, shard):
        self.size = lax.axis_size("dp")
        self.ring = self.size // 4
        self.pieces, self.stage = [shard], 0
        self.begin()

    def begin(self):
        if self.stage < self.ring - 1:
            links = [(i, (i + 4) % self.size) for i in range(self.size)]
            self.wait = lax.ppermute(self.pieces[-1], "dp", links)
        elif self.stage == self.ring - 1:
            self.column = jnp.stack(self.pieces)
            self.wait = swap(self.column, "dp", 2, self.size)
        else:
            self.wait = swap(jnp.concatenate([self.column, self.pieces[-1]]), "dp", 1, self.size)

    def step(self, value=None):
        if self.stage > self.ring:
            return value
        if value is not None:
            value, self.wait = tie(value, self.wait)
        self.pieces.append(self.wait)
        self.stage += 1
        if self.stage <= self.ring:
            self.begin()
        return value

    def finish(self):
        while self.stage <= self.ring:
            self.step()
        rows, cols = self.pieces[0].shape
        anywhere = pl.BlockSpec(memory_space=pl.ANY)
        full = pl.pallas_call(
            functools.partial(assemble_kernel, self.ring),
            in_specs=[anywhere] * (self.ring + 2),
            out_specs=pl.BlockSpec(memory_space=pltpu.VMEM),
            out_shape=jax.ShapeDtypeStruct((self.size, rows, cols), bf16),
            scratch_shapes=[pltpu.SemaphoreType.DMA((self.size,))],
            compiler_params=pltpu.CompilerParams(vmem_limit_bytes=32 << 20),
        )(*self.pieces)
        return full.reshape(self.size * rows, cols)


def scatter_grads(grad_w):
    return lax.psum_scatter(grad_w, "dp", scatter_dimension=0, tiled=True)


def unpack(local, first, second):
    local = local.astype(f32)
    cut = local.shape[1] - second.shape[0]
    return local[:, :cut].reshape(first.shape), local[:, cut:].T


def finish_spatial(gw_mlp, gw_attn, dmod_attn, dmod_mlp):
    small = jnp.concatenate([dmod_attn.reshape(-1), dmod_mlp.reshape(-1)]).reshape(-1, 128)
    return tail([*gw_mlp, gw_attn], small)


def body(
    video_in,
    condition,
    adaln_spatial,
    qkv_spatial,
    proj_spatial,
    up_spatial,
    down_spatial,
    adaln_temporal,
    qkv_temporal,
    proj_temporal,
    up_temporal,
    down_temporal,
    grad_output,
):
    rows, tokens, width = video_in.shape
    clips = condition.shape[0]
    dp, me = lax.axis_size("dp"), lax.axis_index("dp")
    spatial = Layer(rows, tokens, clips, True, me * rows)
    temporal = Layer(rows * dp, tokens // dp, clips, False, 0)

    w_mlp_s = gather_weights(up_spatial, down_spatial)
    w_mlp_t = gather_weights(up_temporal, down_temporal)

    share = adaln_spatial.shape[0]
    cond_rows = lax.dynamic_slice_in_dim(condition, me * share, share, 1)
    silu_rows, silu_pull = jax.vjp(jax.nn.silu, cond_rows)
    silu_low = silu_rows.astype(bf16)
    flat_s = adaln_spatial.reshape(share, -1)
    flat_t = adaln_temporal.reshape(share, -1)
    mods = jnp.stack([dot(silu_low, flat_s), dot(silu_low, flat_t)]).reshape(-1, width)
    w_attn_s, mods, hidden = head(pack(qkv_spatial, proj_spatial), mods, video_in, clips)

    keep = lambda value: value
    mod_s, mod_t = mods.reshape(2, clips, 6, width)
    fused = lax.axis_size("tensor") == 2 and rows % clips == 0
    if fused:
        flat = video_in.reshape(rows * tokens, width)
        mine = [spatial.flat(h) for h in hidden]
        s1, _, b1, q1, *kept1, w_attn_t = forward_call(
            spatial, True, flat, mod_s, w_attn_s, mine, pack(qkv_temporal, proj_temporal)
        )
        w_attn_t = w_attn_t.reshape(width, -1)
        kept1 = (flat, b1, mine, kept1[:2], kept1[2:])
        s2, low2, b2, q2, *kept2 = forward_call(spatial, False, s1, mod_s, w_mlp_s)
        kept2 = (s1, b2, kept2[:2], kept2[2:4], kept2[4:])
        placed = to_places(spatial.full(low2), bf16).reshape(-1, width)
        placed, grad_output = tie(placed, grad_output)
        s3, _, b3, q3, *kept3 = forward_call(temporal, True, placed, mod_t, w_attn_t)
        kept3 = (placed, b3, kept3[4:], kept3[:2], kept3[2:4])
        grad = to_places(grad_output, bf16)
        _, low4, b4, q4, *kept4 = forward_call(temporal, False, s3, mod_t, w_mlp_t)
        kept4 = (s3, b4, kept4[:2], kept4[2:4], kept4[4:])
        spots = []
        for layer, values in ((spatial, (q1, q2)), (temporal, (q3, q4))):
            for value in values:
                empty = jnp.zeros((2, FRAMES), f32)
                spots.append(
                    lax.dynamic_update_slice_in_dim(empty, value[:, :, 0], layer.first_row // clips, 1)
                )
        squares = jnp.concatenate([jnp.stack([v[i] for v in spots]) for i in range(2)])
    else:
        stream0 = video_in.astype(f32)
        shard, mods = tie(pack(qkv_temporal, proj_temporal), mods)
        mod_s, mod_t = mods.reshape(2, clips, 6, width)
        later = WeightGather(shard)
        s1, g1, kept1 = spatial.attention(stream0, mod_s, w_attn_s, later.step, hidden)
        s2, g2, kept2 = spatial.mlp(s1, mod_s, w_mlp_s, later.step)
        placed = later.step(to_places(s2))
        w_attn_t = later.finish()
        placed, grad_output = tie(placed, grad_output)
        grad = to_places(grad_output)
        s3, g3, kept3 = temporal.attention(placed, mod_t, w_attn_t, keep)
        s4, g4, kept4 = temporal.mlp(s3, mod_t, w_mlp_t, keep)
        video_out = to_frames(s4)
        squares = jnp.stack(
            [spatial.by_frame(v) for v in (s1, s2)]
            + [temporal.by_frame(v) for v in (s3, s4)]
            + [spatial.by_frame(v) for v in (g1, g2)]
            + [temporal.by_frame(v) for v in (g3, g4)]
        )
    by_span = lambda dmod: jnp.moveaxis(dmod.reshape(3, clips, width), 0, 1)
    if fused:
        grad, dmod4, gw4 = mlp_back_call(temporal, grad, mod_t, (*kept4[:5], w_mlp_t), True)
        own4 = scatter_grads(gw4)
        video_out = to_frames(temporal.full(low4))
        grad, video_out = tie(grad, video_out)
        grad, dmod3, gw3 = attention_back_call(temporal, grad, mod_t, (*kept3[:5], w_attn_t))
        grad = temporal.full(grad)
    else:
        grad, dmod4, (gw4,) = temporal.mlp_back(grad, mod_t, kept4, False, keep)
        own4 = scatter_grads(gw4)
        grad, dmod3, (gw3,) = temporal.attention_back(grad, mod_t, kept3, False, keep)
        own3 = scatter_grads(gw3)
    if fused:
        grad, dmod2, up, down = mlp_back_call(
            spatial, to_frames(grad), mod_s, (*kept2[:5], w_mlp_s), False
        )
        own4, gw3 = tie(own4, gw3)
        own3 = scatter_grads(gw3)
        line = jnp.pad(squares.reshape(1, -1), ((0, 0), (0, width - squares.size)))
        small = jnp.concatenate([dmod2, dmod3, dmod4, line], axis=0)
        grad, grad_up_s, down_s, own1, late = attention_back_call(
            spatial, grad, mod_s, (*kept1[:5], w_attn_s), (up, down), small
        )
        grad = spatial.full(grad)
        dmod1, dmod2, dmod3, dmod4 = [
            by_span(late[3 * clips * i : 3 * clips * (i + 1)]) for i in range(4)
        ]
        squares = late[12 * clips, : squares.size].reshape(8, FRAMES)
    else:
        early = AllSum(
            jnp.concatenate([dmod3.reshape(-1), dmod4.reshape(-1), squares.reshape(-1)]).reshape(-1, 128)
        )
        grad = early.step(to_frames(grad).astype(f32))
        grad, dmod2, gw2 = spatial.mlp_back(grad, mod_s, kept2, True, early.step)
        grad, own4 = tie(grad, own4)
        grad, dmod1, (gw1,) = spatial.attention_back(grad, mod_s, kept1, False, early.step)
        grad_up_s, down_s, own1, late = finish_spatial(gw2, gw1, dmod1, dmod2)
        late = late.reshape(2, clips, 3, width)
        dmod1, dmod2 = late[0], late[1]
        cut = clips * 3 * width
        flat_early = early.finish().reshape(-1)
        dmod3 = flat_early[:cut].reshape(clips, 3, width)
        dmod4 = flat_early[cut : 2 * cut].reshape(clips, 3, width)
        squares = flat_early[2 * cut :].reshape(8, FRAMES)
    grad_up_t, grad_down_t = unpack(own4, up_temporal, down_temporal)
    grad_qkv_t, grad_proj_t = unpack(own3, qkv_temporal, proj_temporal)
    grad_down_s = down_s.T
    grad_qkv_s, grad_proj_s = unpack(own1, qkv_spatial, proj_spatial)
    frame_rms = jnp.sqrt(squares / (clips * PATCHES * width))
    shift_grad = jnp.stack([d[:, 0] for d in (dmod1, dmod2, dmod3, dmod4)])
    silu_wide = silu_low.astype(f32)

    def adaln_back(flat, dmod_attn, dmod_mlp, shape):
        dmod = jnp.concatenate([dmod_attn, dmod_mlp], axis=1).reshape(clips, -1)
        grad_w = jnp.sum(silu_wide[:, :, None] * dmod[:, None, :], axis=0).reshape(shape)
        back = lax.dot_general(
            dmod, flat.astype(f32), (((1,), (1,)), ((), ())), precision=highest
        )
        return grad_w, back

    adaln_t_grad, back_t = adaln_back(flat_t, dmod3, dmod4, adaln_temporal.shape)
    adaln_s_grad, back_s = adaln_back(flat_s, dmod1, dmod2, adaln_spatial.shape)
    condition_grad = silu_pull(back_s + back_t)[0]
    return (
        video_out,
        grad,
        condition_grad,
        adaln_s_grad,
        grad_qkv_s,
        grad_proj_s,
        grad_up_s,
        grad_down_s,
        adaln_t_grad,
        grad_qkv_t,
        grad_proj_t,
        grad_up_t,
        grad_down_t,
        frame_rms,
        shift_grad,
    )


def solution(mesh):
    return jax.shard_map(
        body,
        mesh=mesh,
        in_specs=(
            P("dp", "tensor", None),
            P(),
            P("dp", None, None),
            P("dp", None, "tensor"),
            P("tensor", "dp"),
            P("dp", "tensor"),
            P("tensor", "dp"),
            P("dp", None, None),
            P("dp", None, "tensor"),
            P("tensor", "dp"),
            P("dp", "tensor"),
            P("tensor", "dp"),
            P("dp", "tensor", None),
        ),
        out_specs=(
            P("dp", "tensor", None),
            P("dp", "tensor", None),
            P(None, "dp"),
            P("dp", None, None),
            P("dp", None, "tensor"),
            P("tensor", "dp"),
            P("dp", "tensor"),
            P("tensor", "dp"),
            P("dp", None, None),
            P("dp", None, "tensor"),
            P("tensor", "dp"),
            P("dp", "tensor"),
            P("tensor", "dp"),
            P(),
            P(),
        ),
        check_vma=False,
    )
```

```python
import functools

import jax
import jax.numpy as jnp
from jax import lax
from jax.experimental import pallas as pl
from jax.experimental.pallas import tpu as pltpu
from jax.sharding import PartitionSpec as P

HEAD_DIM = 72
PATCHES = 256
FRAMES = 16

highest = lax.Precision.HIGHEST
epsilon = 1e-06
bf16 = jnp.bfloat16
f32 = jnp.float32
MESH = pl.DeviceIdType.MESH


def dot(a, b):
    return jnp.dot(a, b, preferred_element_type=f32)


def dot_nt(a, b):
    return lax.dot_general(a, b, (((1,), (1,)), ((), ())), preferred_element_type=f32)


def dot_tn(a, b):
    return lax.dot_general(a, b, (((0,), (0,)), ((), ())), preferred_element_type=f32)


def layer_norm(stream):
    average = jnp.mean(stream, axis=-1, keepdims=True)
    centered = stream - average
    inverse = lax.rsqrt(jnp.mean(centered * centered, axis=-1, keepdims=True) + epsilon)
    return (centered * inverse, inverse)


def gelu_tanh(pre_act):
    return jax.nn.gelu(pre_act, approximate=True)


def swap(value, axis, stride, size):
    return lax.ppermute(value, axis, [(i, i ^ stride) for i in range(size)])


def all_sum(value, axes):
    for axis in axes:
        size = lax.axis_size(axis)
        if size & (size - 1):
            value = lax.psum(value, axis)
            continue
        stride = 1
        while stride < size:
            value = value + swap(value, axis, stride, size)
            stride *= 2
    return value


def gather_tokens(local):
    size = lax.axis_size("tensor")
    if size == 2:
        other = swap(local, "tensor", 1, 2)
        return [local, other]
    return list(lax.all_gather(local, "tensor", axis=0, tiled=False))


def scatter_tokens(parts):
    size = lax.axis_size("tensor")
    if size == 2:
        return parts[0] + swap(parts[1].astype(bf16), "tensor", 1, 2).astype(f32)
    stacked = jnp.stack([part.astype(bf16) for part in parts])
    return lax.psum_scatter(stacked, "tensor", scatter_dimension=0, tiled=False).astype(f32)


def softmax_scores(queries, keys, residue):
    scores = dot_nt(queries, keys) * HEAD_DIM ** (-0.5)
    if residue:
        row = lax.broadcasted_iota(jnp.int32, scores.shape, 0)
        col = lax.broadcasted_iota(jnp.int32, scores.shape, 1)
        scores = jnp.where(lax.rem(row, residue) == lax.rem(col, residue), scores, -1e30)
    unnormed = jnp.exp(scores - jnp.max(scores, axis=-1, keepdims=True))
    return unnormed * (1.0 / jnp.sum(unnormed, axis=-1, keepdims=True))


def joined(refs):
    blocks = [ref[0] for ref in refs]
    return blocks[0] if len(blocks) == 1 else jnp.concatenate(blocks, axis=0)


def store_rows(refs, columns, value):
    start = 0
    for ref in refs:
        ref[0, :, columns] = value[start : start + ref.shape[1]]
        start += ref.shape[1]


def attend_kernel(count, residue, *refs):
    ins, outs = refs[:count], refs[count:]
    qkv = joined(ins)
    inner = qkv.shape[1] // 3
    for start in range(0, inner, HEAD_DIM):
        q, k, v = (
            qkv[:, part * inner + start : part * inner + start + HEAD_DIM] for part in range(3)
        )
        probs = softmax_scores(q, k, residue).astype(bf16)
        store_rows(outs, slice(start, start + HEAD_DIM), dot(probs, v).astype(bf16))


def attend_back_kernel(count, residue, *refs):
    ins, grads, outs = refs[:count], refs[count : 2 * count], refs[2 * count :]
    qkv, grad_att = joined(ins), joined(grads)
    inner = grad_att.shape[1]
    for start in range(0, inner, HEAD_DIM):
        q, k, v = (
            qkv[:, part * inner + start : part * inner + start + HEAD_DIM] for part in range(3)
        )
        grad_out = grad_att[:, start : start + HEAD_DIM]
        probs = softmax_scores(q, k, residue)
        grad_probs = dot_nt(grad_out, v)
        mean = jnp.sum(probs * grad_probs, axis=-1, keepdims=True)
        grad_scaled = (probs * (grad_probs - mean) * HEAD_DIM ** (-0.5)).astype(bf16)
        results = (
            dot(grad_scaled, k),
            dot_tn(grad_scaled, q),
            dot_tn(probs.astype(bf16), grad_out),
        )
        for part, value in enumerate(results):
            left = part * inner + start
            store_rows(outs, slice(left, left + HEAD_DIM), value.astype(bf16))


def attend_call(kernel, residue, operands, widths):
    count = len(operands[0])
    rows, tokens = operands[0][0].shape[:2]
    spec = lambda width: pl.BlockSpec((1, tokens, width), lambda r: (r, 0, 0))
    flat = [value for group in operands for value in group]
    length = count * tokens
    heads = widths // HEAD_DIM
    return pl.pallas_call(
        functools.partial(kernel, count, residue),
        grid=(rows,),
        in_specs=[spec(value.shape[2]) for value in flat],
        out_specs=[spec(widths) for _ in range(count)],
        out_shape=[jax.ShapeDtypeStruct((rows, tokens, widths), bf16) for _ in range(count)],
        cost_estimate=pl.CostEstimate(
            flops=rows * heads * length * length * HEAD_DIM * 4,
            bytes_accessed=sum(v.size * 2 for v in flat),
            transcendentals=rows * heads * length * length,
        ),
        compiler_params=pltpu.CompilerParams(vmem_limit_bytes=48 << 20),
    )(*flat)


def weight_grad_kernel(count, *refs):
    ins, outs = refs[: 4 * count], refs[4 * count :]
    left = 0
    for pair in range(2):
        base = 2 * pair * count
        out = outs[pair % len(outs)]
        left = left if len(outs) == 1 else 0
        rows = jnp.concatenate([ref[...] for ref in ins[base : base + count]], axis=0)
        cols = ins[base + count : base + 2 * count]
        width = cols[0].shape[1]
        step = width if width % 1152 else 1152
        for start in range(0, width, step):
            right = jnp.concatenate([ref[:, start : start + step] for ref in cols], axis=0)
            out[:, left + start : left + start + step] = dot_tn(rows, right).astype(bf16)
        left += width


def weight_grad(first, second, split):
    count, width = len(first[0]), first[0][0].shape[1]
    block = 384 if width % 384 == 0 else width
    ins, specs = [], []
    for rows, cols in (first, second):
        ins += rows + cols
        specs += [pl.BlockSpec((r.shape[0], block), lambda i: (0, i)) for r in rows]
        specs += [pl.BlockSpec(c.shape, lambda i: (0, 0)) for c in cols]
    wide = [first[1][0].shape[1], second[1][0].shape[1]]
    total = sum(wide)
    wide = wide if split else [total]
    tokens = count * first[0][0].shape[0]
    return pl.pallas_call(
        functools.partial(weight_grad_kernel, count),
        grid=(width // block,),
        in_specs=specs,
        out_specs=[pl.BlockSpec((block, w), lambda i: (i, 0)) for w in wide],
        out_shape=[jax.ShapeDtypeStruct((width, w), bf16) for w in wide],
        cost_estimate=pl.CostEstimate(
            flops=2 * tokens * width * total,
            bytes_accessed=2 * width * total + 2 * tokens * (2 * width + total),
            transcendentals=0,
        ),
        compiler_params=pltpu.CompilerParams(vmem_limit_bytes=48 << 20),
    )(*ins)


def tie(*values):
    return lax.optimization_barrier(values)


class AllSum:
    def __init__(self, value):
        self.value = value
        self.pairs = [
            (axis, 1 << bit)
            for axis in ("tensor", "dp")
            for bit in range(lax.axis_size(axis).bit_length() - 1)
        ]
        self.begin()

    def begin(self):
        axis, stride = self.pairs[0]
        self.wait = swap(self.value, axis, stride, lax.axis_size(axis))

    def step(self, value=None):
        if not self.pairs:
            return value
        if value is not None:
            value, self.wait = tie(value, self.wait)
        self.value = self.value + self.wait
        self.pairs.pop(0)
        if self.pairs:
            self.begin()
        return value

    def finish(self):
        while self.pairs:
            self.step()
        return self.value


def exchange_pairs():
    return [
        (axis, 1 << bit)
        for axis in ("tensor", "dp")
        for bit in range(lax.axis_size(axis).bit_length() - 1)
    ]


class Scatter:
    def __init__(self, grad, out, refs, flipped):
        self.grad, self.out, self.flipped = grad, out, flipped
        self.own, self.own_sem, self.core_in, self.y_in, self.ring_in, self.send_sem, self.recv_sem = refs
        self.ring = grad.shape[0]
        self.stages = self.ring + 2
        self.chunks = self.send_sem.shape[1]
        self.width = grad.shape[-1] // self.chunks
        me, size = lax.axis_index("dp"), 4 * self.ring
        self.me, self.at, self.y, self.core = me, me // 4, lax.rem(me // 2, 2), lax.rem(me, 2)
        self.after, self.before = lax.rem(me + 4, size), lax.rem(me + size - 4, size)
        self.pending = {}
        self.load = None

    @staticmethod
    def scratch(ring, rows, cols, flips=True):
        chunks = cols // 384 if cols % 384 == 0 else 1
        return [
            pltpu.VMEM((ring, 2, rows, cols), bf16),
            pltpu.SemaphoreType.DMA,
            pltpu.VMEM((ring, 2, rows, cols), bf16),
            pltpu.VMEM((ring, rows, cols), bf16),
            pltpu.VMEM((ring - 1, 2 if flips else 1, rows, cols), bf16),
            pltpu.SemaphoreType.DMA((ring + 1, chunks)),
            pltpu.SemaphoreType.DMA((ring + 1, chunks)),
        ]

    def neighbours(self):
        return [{"dp": partner} for partner in (self.after, self.before, self.me ^ 1, self.me ^ 2)]

    def begin(self):
        self.load = pltpu.make_async_copy(self.grad.at[:, :, self.core], self.own, self.own_sem)
        self.load.start()

    def send(self, s, j, source, target, partner):
        copy = pltpu.make_async_remote_copy(
            src_ref=source, dst_ref=target, send_sem=self.send_sem.at[s, j], recv_sem=self.recv_sem.at[s, j],
            device_id={"dp": partner}, device_id_type=MESH,
        )
        copy.start()
        self.pending[s, j] = copy

    def stage(self, s, j):
        cols = pl.ds(j * self.width, self.width)
        ring, y, at = self.ring, self.y, self.at
        if s == 0:
            source = self.grad.at[:, :, 1 - self.core, :, cols]
            return self.send(s, j, source, self.core_in.at[:, :, :, cols], self.me ^ 1)
        if self.load is not None:
            self.load.wait()
            self.load = None
        self.pending[s - 1, j].wait_recv()
        flipped = self.flipped(j)
        if s == 1:
            total = self.own[:, :, :, cols].astype(f32) + self.core_in[:, :, :, cols].astype(f32)
            self.own[:, :, :, cols] = total.astype(bf16)
        if not flipped:
            if s == 1:
                return self.send(s, j, self.own.at[:, 1 - y, :, cols], self.y_in.at[:, :, cols], self.me ^ 2)
            h = s - 2
            if h == 0:
                total = self.own[:, y, :, cols].astype(f32) + self.y_in[:, :, cols].astype(f32)
                self.y_in[:, :, cols] = total.astype(bf16)
                source = self.y_in.at[lax.rem(at + ring - 1, ring), :, cols]
            else:
                total = self.y_in[lax.rem(at + ring - 1 - h, ring), :, cols].astype(f32)
                total = total + self.ring_in[h - 1, 0, :, cols].astype(f32)
                if h == ring - 1:
                    self.out[:, cols] = total
                    return None
                self.ring_in[h - 1, 0, :, cols] = total.astype(bf16)
                source = self.ring_in.at[h - 1, 0, :, cols]
            return self.send(s, j, source, self.ring_in.at[h, 0, :, cols], self.after)
        h = s - 1
        if h == 0:
            source = self.own.at[lax.rem(at + ring - 1, ring), :, :, cols]
            return self.send(s, j, source, self.ring_in.at[h, :, :, cols], self.after)
        if h < ring:
            total = self.own[lax.rem(at + ring - 1 - h, ring), :, :, cols].astype(f32)
            total = total + self.ring_in[h - 1, :, :, cols].astype(f32)
            self.ring_in[h - 1, :, :, cols] = total.astype(bf16)
            if h < ring - 1:
                source = self.ring_in.at[h - 1, :, :, cols]
                return self.send(s, j, source, self.ring_in.at[h, :, :, cols], self.after)
            source = self.ring_in.at[h - 1, 1 - y, :, cols]
            return self.send(s, j, source, self.y_in.at[0, :, cols], self.me ^ 2)
        total = self.ring_in[ring - 2, y, :, cols].astype(f32)
        self.out[:, cols] = total + self.y_in[0, :, cols].astype(f32)
        return None

    def finish(self):
        for copy in self.pending.values():
            copy.wait_send()


class Pipeline:
    def __init__(self):
        self.jobs, self.queue, self.flight = [], [], []

    def add(self, jobs):
        self.jobs = self.jobs + jobs
        self.queue += [(job, j) for job in jobs for j in range(job.chunks)]
        for job in jobs:
            job.begin()

    def tick(self):
        for entry in self.flight:
            job, j, s, age = entry
            if age >= max(2 * s - 1, 1):
                job.stage(s, j)
                entry[2] += 1
            entry[3] += 1
        self.flight = [entry for entry in self.flight if entry[2] < entry[0].stages]
        if self.queue:
            job, j = self.queue.pop(0)
            job.stage(0, j)
            self.flight.append([job, j, 1, 1])
        return bool(self.queue or self.flight)

    def finish(self):
        while self.tick():
            pass
        for job in self.jobs:
            job.finish()


class SmallSum:
    def __init__(self, pairs, value, out, refs):
        self.slots, self.landed, self.send_sem, self.recv_sem = refs
        self.value, self.out, self.copies = value, out, []
        self.partners = [{axis: lax.axis_index(axis) ^ stride} for axis, stride in pairs]
        self.k = 0

    @staticmethod
    def scratch(count, shape):
        return [
            pltpu.VMEM((count + 1,) + shape, f32),
            pltpu.VMEM((count,) + shape, f32),
            pltpu.SemaphoreType.DMA((count,)),
            pltpu.SemaphoreType.DMA((count,)),
        ]

    def tick(self):
        k, self.k = self.k, self.k + 1
        if k > len(self.partners):
            return False
        if k == 0:
            self.slots[0] = self.value[...]
        else:
            self.copies[k - 1].wait_recv()
            self.slots[k] = self.slots[k - 1] + self.landed[k - 1]
        if k == len(self.partners):
            self.out[...] = self.slots[k]
            return False
        copy = pltpu.make_async_remote_copy(
            src_ref=self.slots.at[k], dst_ref=self.landed.at[k],
            send_sem=self.send_sem.at[k], recv_sem=self.recv_sem.at[k],
            device_id=self.partners[k], device_id_type=MESH,
        )
        copy.start()
        self.copies.append(copy)
        return True

    def finish(self):
        while self.tick():
            pass
        for copy in self.copies:
            copy.wait_send()


def greet(partners):
    barrier = pltpu.get_barrier_semaphore()
    for partner in partners:
        pl.semaphore_signal(barrier, inc=1, device_id=partner, device_id_type=MESH)
    pl.semaphore_wait(barrier, len(partners))


class Swap:
    def __init__(self, source, target, sems, k):
        self.copy = pltpu.make_async_remote_copy(
            src_ref=source, dst_ref=target, send_sem=sems.at[0, k], recv_sem=sems.at[1, k],
            device_id={"tensor": 1 - lax.axis_index("tensor")}, device_id_type=MESH,
        )
        self.copy.start()


class Exchange:
    def __init__(self, source, target, sems):
        self.source, self.target = source, target
        self.send_sem, self.recv_sem, self.own_sem = sems
        self.size, self.me = source.shape[0], lax.axis_index("dp")

    @staticmethod
    def scratch(size):
        return [pltpu.SemaphoreType.DMA((size - 1,))] * 2 + [pltpu.SemaphoreType.DMA]

    def others(self):
        return [{"dp": lax.rem(self.me + k, self.size)} for k in range(1, self.size)]

    def start(self):
        self.own = pltpu.make_async_copy(
            self.source.at[self.me], self.target.at[self.me], self.own_sem
        )
        self.own.start()
        self.copies = []
        for k, partner in enumerate(self.others()):
            copy = pltpu.make_async_remote_copy(
                src_ref=self.source.at[partner["dp"]], dst_ref=self.target.at[self.me],
                send_sem=self.send_sem.at[k], recv_sem=self.recv_sem.at[k],
                device_id=partner, device_id_type=MESH,
            )
            copy.start()
            self.copies.append(copy)

    def finish(self):
        self.own.wait()
        for copy in self.copies:
            copy.wait_recv()
        for copy in self.copies:
            copy.wait_send()


def spread(value, rows, clips):
    return value.reshape(rows // clips, clips, value.shape[0] // rows, value.shape[1])


def clip_rows(mods, clips, span):
    rows = [mods[6 * c + span : 6 * c + span + 1, :] for c in range(clips)]
    return jnp.stack(rows, axis=0)[None]


def clip_sums(value, rows, clips):
    return jnp.sum(spread(value, rows, clips), axis=(0, 2))


def norm_back_rows(grad, grad_hidden, stream, scale, rows, clips):
    stream = stream.astype(f32)
    centered = stream - jnp.mean(stream, axis=-1, keepdims=True)
    inverse = lax.rsqrt(jnp.mean(centered * centered, axis=-1, keepdims=True) + epsilon)
    normed = centered * inverse
    grad_normed = (spread(grad_hidden, rows, clips) * (1.0 + scale)).reshape(grad_hidden.shape)
    flat = grad_normed - jnp.mean(grad_normed, axis=-1, keepdims=True)
    slope = jnp.mean(grad_normed * normed, axis=-1, keepdims=True)
    grad_in = grad.astype(f32) + inverse * (flat - normed * slope)
    return grad_in, clip_sums(grad_hidden, rows, clips), clip_sums(grad_hidden * normed, rows, clips)


def gradient_blocks(target, value):
    ring, rows = target.shape[0], target.shape[3]
    for k in range(4 * ring):
        target[k // 4, (k // 2) % 2, k % 2] = value[k * rows : (k + 1) * rows].astype(bf16)


def attention_back_kernel(rows, clips, spatial, extra, tailing, pairs, *refs):
    grad, branch, stream, mods, hidden0, hidden1, qkv0, qkv1, att0, att1, weights, *refs = refs
    others, refs = refs[:extra], refs[extra:]
    if tailing:
        dmod_in, grad_out, *refs = refs
    other_outs, refs = refs[:extra], refs[extra:]
    if tailing:
        own_outs, small_out, early_out, refs = refs[:4], refs[4], refs[5], refs[6:]
    else:
        dmod_out, gw_out, landed, *refs = refs
    w, w_sem, db0, db1, part_out, part_in, keep, ga0, ga1, x_sems, *refs = refs
    dqkv, refs = (refs[:3], refs[3:6]), refs[6:]
    inner = att0.shape[1]
    count = grad.shape[0]
    jobs = []
    for i in range(extra):
        jobs.append(Scatter(others[i], other_outs[i], refs[7 * i : 7 * i + 7], lambda j: j % 6 == 5))
    refs = refs[7 * extra :]
    greeted = [{"tensor": 1 - lax.axis_index("tensor")}]
    if tailing:
        small, gw, refs = refs[0], refs[1:5], refs[5:]
        own_jobs = [
            Scatter(gw[i], own_outs[i], refs[7 * i : 7 * i + 7], lambda j: False) for i in range(4)
        ]
        total = SmallSum(pairs, small, small_out, refs[28:32])
        early = SmallSum(pairs, dmod_in, early_out, refs[32:])
        greeted = total.partners + [{"dp": jobs[0].after}, {"dp": jobs[0].before}]
    else:
        low, *refs = refs
        exchange = Exchange(low, landed, refs)
        greeted += exchange.others()
    greet(greeted)
    load = pltpu.make_async_copy(weights, w, w_sem)
    load.start()
    db0[...] = (
        (spread(grad[...].astype(f32), rows, clips) * clip_rows(mods, clips, 2)).reshape(grad.shape).astype(bf16)
    )
    first = Swap(db0, db1, x_sems, 0)
    pipeline = Pipeline()
    pipeline.add(jobs)

    def tick():
        pipeline.tick()
        if tailing:
            early.tick()

    dgate = clip_sums(grad[...].astype(f32) * branch[...], rows, clips)
    load.wait()
    w_proj = w[:, 3 * inner :]
    ga0[...] = dot(db0[...], w_proj).astype(bf16)
    tick()
    tick()

    def heads(pieces):
        take = lambda refs, cols: (
            refs[pieces[0][0]][pl.ds(*pieces[0][1:]), cols]
            if len(pieces) == 1
            else jnp.concatenate([refs[i][pl.ds(r, n), cols] for i, r, n in pieces], axis=0)
        )
        residue = 0 if spatial else count // FRAMES
        for h, start in enumerate(range(0, inner, HEAD_DIM)):
            q, k, v = (
                take((qkv0, qkv1), slice(p * inner + start, p * inner + start + HEAD_DIM)) for p in range(3)
            )
            cols = slice(start, start + HEAD_DIM)
            grad_out_h = take((ga0, ga1), cols)
            probs = softmax_scores(q, k, residue)
            grad_probs = dot_nt(grad_out_h, v)
            mean = jnp.sum(probs * grad_probs, axis=-1, keepdims=True)
            scaled = (probs * (grad_probs - mean) * HEAD_DIM ** (-0.5)).astype(bf16)
            results = (dot(scaled, k), dot_tn(scaled, q), dot_tn(probs.astype(bf16), grad_out_h))
            for p, value in enumerate(results):
                at = 0
                for i, r, n in pieces:
                    dqkv[i][p][pl.ds(r, n), cols] = value[at : at + n].astype(bf16)
                    at += n
            if h % 4 == 3:
                tick()

    def grad_hidden(i):
        value = dot_nt(dqkv[i][0][...], w[:, :inner])
        value += dot_nt(dqkv[i][1][...], w[:, inner : 2 * inner])
        return value + dot_nt(dqkv[i][2][...], w[:, 2 * inner : 3 * inner])

    if not spatial:
        heads([(0, 0, count)])
    first.copy.wait_recv()
    ga1[...] = dot(db1[...], w_proj).astype(bf16)
    tick()
    if spatial:
        tokens = count // rows
        for r in range(rows):
            heads([(0, r * tokens, tokens), (1, r * tokens, tokens)])
    else:
        heads([(1, 0, count)])
    part_out[...] = grad_hidden(1).astype(bf16)
    second = Swap(part_out, part_in, x_sems, 1)
    tick()
    keep[...] = grad_hidden(0)
    tick()
    both = lambda a, b: jnp.concatenate([a[...], b[...]], axis=0)
    for p in range(4):
        left = both(hidden0, hidden1) if p < 3 else both(db0, db1)
        right = both(dqkv[0][p], dqkv[1][p]) if p < 3 else both(att0, att1)
        value = dot_tn(left, right)
        cols = slice(p * inner, (p + 1) * inner)
        if tailing:
            gradient_blocks(gw[p], value)
        else:
            gw_out[:, cols] = value.astype(bf16)
        if p % 2:
            tick()
    if tailing:
        pipeline.add(own_jobs)
    second.copy.wait_recv()
    result, dshift, dscale = norm_back_rows(
        grad[...], keep[...] + part_in[...].astype(f32), stream[...], clip_rows(mods, clips, 1), rows, clips
    )
    if tailing:
        grad_out[...] = result
    else:
        low[...] = result.reshape(low.shape).astype(bf16)
        exchange.start()
    dmod = (dshift, dscale, dgate)
    if tailing:
        for k, value in enumerate(dmod):
            small[k * clips : (k + 1) * clips] = value
        more = total.tick()
        while more:
            pipeline.tick()
            more = total.tick()
        pipeline.finish()
        total.finish()
        early.finish()
    else:
        for k, value in enumerate(dmod):
            dmod_out[k * clips : (k + 1) * clips] = value
        pipeline.finish()
        exchange.finish()
    for exchange in (first, second):
        exchange.copy.wait_send()


def attention_back_call(layer, grad, mod, stored, others=(), dmod_in=None):
    stream, branch, hidden, qkv, attended, weights = stored
    rows, clips, count = layer.rows, layer.clips, layer.rows * layer.tokens
    width, inner, ring = weights.shape[0], attended[0].shape[1], lax.axis_size("dp") // 4
    share = width // (4 * ring)
    pairs = exchange_pairs()
    others = [g.reshape(ring, 2, 2, share, g.shape[1]) for g in others]
    vmem, anywhere = pl.BlockSpec(memory_space=pltpu.VMEM), pl.BlockSpec(memory_space=pl.ANY)
    args = [layer.flat(grad), layer.flat(branch), layer.flat(stream), mod.reshape(-1, width)]
    args += [*hidden, *qkv, *attended]
    specs = [vmem] * len(args) + [anywhere] * (1 + len(others))
    args += [weights, *others]
    shape = jax.ShapeDtypeStruct
    outs = [shape((count, width), f32)] if dmod_in is not None else []
    scratch = [pltpu.VMEM(weights.shape, bf16), pltpu.SemaphoreType.DMA]
    scratch += [pltpu.VMEM((count, width), bf16)] * 4 + [pltpu.VMEM((count, width), f32)]
    scratch += [pltpu.VMEM((count, inner), bf16)] * 2 + [pltpu.SemaphoreType.DMA((2, 2))]
    scratch += [pltpu.VMEM((count, inner), bf16)] * 6
    outs += [shape((share, g.shape[-1]), f32) for g in others]
    for g in others:
        scratch += Scatter.scratch(ring, share, g.shape[-1])
    tailing = dmod_in is not None
    if tailing:
        args.append(dmod_in)
        specs.append(vmem)
        outs += [shape((share, inner), f32)] * 4
        total = (3 * clips, width)
        outs += [shape(total, f32), shape(dmod_in.shape, f32)]
        scratch.append(pltpu.VMEM(total, f32))
        scratch += [pltpu.VMEM((ring, 2, 2, share, inner), bf16)] * 4
        for _ in range(4):
            scratch += Scatter.scratch(ring, share, inner, False)
        scratch += SmallSum.scratch(len(pairs), total) + SmallSum.scratch(len(pairs), dmod_in.shape)
    else:
        blocks = (4 * ring, count // (4 * ring), width)
        outs += [shape((3 * clips, width), f32), shape((width, 4 * inner), bf16), shape(blocks, bf16)]
        scratch += [pltpu.VMEM(blocks, bf16)] + Exchange.scratch(4 * ring)
    return pl.pallas_call(
        functools.partial(attention_back_kernel, rows, clips, layer.spatial, len(others), tailing, pairs),
        in_specs=specs,
        out_specs=[vmem] * len(outs),
        out_shape=outs,
        scratch_shapes=scratch,
        cost_estimate=pl.CostEstimate(flops=1 << 35, bytes_accessed=1 << 25, transcendentals=0),
        compiler_params=pltpu.CompilerParams(
            collective_id=2 + layer.spatial, has_side_effects=True, vmem_limit_bytes=62 << 20
        ),
    )(*args)


class Gather:
    def __init__(self, ring, shard, out, refs):
        self.ring, self.shard, self.out = ring, shard, out
        self.own_sem, self.send_sem, self.recv_sem = refs
        self.me, self.size, self.sent = lax.axis_index("dp"), 4 * ring, []
        self.k = 0

    @staticmethod
    def scratch(ring):
        return [pltpu.SemaphoreType.DMA] + [pltpu.SemaphoreType.DMA((4 * ring,))] * 2

    def neighbours(self):
        me, size = self.me, self.size
        around = (lax.rem(me + 4, size), lax.rem(me + size - 4, size), me ^ 1, me ^ 2)
        return [{"dp": partner} for partner in around]

    def back(self, device, k):
        return lax.rem(device + self.size - 4 * k, self.size)

    def send(self, source, place, slot, partner):
        copy = pltpu.make_async_remote_copy(
            src_ref=source, dst_ref=self.out.at[place],
            send_sem=self.send_sem.at[slot], recv_sem=self.recv_sem.at[slot],
            device_id={"dp": partner}, device_id_type=MESH,
        )
        copy.start()
        self.sent.append(copy)

    def landed(self, place, slot):
        pltpu.make_async_remote_copy(
            src_ref=self.out.at[place], dst_ref=self.out.at[place],
            send_sem=self.send_sem.at[slot], recv_sem=self.recv_sem.at[slot],
            device_id={"dp": self.me ^ 1}, device_id_type=MESH,
        ).wait_recv()

    def step(self):
        k, self.k = self.k, self.k + 1
        ring, me = self.ring, self.me
        if k == 0:
            self.keep = pltpu.make_async_copy(self.shard, self.out.at[me], self.own_sem)
            self.keep.start()
        if k < ring:
            place = self.back(me, k)
            if k:
                self.landed(place, k - 1)
            source = self.out.at[place] if k else self.shard
            if k < ring - 1:
                self.send(source, place, k, lax.rem(me + 4, self.size))
            self.send(source, place, ring + k, me ^ 2)
            self.send(source, place, 2 * ring + k, me ^ 1)
        if 0 < k <= ring:
            place = self.back(me ^ 2, k - 1)
            self.landed(place, ring + k - 1)
            self.send(self.out.at[place], place, 3 * ring + k - 1, me ^ 1)

    def finish(self):
        while self.k <= self.ring:
            self.step()
        for k in range(self.ring):
            self.landed(self.back(self.me ^ 1, k), 2 * self.ring + k)
            self.landed(self.back(self.me ^ 3, k), 3 * self.ring + k)
        self.keep.wait()
        for copy in self.sent:
            copy.wait_send()


class Pieces:
    def __init__(self, rows, clips, count, spatial):
        self.number = rows if spatial else 2
        self.rows, self.clips = rows // self.number, clips
        self.count = count // self.number

    def at(self, i):
        return pl.ds(i * self.count, self.count)

    def times(self, value, mods, span, i, one=0.0):
        if self.rows % self.clips == 0:
            rows = one + clip_rows(mods, self.clips, span)
            return (spread(value, self.rows, self.clips) * rows).reshape(value.shape)
        return value * (one + self.row(mods, span, i))

    def plus(self, value, mods, span, i):
        if self.rows % self.clips == 0:
            rows = clip_rows(mods, self.clips, span)
            return (spread(value, self.rows, self.clips) + rows).reshape(value.shape)
        return value + self.row(mods, span, i)

    def row(self, mods, span, i):
        at = 6 * (i * self.rows % self.clips) + span
        return mods[at : at + 1, :]

    def swap(self, source, target, sems, i, first):
        return Swap(source.at[self.at(i)], target.at[self.at(i)], sems, first + i).copy


def frame_sums(value, rows, clips):
    frames = rows // clips
    view = (value * value).reshape(frames, value.shape[0] // frames, value.shape[1])
    sums = jnp.sum(jnp.sum(view, axis=1), axis=-1, keepdims=True)
    return jnp.broadcast_to(sums, (frames, 128))


def sublayer_end(pieces, stream, mods, span, keep, part_in, swaps, outs, regroup=None):
    stream_out, stream_low, branch_out, squares, rows, clips = outs
    for i, swap_i in enumerate(swaps):
        at = pieces.at(i)
        swap_i.wait_recv()
        branch = keep[at, :] + part_in[at, :].astype(f32)
        branch_out[at, :] = branch
        gated = pieces.times(branch, mods, span, i)
        keep[at, :] = gated
        total = stream[at, :].astype(f32) + gated
        stream_out[at, :] = total
        stream_low[at, :] = total.astype(bf16)
        if regroup:
            size, some = regroup.size, total.shape[0] // regroup.size
            for d in range(size):
                regroup.source[d, i * some : (i + 1) * some, :] = total[
                    d * some : (d + 1) * some
                ].astype(bf16)
    if regroup:
        regroup.start()
    squares[0] = frame_sums(stream_out[...], rows, clips)
    squares[1] = frame_sums(keep[...], rows, clips)


def attention_kernel(rows, clips, spatial, given, ring, *refs):
    stream, mods, *refs = refs
    if given:
        hidden0, hidden1, *refs = refs
    weights, *refs = refs
    if ring:
        shard, *refs = refs
    stream_out, stream_low, branch_out, squares, qkv0, qkv1, att0, att1, *refs = refs
    if not given:
        hidden0, hidden1, *refs = refs
    if ring:
        gathered, *refs = refs
    w, w_sem, part_out, part_in, keep, x_sems, *refs = refs
    pieces = Pieces(rows, clips, stream.shape[0], spatial)
    inner, count = att0.shape[1], stream.shape[0]
    gather = Gather(ring, shard, gathered, refs) if ring else None
    step = gather.step if ring else (lambda: None)
    greeted = gather.neighbours() if ring else []
    greet([{"tensor": 1 - lax.axis_index("tensor")}] + greeted)
    load = pltpu.make_async_copy(weights, w, w_sem)
    load.start()
    step()
    arrivals = []
    for i in range(pieces.number if not given else 0):
        normed = norm_rows(stream[pieces.at(i), :].astype(f32))
        value = pieces.plus(pieces.times(normed, mods, 1, i, 1.0), mods, 0, i)
        hidden0[pieces.at(i), :] = value.astype(bf16)
        arrivals.append(pieces.swap(hidden0, hidden1, x_sems, i, 0))
    load.wait()
    w_qkv = w[:, : 3 * inner]
    qkv0[...] = dot(hidden0[...], w_qkv).astype(bf16)
    step()

    def heads(group):
        residue = 0 if spatial else count // FRAMES

        def take(refs, cols):
            values = [refs[i][pl.ds(r, n), cols] for i, r, n in group]
            return values[0] if len(values) == 1 else jnp.concatenate(values, axis=0)

        for start in range(0, inner, HEAD_DIM):
            q, k, v = (
                take((qkv0, qkv1), slice(p * inner + start, p * inner + start + HEAD_DIM)) for p in range(3)
            )
            value = dot(softmax_scores(q, k, residue).astype(bf16), v).astype(bf16)
            at = 0
            for i, r, n in group:
                (att0, att1)[i][pl.ds(r, n), start : start + HEAD_DIM] = value[at : at + n]
                at += n

    swaps = []
    w_proj = w[:, 3 * inner :]
    if spatial:
        tokens = pieces.count
        for r in range(pieces.number):
            if not given:
                arrivals[r].wait_recv()
            at = pieces.at(r)
            qkv1[at, :] = dot(hidden1[at, :], w_qkv).astype(bf16)
            heads([(0, r * tokens, tokens), (1, r * tokens, tokens)])
            part_out[at, :] = dot_nt(att1[at, :], w_proj).astype(bf16)
            swaps.append(pieces.swap(part_out, part_in, x_sems, r, pieces.number))
            step()
    else:
        heads([(0, 0, count)])
        for arrival in arrivals:
            arrival.wait_recv()
        qkv1[...] = dot(hidden1[...], w_qkv).astype(bf16)
        heads([(1, 0, count)])
        for i in range(pieces.number):
            at = pieces.at(i)
            part_out[at, :] = dot_nt(att1[at, :], w_proj).astype(bf16)
            swaps.append(pieces.swap(part_out, part_in, x_sems, i, pieces.number))
    keep[...] = dot_nt(att0[...], w_proj)
    step()
    sublayer_end(
        pieces, stream, mods, 2, keep, part_in, swaps,
        (stream_out, stream_low, branch_out, squares, rows, clips),
    )
    if ring:
        gather.finish()
    for copy in arrivals + swaps:
        copy.wait_send()


def mlp_kernel(rows, clips, spatial, *refs):
    stream, mods, weights, *refs = refs
    if not spatial:
        low, *refs = refs
    stream_out, stream_low, branch_out, squares, hidden0, hidden1, pre0, pre1, act0, act1, *refs = refs
    landed, *refs = refs
    w, w_sem, part_out, part_in, keep, x_sems, *refs = refs
    if spatial:
        low, *refs = refs
    regroup = Exchange(low, landed, refs)
    greeted = [{"tensor": 1 - lax.axis_index("tensor")}] + regroup.others()
    pieces = Pieces(rows, clips, stream.shape[0], spatial)
    inner = act0.shape[1]
    greet(greeted)
    load = pltpu.make_async_copy(weights, w, w_sem)
    load.start()
    arrivals, swaps = [], []
    for i in range(pieces.number):
        normed = norm_rows(stream[pieces.at(i), :].astype(f32))
        value = pieces.plus(pieces.times(normed, mods, 4, i, 1.0), mods, 3, i)
        hidden0[pieces.at(i), :] = value.astype(bf16)
        arrivals.append(pieces.swap(hidden0, hidden1, x_sems, i, 0))
    if not spatial:
        regroup.start()
    load.wait()
    block = 768 if inner % 768 == 0 else inner

    def through(hidden, pre, act, at):
        for start in range(0, inner, block):
            cols = slice(start, start + block)
            value = dot(hidden[at, :], w[:, cols])
            pre[at, cols] = value
            act[at, cols] = gelu_tanh(value).astype(bf16)

    w_down = w[:, inner:]
    everything = pl.ds(0, stream.shape[0])
    through(hidden0, pre0, act0, everything)
    for i, arrival in enumerate(arrivals):
        at = pieces.at(i)
        arrival.wait_recv()
        through(hidden1, pre1, act1, at)
        part_out[at, :] = dot_nt(act1[at, :], w_down).astype(bf16)
        swaps.append(pieces.swap(part_out, part_in, x_sems, i, pieces.number))
    keep[...] = dot_nt(act0[...], w_down)
    sublayer_end(
        pieces, stream, mods, 5, keep, part_in, swaps,
        (stream_out, stream_low, branch_out, squares, rows, clips), regroup if spatial else None,
    )
    regroup.finish()
    for copy in arrivals + swaps:
        copy.wait_send()


def forward_call(layer, attends, stream, mod, weights, hidden=None, shard=None, ride=None):
    rows, clips, count = layer.rows, layer.clips, layer.rows * layer.tokens
    width = weights.shape[0]
    inner = weights.shape[1] // (4 if attends else 2)
    number = rows if layer.spatial else 2
    ring = lax.axis_size("dp") // 4 if shard is not None else 0
    vmem, anywhere = pl.BlockSpec(memory_space=pltpu.VMEM), pl.BlockSpec(memory_space=pl.ANY)
    args, specs = [stream, mod.reshape(-1, width)], [vmem, vmem]
    if hidden:
        args, specs = args + list(hidden), specs + [vmem, vmem]
    args, specs = args + [weights], specs + [anywhere]
    shape = jax.ShapeDtypeStruct
    outs = [shape((count, width), kind) for kind in (f32, bf16, f32)]
    outs.append(shape((2, rows // clips, 128), f32))
    if attends:
        outs += [shape((count, 3 * inner), bf16)] * 2 + [shape((count, inner), bf16)] * 2
        if not hidden:
            outs += [shape((count, width), bf16)] * 2
    else:
        outs += [shape((count, width), bf16)] * 2
        outs += [shape((count, inner), f32)] * 2 + [shape((count, inner), bf16)] * 2
    out_specs = [vmem] * len(outs)
    scratch = [pltpu.VMEM(weights.shape, bf16), pltpu.SemaphoreType.DMA]
    scratch += [pltpu.VMEM((count, width), bf16)] * 2 + [pltpu.VMEM((count, width), f32)]
    scratch += [pltpu.SemaphoreType.DMA((2, 2 * number))]
    if ring:
        args, specs = args + [shard], specs + [anywhere]
        outs.append(shape((4 * ring,) + shard.shape, bf16))
        out_specs.append(anywhere)
        scratch += Gather.scratch(ring)
    size = lax.axis_size("dp")
    blocks = shape((size, count // size, width), bf16)
    if ride is not None:
        args, specs = args + [ride], specs + [vmem]
    if not attends:
        outs.append(blocks)
        out_specs.append(vmem)
        scratch += [pltpu.VMEM(blocks.shape, bf16)] if layer.spatial else []
        scratch += Exchange.scratch(size)
    if attends:
        kernel = functools.partial(attention_kernel, rows, clips, layer.spatial, bool(hidden), ring)
    else:
        kernel = functools.partial(mlp_kernel, rows, clips, layer.spatial)
    return pl.pallas_call(
        kernel,
        in_specs=specs,
        out_specs=out_specs,
        out_shape=outs,
        scratch_shapes=scratch,
        cost_estimate=pl.CostEstimate(flops=1 << 35, bytes_accessed=1 << 25, transcendentals=0),
        compiler_params=pltpu.CompilerParams(
            collective_id=6 + 2 * attends + layer.spatial, has_side_effects=True, vmem_limit_bytes=60 << 20
        ),
    )(*args)


def gelu_slope(value):
    root, cubic = 0.7978845608028654, 0.044715
    square = value * value
    bend = jnp.tanh(root * (value + cubic * square * value))
    return 0.5 * (1.0 + bend) + 0.5 * value * (1.0 - bend * bend) * root * (1.0 + 3.0 * cubic * square)


def mlp_back_kernel(rows, clips, extra, packed, rides, *refs):
    grad, branch, stream, mods, hidden0, hidden1, pre0, pre1, act0, act1, weights, *refs = refs
    others, refs = refs[:extra], refs[extra:]
    if rides:
        ride, *refs = refs
    grad_out, dmod_out, *refs = refs
    gw_outs, refs = refs[: 2 - packed], refs[2 - packed :]
    other_outs, refs = refs[:extra], refs[extra:]
    if rides:
        landed, *refs = refs
    w, w_sem, db0, db1, part_out, part_in, keep, dpre0, dpre1, gw, gw_sem, x_sems, *refs = refs
    inner = act0.shape[1]
    jobs = [
        Scatter(others[i], other_outs[i], refs[7 * i : 7 * i + 7], lambda j: False) for i in range(extra)
    ]
    greeted = [{"tensor": 1 - lax.axis_index("tensor")}]
    if rides:
        exchange = Exchange(ride, landed, refs[7 * extra :])
        greeted += exchange.others()
    elif extra:
        greeted += jobs[0].neighbours()
    greet(greeted)
    load = pltpu.make_async_copy(weights, w, w_sem)
    load.start()
    db0[...] = (
        (spread(grad[...].astype(f32), rows, clips) * clip_rows(mods, clips, 5)).reshape(grad.shape).astype(bf16)
    )
    first = Swap(db0, db1, x_sems, 0)
    if rides:
        exchange.start()
    pipeline = Pipeline()
    pipeline.add(jobs)
    tick = pipeline.tick
    dgate = clip_sums(grad[...].astype(f32) * branch[...], rows, clips)
    load.wait()
    block = 768 if inner % 768 == 0 else inner

    def through(db, pre, dpre):
        for start in range(0, inner, block):
            cols = slice(start, start + block)
            dact = dot(db[...], w[:, inner + start : inner + start + block])
            dpre[:, cols] = (dact * gelu_slope(pre[:, cols])).astype(bf16)
        tick()

    tick()
    through(db0, pre0, dpre0)
    first.copy.wait_recv()
    through(db1, pre1, dpre1)
    part_out[...] = dot_nt(dpre1[...], w[:, :inner]).astype(bf16)
    second = Swap(part_out, part_in, x_sems, 1)
    tick()
    keep[...] = dot_nt(dpre0[...], w[:, :inner])
    tick()
    both = lambda a, b, cols: jnp.concatenate([a[:, cols], b[:, cols]], axis=0)
    whole = slice(0, grad.shape[1])
    stored = []
    for p, (left, right) in enumerate((((hidden0, hidden1), (dpre0, dpre1)), ((db0, db1), (act0, act1)))):
        tall = both(*left, whole)
        for start in range(0, inner, block):
            slot = len(stored) % 2
            if len(stored) > 1:
                stored[-2].wait()
            gw[slot] = dot_tn(tall, both(*right, slice(start, start + block))).astype(bf16)
            at = start + inner if packed and p else start
            out = gw_outs[0 if packed else p].at[:, pl.ds(at, block)]
            copy = pltpu.make_async_copy(gw.at[slot], out, gw_sem.at[slot])
            copy.start()
            stored.append(copy)
            if len(stored) % 2:
                tick()
    second.copy.wait_recv()
    result, dshift, dscale = norm_back_rows(
        grad[...], keep[...] + part_in[...].astype(f32), stream[...], clip_rows(mods, clips, 4), rows, clips
    )
    grad_out[...] = result
    for k, value in enumerate((dshift, dscale, dgate)):
        dmod_out[k * clips : (k + 1) * clips] = value
    pipeline.finish()
    if rides:
        exchange.finish()
    for copy in stored[-2:]:
        copy.wait()
    for exchange in (first, second):
        exchange.copy.wait_send()


def mlp_back_call(layer, grad, mod, stored, packed, others=(), ride=None):
    stream, branch, hidden, pre, active, weights = stored
    rows, clips, count = layer.rows, layer.clips, layer.rows * layer.tokens
    width, inner, ring = weights.shape[0], active[0].shape[1], lax.axis_size("dp") // 4
    share = width // (4 * ring)
    others = [g.reshape(ring, 2, 2, share, g.shape[1]) for g in others]
    vmem, anywhere = pl.BlockSpec(memory_space=pltpu.VMEM), pl.BlockSpec(memory_space=pl.ANY)
    args = [layer.flat(grad), layer.flat(branch), layer.flat(stream), mod.reshape(-1, width)]
    args += [*hidden, *pre, *active]
    specs = [vmem] * len(args) + [anywhere] * (1 + len(others))
    args += [weights, *others]
    shape = jax.ShapeDtypeStruct
    gw = [shape((width, 2 * inner), bf16)] if packed else [shape((width, inner), bf16)] * 2
    outs = [shape((count, width), f32), shape((3 * clips, width), f32)] + gw
    outs += [shape((share, g.shape[-1]), f32) for g in others]
    rides = ride is not None
    if rides:
        args, specs = args + [ride], specs + [vmem]
        outs.append(shape(ride.shape, bf16))
    block = 768 if inner % 768 == 0 else inner
    scratch = [pltpu.VMEM(weights.shape, bf16), pltpu.SemaphoreType.DMA]
    scratch += [pltpu.VMEM((count, width), bf16)] * 4 + [pltpu.VMEM((count, width), f32)]
    scratch += [pltpu.VMEM((count, inner), bf16)] * 2
    scratch += [pltpu.VMEM((2, width, block), bf16), pltpu.SemaphoreType.DMA((2,))]
    scratch += [pltpu.SemaphoreType.DMA((2, 2))]
    for g in others:
        scratch += Scatter.scratch(ring, share, g.shape[-1], False)
    if rides:
        scratch += Exchange.scratch(4 * ring)
    return pl.pallas_call(
        functools.partial(mlp_back_kernel, rows, clips, len(others), packed, rides),
        in_specs=specs,
        out_specs=[vmem, vmem] + [anywhere] * len(gw) + [vmem] * (len(others) + rides),
        out_shape=outs,
        scratch_shapes=scratch,
        cost_estimate=pl.CostEstimate(flops=1 << 35, bytes_accessed=1 << 25, transcendentals=0),
        compiler_params=pltpu.CompilerParams(
            collective_id=4 + layer.spatial, has_side_effects=True, vmem_limit_bytes=62 << 20
        ),
    )(*args)


def tail_kernel(count, pairs, *refs):
    grads, small = refs[:count], refs[count]
    outs, small_out = refs[count + 1 : 2 * count + 1], refs[2 * count + 1]
    scratch = refs[2 * count + 2 :]
    jobs = [
        Scatter(grads[i], outs[i], scratch[7 * i : 7 * i + 7], lambda j: j % 6 == 5)
        for i in range(count)
    ]
    total = SmallSum(pairs, small, small_out, scratch[7 * count :])
    greet(total.partners + [{"dp": jobs[0].after}, {"dp": jobs[0].before}])
    pipeline = Pipeline()
    total.tick()
    pipeline.add(jobs)
    for _ in range(len(pairs)):
        pipeline.tick()
        total.tick()
    pipeline.finish()
    total.finish()


def tail(grads, small):
    ring = lax.axis_size("dp") // 4
    grads = [grad.reshape(ring, 2, 2, -1, grad.shape[1]) for grad in grads]
    pairs = exchange_pairs()
    anywhere, vmem = pl.BlockSpec(memory_space=pl.ANY), pl.BlockSpec(memory_space=pltpu.VMEM)
    scratch = []
    for grad in grads:
        scratch += Scatter.scratch(ring, *grad.shape[3:])
    return pl.pallas_call(
        functools.partial(tail_kernel, len(grads), pairs),
        in_specs=[anywhere] * len(grads) + [vmem],
        out_specs=[vmem] * (len(grads) + 1),
        out_shape=[jax.ShapeDtypeStruct(grad.shape[3:], f32) for grad in grads]
        + [jax.ShapeDtypeStruct(small.shape, f32)],
        scratch_shapes=scratch + SmallSum.scratch(len(pairs), small.shape),
        compiler_params=pltpu.CompilerParams(
            collective_id=0, has_side_effects=True, vmem_limit_bytes=56 << 20
        ),
    )(*grads, small)


class Layer:
    def __init__(self, rows, tokens, clips, spatial, first_row):
        self.rows, self.tokens, self.clips, self.spatial = rows, tokens, clips, spatial
        self.first_row = first_row

    def by_row(self, table):
        if self.rows % self.clips == 0:
            width = table.shape[-1]
            spread = jnp.broadcast_to(table[None], (self.rows // self.clips, self.clips, width))
            return spread.reshape(self.rows, 1, width)
        start = lax.rem(self.first_row, self.clips)
        return lax.dynamic_slice_in_dim(table, start, self.rows, 0)[:, None, :]

    def by_clip(self, sums):
        width = sums.shape[-1]
        if self.rows % self.clips == 0:
            return jnp.sum(sums.reshape(self.rows // self.clips, self.clips, width), axis=0)
        start = lax.rem(self.first_row, self.clips)
        empty = jnp.zeros((self.clips, width), f32)
        return lax.dynamic_update_slice_in_dim(empty, sums, start, 0)

    def by_frame(self, entries):
        per_row = jnp.sum(entries * entries, axis=(1, 2))
        frames = max(self.rows // self.clips, 1)
        sums = jnp.sum(per_row.reshape(frames, -1), axis=1)
        if frames == FRAMES:
            return sums
        start = self.first_row // self.clips
        return lax.dynamic_update_slice_in_dim(jnp.zeros((FRAMES,), f32), sums, start, 0)

    def modulated(self, stream, mod, offset):
        normed = layer_norm(stream)[0]
        scale = 1.0 + self.by_row(mod[:, offset + 1])
        return (normed * scale + self.by_row(mod[:, offset])).astype(bf16)

    def flat(self, value):
        return value.reshape(self.rows * self.tokens, value.shape[-1])

    def full(self, value):
        return value.reshape(self.rows, self.tokens, value.shape[-1])

    def attend(self, kernel, operands, widths):
        if self.spatial:
            views = [[self.full(value) for value in group] for group in operands]
            return [self.flat(v) for v in attend_call(kernel, 0, views, widths)]
        count = self.rows * self.tokens
        out = []
        for i in range(len(operands[0])):
            views = [[group[i][None]] for group in operands]
            out.append(attend_call(kernel, count // FRAMES, views, widths)[0][0])
        return out

    def attention(self, stream, mod, weights, pump, hidden=None):
        inner = weights.shape[1] // 4
        if hidden is None:
            hidden = gather_tokens(self.modulated(stream, mod, 0))
        hidden = [self.flat(h) for h in hidden]
        w_qkv, w_proj = weights[:, : 3 * inner], weights[:, 3 * inner :]
        qkv = [dot(h, w_qkv).astype(bf16) for h in hidden]
        attended = self.attend(attend_kernel, [qkv], inner)
        attended[-1] = pump(attended[-1])
        partial = [self.full(dot_nt(a, w_proj)) for a in attended]
        branch = scatter_tokens(partial)
        branch = pump(branch)
        gated = self.by_row(mod[:, 2]) * branch
        return stream + gated, gated, (stream, branch, hidden, qkv, attended, w_qkv, w_proj)

    def mlp(self, stream, mod, weights, pump):
        inner = weights.shape[1] // 2
        hidden = [self.flat(h) for h in gather_tokens(self.modulated(stream, mod, 3))]
        hidden[-1] = pump(hidden[-1])
        w_up, w_down = weights[:, :inner], weights[:, inner:]
        pre = [dot(h, w_up) for h in hidden]
        active = [gelu_tanh(p).astype(bf16) for p in pre]
        branch = scatter_tokens([self.full(dot_nt(a, w_down)) for a in active])
        branch = pump(branch)
        gated = self.by_row(mod[:, 5]) * branch
        return stream + gated, gated, (stream, branch, hidden, pre, active, w_up, w_down)

    def branch_back(self, grad, mod, offset, branch):
        grad_branch = (grad * self.by_row(mod[:, offset + 2])).astype(bf16)
        grad_gate = self.by_clip(jnp.sum(grad * branch, axis=1))
        return [self.flat(g) for g in gather_tokens(grad_branch)], grad_gate

    def norm_back(self, grad, grad_hidden, stream, mod, offset):
        normed, inverse = layer_norm(stream)
        grad_normed = grad_hidden * (1.0 + self.by_row(mod[:, offset + 1]))
        centered = grad_normed - jnp.mean(grad_normed, axis=-1, keepdims=True)
        grad_in = inverse * (
            centered - normed * jnp.mean(grad_normed * normed, axis=-1, keepdims=True)
        )
        shift = self.by_clip(jnp.sum(grad_hidden, axis=1))
        scale = self.by_clip(jnp.sum(grad_hidden * normed, axis=1))
        return grad + grad_in, shift, scale

    def mlp_back(self, grad, mod, stored, split, pump):
        stream, branch, hidden, pre, active, w_up, w_down = stored
        grad_branch, gate = self.branch_back(grad, mod, 3, branch)
        grad_branch[-1] = pump(grad_branch[-1])
        grad_pre = [
            jax.vjp(gelu_tanh, p)[1](dot(g, w_down))[0].astype(bf16)
            for p, g in zip(pre, grad_branch)
        ]
        grad_pre[-1] = pump(grad_pre[-1])
        grad_hidden = scatter_tokens([self.full(dot_nt(g, w_up)) for g in grad_pre])
        grad_w = weight_grad((hidden, grad_pre), (grad_branch, active), split)
        grad_hidden, *grad_w = tie(grad_hidden, *grad_w)
        grad_hidden = pump(grad_hidden)
        grad, shift, scale = self.norm_back(grad, grad_hidden, stream, mod, 3)
        return grad, jnp.stack([shift, scale, gate], axis=1), grad_w

    def attention_back(self, grad, mod, stored, split, pump):
        stream, branch, hidden, qkv, attended, w_qkv, w_proj = stored
        grad_branch, gate = self.branch_back(grad, mod, 0, branch)
        grad_branch[-1] = pump(grad_branch[-1])
        grad_att = [dot(g, w_proj).astype(bf16) for g in grad_branch]
        grad_qkv = self.attend(attend_back_kernel, [qkv, grad_att], w_qkv.shape[1])
        grad_qkv[-1] = pump(grad_qkv[-1])
        grad_hidden = scatter_tokens([self.full(dot_nt(g, w_qkv)) for g in grad_qkv])
        grad_w = weight_grad((hidden, grad_qkv), (grad_branch, attended), split)
        grad_hidden, *grad_w = tie(grad_hidden, *grad_w)
        grad_hidden = pump(grad_hidden)
        grad, shift, scale = self.norm_back(grad, grad_hidden, stream, mod, 0)
        return grad, jnp.stack([shift, scale, gate], axis=1), grad_w


def to_places(stream, kind=f32):
    return lax.all_to_all(
        stream.astype(bf16), "dp", split_axis=1, concat_axis=0, tiled=True
    ).astype(kind)


def to_frames(stream):
    return lax.all_to_all(stream.astype(bf16), "dp", split_axis=0, concat_axis=1, tiled=True)


def pack(first, second):
    return jnp.concatenate([first.reshape(first.shape[0], -1), second.T], axis=1)


def gather_weights(first, second):
    return lax.all_gather(pack(first, second), "dp", axis=0, tiled=True)


def norm_rows(value):
    centered = value - jnp.mean(value, axis=-1, keepdims=True)
    return centered * lax.rsqrt(jnp.mean(centered * centered, axis=-1, keepdims=True) + epsilon)


def head_kernel(
    ring, clips, pairs, shard, small, video, out, small_out, hidden, other,
    slots, landed_small, own_sem, send_sem, recv_sem, pair_send, pair_recv, x_send, x_recv,
):
    size, me = 4 * ring, lax.axis_index("dp")
    tensor = lax.axis_index("tensor")
    after, before = lax.rem(me + 4, size), lax.rem(me + size - 4, size)
    beside, core = me ^ 2, me ^ 1
    exchange = lax.axis_size("tensor") == 2
    barrier = pltpu.get_barrier_semaphore()
    partners = [{"dp": me ^ stride} for stride in pairs]
    greeted = partners + [{"dp": after}, {"dp": before}]
    if exchange:
        greeted.append({"tensor": 1 - tensor})
    for partner in greeted:
        pl.semaphore_signal(barrier, inc=1, device_id=partner, device_id_type=MESH)
    pl.semaphore_wait(barrier, len(greeted))
    keep = pltpu.make_async_copy(shard, out.at[me], own_sem)
    keep.start()
    sent = []

    def send(source, target, out_sem, in_sem, partner):
        copy = pltpu.make_async_remote_copy(
            src_ref=source, dst_ref=target, send_sem=out_sem, recv_sem=in_sem,
            device_id=partner, device_id_type=MESH,
        )
        copy.start()
        sent.append(copy)
        return copy

    def pass_on(source, place, slot, partner):
        send(source, out.at[place], send_sem.at[slot], recv_sem.at[slot], {"dp": partner})

    def landed(place, slot):
        pltpu.make_async_remote_copy(
            src_ref=out.at[place], dst_ref=out.at[place],
            send_sem=send_sem.at[slot], recv_sem=recv_sem.at[slot],
            device_id={"dp": core}, device_id_type=MESH,
        ).wait_recv()

    flying = []

    def pair_step(k):
        if k == 0:
            slots[0] = small[...]
        else:
            flying[k - 1].wait_recv()
            slots[k] = slots[k - 1] + landed_small[k - 1]
        if k < len(partners):
            flying.append(
                send(slots.at[k], landed_small.at[k], pair_send.at[k], pair_recv.at[k], partners[k])
            )

    pair_step(0)
    step = 1
    for k in range(ring):
        place = lax.rem(me + size - 4 * k, size)
        if k:
            landed(place, k - 1)
        source = shard if k == 0 else out.at[place]
        if k < ring - 1:
            pass_on(source, place, k, after)
        pass_on(source, place, ring + k, beside)
        pass_on(source, place, 2 * ring + k, core)
        if k:
            place = lax.rem((me ^ 2) + size - 4 * (k - 1), size)
            landed(place, ring + k - 1)
            pass_on(out.at[place], place, 3 * ring + k - 1, core)
        if step <= len(partners):
            pair_step(step)
            step += 1
    while step <= len(partners):
        pair_step(step)
        step += 1
    small_out[...] = slots[len(partners)]
    if exchange:
        rows = video.shape[0]
        for r in range(rows):
            clip = r % clips if rows % clips == 0 else lax.rem(me * rows + r, clips)
            shift = slots[len(partners), pl.ds(6 * clip, 1), :]
            scale = slots[len(partners), pl.ds(6 * clip + 1, 1), :]
            normed = norm_rows(video[r].astype(f32))
            hidden[r] = (normed * (1.0 + scale) + shift).astype(bf16)
        swapped = send(hidden, other, x_send, x_recv, {"tensor": 1 - tensor})
    place = lax.rem((me ^ 2) + size - 4 * (ring - 1), size)
    landed(place, 2 * ring - 1)
    pass_on(out.at[place], place, 4 * ring - 1, core)
    for k in range(ring):
        landed(lax.rem(core + size - 4 * k, size), 2 * ring + k)
        landed(lax.rem((core ^ 2) + size - 4 * k, size), 3 * ring + k)
    keep.wait()
    if exchange:
        swapped.wait_recv()
    for copy in sent:
        copy.wait_send()


def head(shard, small, video, clips):
    ring = lax.axis_size("dp") // 4
    rows, cols = shard.shape
    pairs = [1 << bit for bit in range(lax.axis_size("dp").bit_length() - 1)]
    count = len(pairs)
    vmem, anywhere = pl.BlockSpec(memory_space=pltpu.VMEM), pl.BlockSpec(memory_space=pl.ANY)
    full, total, mine, other = pl.pallas_call(
        functools.partial(head_kernel, ring, clips, pairs),
        in_specs=[anywhere, vmem, vmem],
        out_specs=[anywhere, vmem, vmem, vmem],
        out_shape=[
            jax.ShapeDtypeStruct((4 * ring, rows, cols), bf16),
            jax.ShapeDtypeStruct(small.shape, f32),
            jax.ShapeDtypeStruct(video.shape, bf16),
            jax.ShapeDtypeStruct(video.shape, bf16),
        ],
        scratch_shapes=[
            pltpu.VMEM((count + 1,) + small.shape, f32),
            pltpu.VMEM((count,) + small.shape, f32),
            pltpu.SemaphoreType.DMA,
            pltpu.SemaphoreType.DMA((4 * ring,)),
            pltpu.SemaphoreType.DMA((4 * ring,)),
            pltpu.SemaphoreType.DMA((count,)),
            pltpu.SemaphoreType.DMA((count,)),
            pltpu.SemaphoreType.DMA,
            pltpu.SemaphoreType.DMA,
        ],
        cost_estimate=pl.CostEstimate(flops=1 << 35, bytes_accessed=8 * ring * rows * cols, transcendentals=0),
        compiler_params=pltpu.CompilerParams(
            collective_id=1, has_side_effects=True, vmem_limit_bytes=32 << 20
        ),
    )(shard, small, video)
    hidden = [mine, other] if lax.axis_size("tensor") == 2 else None
    return full.reshape(4 * ring * rows, cols), total, hidden


def assemble_kernel(ring, own, *refs):
    hops, beside, core, out, sems = refs[: ring - 1], *refs[ring - 1 :]
    size, me = 4 * ring, lax.axis_index("dp")
    copies = []

    def put(source, place):
        copy = pltpu.make_async_copy(source, out.at[place], sems.at[len(copies)])
        copy.start()
        copies.append(copy)

    for k in range(ring):
        back = lambda device: lax.rem(device + size - 4 * k, size)
        put(own if k == 0 else hops[k - 1], back(me))
        put(beside.at[k], back(me ^ 2))
        put(core.at[k], back(me ^ 1))
        put(core.at[ring + k], back(me ^ 3))
    for copy in copies:
        copy.wait()


class WeightGather:
    def __init__(self, shard):
        self.size = lax.axis_size("dp")
        self.ring = self.size // 4
        self.pieces, self.stage = [shard], 0
        self.begin()

    def begin(self):
        if self.stage < self.ring - 1:
            links = [(i, (i + 4) % self.size) for i in range(self.size)]
            self.wait = lax.ppermute(self.pieces[-1], "dp", links)
        elif self.stage == self.ring - 1:
            self.column = jnp.stack(self.pieces)
            self.wait = swap(self.column, "dp", 2, self.size)
        else:
            self.wait = swap(jnp.concatenate([self.column, self.pieces[-1]]), "dp", 1, self.size)

    def step(self, value=None):
        if self.stage > self.ring:
            return value
        if value is not None:
            value, self.wait = tie(value, self.wait)
        self.pieces.append(self.wait)
        self.stage += 1
        if self.stage <= self.ring:
            self.begin()
        return value

    def finish(self):
        while self.stage <= self.ring:
            self.step()
        rows, cols = self.pieces[0].shape
        anywhere = pl.BlockSpec(memory_space=pl.ANY)
        full = pl.pallas_call(
            functools.partial(assemble_kernel, self.ring),
            in_specs=[anywhere] * (self.ring + 2),
            out_specs=pl.BlockSpec(memory_space=pltpu.VMEM),
            out_shape=jax.ShapeDtypeStruct((self.size, rows, cols), bf16),
            scratch_shapes=[pltpu.SemaphoreType.DMA((self.size,))],
            compiler_params=pltpu.CompilerParams(vmem_limit_bytes=32 << 20),
        )(*self.pieces)
        return full.reshape(self.size * rows, cols)


def scatter_grads(grad_w):
    return lax.psum_scatter(grad_w, "dp", scatter_dimension=0, tiled=True)


def unpack(local, first, second):
    local = local.astype(f32)
    cut = local.shape[1] - second.shape[0]
    return local[:, :cut].reshape(first.shape), local[:, cut:].T


def finish_spatial(gw_mlp, gw_attn, dmod_attn, dmod_mlp):
    small = jnp.concatenate([dmod_attn.reshape(-1), dmod_mlp.reshape(-1)]).reshape(-1, 128)
    return tail([*gw_mlp, gw_attn], small)


def body(
    video_in,
    condition,
    adaln_spatial,
    qkv_spatial,
    proj_spatial,
    up_spatial,
    down_spatial,
    adaln_temporal,
    qkv_temporal,
    proj_temporal,
    up_temporal,
    down_temporal,
    grad_output,
):
    rows, tokens, width = video_in.shape
    clips = condition.shape[0]
    dp, me = lax.axis_size("dp"), lax.axis_index("dp")
    spatial = Layer(rows, tokens, clips, True, me * rows)
    temporal = Layer(rows * dp, tokens // dp, clips, False, 0)

    w_mlp_s = gather_weights(up_spatial, down_spatial)
    w_mlp_t = gather_weights(up_temporal, down_temporal)

    share = adaln_spatial.shape[0]
    cond_rows = lax.dynamic_slice_in_dim(condition, me * share, share, 1)
    silu_rows, silu_pull = jax.vjp(jax.nn.silu, cond_rows)
    silu_low = silu_rows.astype(bf16)
    flat_s = adaln_spatial.reshape(share, -1)
    flat_t = adaln_temporal.reshape(share, -1)
    mods = jnp.stack([dot(silu_low, flat_s), dot(silu_low, flat_t)]).reshape(-1, width)
    w_attn_s, mods, hidden = head(pack(qkv_spatial, proj_spatial), mods, video_in, clips)

    keep = lambda value: value
    mod_s, mod_t = mods.reshape(2, clips, 6, width)
    fused = lax.axis_size("tensor") == 2 and rows % clips == 0 and tokens % (8 * dp) == 0
    if fused:
        flat = video_in.reshape(rows * tokens, width)
        mine = [spatial.flat(h) for h in hidden]
        s1, _, b1, q1, *kept1, w_attn_t = forward_call(
            spatial, True, flat, mod_s, w_attn_s, mine, pack(qkv_temporal, proj_temporal)
        )
        w_attn_t = w_attn_t.reshape(width, -1)
        kept1 = (flat, b1, mine, kept1[:2], kept1[2:])
        s2, _, b2, q2, *kept2, placed = forward_call(spatial, False, s1, mod_s, w_mlp_s)
        kept2 = (s1, b2, kept2[:2], kept2[2:4], kept2[4:])
        placed = placed.reshape(-1, width)
        by_place = grad_output.astype(bf16).reshape(rows, dp, tokens // dp, width)
        by_place = jnp.moveaxis(by_place, 1, 0).reshape(dp, -1, width)
        s3, _, b3, q3, *kept3 = forward_call(temporal, True, placed, mod_t, w_attn_t)
        kept3 = (placed, b3, kept3[4:], kept3[:2], kept3[2:4])
        _, low4, b4, q4, *kept4, grad = forward_call(temporal, False, s3, mod_t, w_mlp_t, ride=by_place)
        grad = grad.reshape(-1, width)
        kept4 = (s3, b4, kept4[:2], kept4[2:4], kept4[4:])
        spots = []
        for layer, values in ((spatial, (q1, q2)), (temporal, (q3, q4))):
            for value in values:
                empty = jnp.zeros((2, FRAMES), f32)
                spots.append(
                    lax.dynamic_update_slice_in_dim(empty, value[:, :, 0], layer.first_row // clips, 1)
                )
        squares = jnp.concatenate([jnp.stack([v[i] for v in spots]) for i in range(2)])
    else:
        stream0 = video_in.astype(f32)
        shard, mods = tie(pack(qkv_temporal, proj_temporal), mods)
        mod_s, mod_t = mods.reshape(2, clips, 6, width)
        later = WeightGather(shard)
        s1, g1, kept1 = spatial.attention(stream0, mod_s, w_attn_s, later.step, hidden)
        s2, g2, kept2 = spatial.mlp(s1, mod_s, w_mlp_s, later.step)
        placed = later.step(to_places(s2))
        w_attn_t = later.finish()
        placed, grad_output = tie(placed, grad_output)
        grad = to_places(grad_output)
        s3, g3, kept3 = temporal.attention(placed, mod_t, w_attn_t, keep)
        s4, g4, kept4 = temporal.mlp(s3, mod_t, w_mlp_t, keep)
        video_out = to_frames(s4)
        squares = jnp.stack(
            [spatial.by_frame(v) for v in (s1, s2)]
            + [temporal.by_frame(v) for v in (s3, s4)]
            + [spatial.by_frame(v) for v in (g1, g2)]
            + [temporal.by_frame(v) for v in (g3, g4)]
        )
    by_span = lambda dmod: jnp.moveaxis(dmod.reshape(3, clips, width), 0, 1)
    if fused:
        grad, dmod4, gw4, by_frame = mlp_back_call(
            temporal, grad, mod_t, (*kept4[:5], w_mlp_t), True, ride=low4.reshape(dp, -1, width)
        )
        framed = lambda blocks: jnp.moveaxis(blocks.reshape(dp, rows, -1, width), 0, 1)
        video_out = framed(by_frame).reshape(video_in.shape)
        own4 = scatter_grads(gw4)
        dmod3, gw3, by_frame = attention_back_call(temporal, grad, mod_t, (*kept3[:5], w_attn_t))
        grad = framed(by_frame).reshape(-1, width)
    else:
        grad, dmod4, (gw4,) = temporal.mlp_back(grad, mod_t, kept4, False, keep)
        own4 = scatter_grads(gw4)
        grad, dmod3, (gw3,) = temporal.attention_back(grad, mod_t, kept3, False, keep)
        own3 = scatter_grads(gw3)
    if fused:
        grad, dmod2, up, down, own3 = mlp_back_call(
            spatial, grad, mod_s, (*kept2[:5], w_mlp_s), False, (gw3,)
        )
        line = jnp.pad(squares.reshape(1, -1), ((0, 0), (0, width - squares.size)))
        small = jnp.concatenate([dmod2, dmod3, dmod4, line], axis=0)
        grad, grad_up_s, down_s, *own1, late, early = attention_back_call(
            spatial, grad, mod_s, (*kept1[:5], w_attn_s), (up, down), small
        )
        grad = spatial.full(grad)
        own1 = jnp.concatenate(own1, axis=1)
        dmod1 = by_span(late)
        dmod2, dmod3, dmod4 = [by_span(early[3 * clips * i : 3 * clips * (i + 1)]) for i in range(3)]
        squares = early[9 * clips, : squares.size].reshape(8, FRAMES)
    else:
        early = AllSum(
            jnp.concatenate([dmod3.reshape(-1), dmod4.reshape(-1), squares.reshape(-1)]).reshape(-1, 128)
        )
        grad = early.step(to_frames(grad).astype(f32))
        grad, dmod2, gw2 = spatial.mlp_back(grad, mod_s, kept2, True, early.step)
        grad, own4 = tie(grad, own4)
        grad, dmod1, (gw1,) = spatial.attention_back(grad, mod_s, kept1, False, early.step)
        grad_up_s, down_s, own1, late = finish_spatial(gw2, gw1, dmod1, dmod2)
        late = late.reshape(2, clips, 3, width)
        dmod1, dmod2 = late[0], late[1]
        cut = clips * 3 * width
        flat_early = early.finish().reshape(-1)
        dmod3 = flat_early[:cut].reshape(clips, 3, width)
        dmod4 = flat_early[cut : 2 * cut].reshape(clips, 3, width)
        squares = flat_early[2 * cut :].reshape(8, FRAMES)
    grad_up_t, grad_down_t = unpack(own4, up_temporal, down_temporal)
    grad_qkv_t, grad_proj_t = unpack(own3, qkv_temporal, proj_temporal)
    grad_down_s = down_s.T
    grad_qkv_s, grad_proj_s = unpack(own1, qkv_spatial, proj_spatial)
    frame_rms = jnp.sqrt(squares / (clips * PATCHES * width))
    shift_grad = jnp.stack([d[:, 0] for d in (dmod1, dmod2, dmod3, dmod4)])
    silu_wide = silu_low.astype(f32)

    def adaln_back(flat, dmod_attn, dmod_mlp, shape):
        dmod = jnp.concatenate([dmod_attn, dmod_mlp], axis=1).reshape(clips, -1)
        grad_w = jnp.sum(silu_wide[:, :, None] * dmod[:, None, :], axis=0).reshape(shape)
        back = lax.dot_general(
            dmod, flat.astype(f32), (((1,), (1,)), ((), ())), precision=highest
        )
        return grad_w, back

    adaln_t_grad, back_t = adaln_back(flat_t, dmod3, dmod4, adaln_temporal.shape)
    adaln_s_grad, back_s = adaln_back(flat_s, dmod1, dmod2, adaln_spatial.shape)
    condition_grad = silu_pull(back_s + back_t)[0]
    return (
        video_out,
        grad,
        condition_grad,
        adaln_s_grad,
        grad_qkv_s,
        grad_proj_s,
        grad_up_s,
        grad_down_s,
        adaln_t_grad,
        grad_qkv_t,
        grad_proj_t,
        grad_up_t,
        grad_down_t,
        frame_rms,
        shift_grad,
    )


def solution(mesh):
    return jax.shard_map(
        body,
        mesh=mesh,
        in_specs=(
            P("dp", "tensor", None),
            P(),
            P("dp", None, None),
            P("dp", None, "tensor"),
            P("tensor", "dp"),
            P("dp", "tensor"),
            P("tensor", "dp"),
            P("dp", None, None),
            P("dp", None, "tensor"),
            P("tensor", "dp"),
            P("dp", "tensor"),
            P("tensor", "dp"),
            P("dp", "tensor", None),
        ),
        out_specs=(
            P("dp", "tensor", None),
            P("dp", "tensor", None),
            P(None, "dp"),
            P("dp", None, None),
            P("dp", None, "tensor"),
            P("tensor", "dp"),
            P("dp", "tensor"),
            P("tensor", "dp"),
            P("dp", None, None),
            P("dp", None, "tensor"),
            P("tensor", "dp"),
            P("dp", "tensor"),
            P("tensor", "dp"),
            P(),
            P(),
        ),
        check_vma=False,
    )
```

```python
import functools

import jax
import jax.numpy as jnp
from jax import lax
from jax.experimental import pallas as pl
from jax.experimental.pallas import tpu as pltpu
from jax.sharding import PartitionSpec as P

HEAD_DIM = 72
PATCHES = 256
FRAMES = 16

highest = lax.Precision.HIGHEST
epsilon = 1e-06
bf16 = jnp.bfloat16
f32 = jnp.float32
MESH = pl.DeviceIdType.MESH


def dot(a, b):
    return jnp.dot(a, b, preferred_element_type=f32)


def dot_nt(a, b):
    return lax.dot_general(a, b, (((1,), (1,)), ((), ())), preferred_element_type=f32)


def dot_tn(a, b):
    return lax.dot_general(a, b, (((0,), (0,)), ((), ())), preferred_element_type=f32)


def layer_norm(stream):
    average = jnp.mean(stream, axis=-1, keepdims=True)
    centered = stream - average
    inverse = lax.rsqrt(jnp.mean(centered * centered, axis=-1, keepdims=True) + epsilon)
    return (centered * inverse, inverse)


def gelu_tanh(pre_act):
    return jax.nn.gelu(pre_act, approximate=True)


def swap(value, axis, stride, size):
    return lax.ppermute(value, axis, [(i, i ^ stride) for i in range(size)])


def all_sum(value, axes):
    for axis in axes:
        size = lax.axis_size(axis)
        if size & (size - 1):
            value = lax.psum(value, axis)
            continue
        stride = 1
        while stride < size:
            value = value + swap(value, axis, stride, size)
            stride *= 2
    return value


def gather_tokens(local):
    size = lax.axis_size("tensor")
    if size == 2:
        other = swap(local, "tensor", 1, 2)
        return [local, other]
    return list(lax.all_gather(local, "tensor", axis=0, tiled=False))


def scatter_tokens(parts):
    size = lax.axis_size("tensor")
    if size == 2:
        return parts[0] + swap(parts[1].astype(bf16), "tensor", 1, 2).astype(f32)
    stacked = jnp.stack([part.astype(bf16) for part in parts])
    return lax.psum_scatter(stacked, "tensor", scatter_dimension=0, tiled=False).astype(f32)


def softmax_scores(queries, keys, residue):
    scores = dot_nt(queries, keys) * HEAD_DIM ** (-0.5)
    if residue:
        row = lax.broadcasted_iota(jnp.int32, scores.shape, 0)
        col = lax.broadcasted_iota(jnp.int32, scores.shape, 1)
        scores = jnp.where(lax.rem(row, residue) == lax.rem(col, residue), scores, -1e30)
    unnormed = jnp.exp(scores - jnp.max(scores, axis=-1, keepdims=True))
    return unnormed * (1.0 / jnp.sum(unnormed, axis=-1, keepdims=True))


def joined(refs):
    blocks = [ref[0] for ref in refs]
    return blocks[0] if len(blocks) == 1 else jnp.concatenate(blocks, axis=0)


def store_rows(refs, columns, value):
    start = 0
    for ref in refs:
        ref[0, :, columns] = value[start : start + ref.shape[1]]
        start += ref.shape[1]


def attend_kernel(count, residue, *refs):
    ins, outs = refs[:count], refs[count:]
    qkv = joined(ins)
    inner = qkv.shape[1] // 3
    for start in range(0, inner, HEAD_DIM):
        q, k, v = (
            qkv[:, part * inner + start : part * inner + start + HEAD_DIM] for part in range(3)
        )
        probs = softmax_scores(q, k, residue).astype(bf16)
        store_rows(outs, slice(start, start + HEAD_DIM), dot(probs, v).astype(bf16))


def attend_back_kernel(count, residue, *refs):
    ins, grads, outs = refs[:count], refs[count : 2 * count], refs[2 * count :]
    qkv, grad_att = joined(ins), joined(grads)
    inner = grad_att.shape[1]
    for start in range(0, inner, HEAD_DIM):
        q, k, v = (
            qkv[:, part * inner + start : part * inner + start + HEAD_DIM] for part in range(3)
        )
        grad_out = grad_att[:, start : start + HEAD_DIM]
        probs = softmax_scores(q, k, residue)
        grad_probs = dot_nt(grad_out, v)
        mean = jnp.sum(probs * grad_probs, axis=-1, keepdims=True)
        grad_scaled = (probs * (grad_probs - mean) * HEAD_DIM ** (-0.5)).astype(bf16)
        results = (
            dot(grad_scaled, k),
            dot_tn(grad_scaled, q),
            dot_tn(probs.astype(bf16), grad_out),
        )
        for part, value in enumerate(results):
            left = part * inner + start
            store_rows(outs, slice(left, left + HEAD_DIM), value.astype(bf16))


def attend_call(kernel, residue, operands, widths):
    count = len(operands[0])
    rows, tokens = operands[0][0].shape[:2]
    spec = lambda width: pl.BlockSpec((1, tokens, width), lambda r: (r, 0, 0))
    flat = [value for group in operands for value in group]
    length = count * tokens
    heads = widths // HEAD_DIM
    return pl.pallas_call(
        functools.partial(kernel, count, residue),
        grid=(rows,),
        in_specs=[spec(value.shape[2]) for value in flat],
        out_specs=[spec(widths) for _ in range(count)],
        out_shape=[jax.ShapeDtypeStruct((rows, tokens, widths), bf16) for _ in range(count)],
        cost_estimate=pl.CostEstimate(
            flops=rows * heads * length * length * HEAD_DIM * 4,
            bytes_accessed=sum(v.size * 2 for v in flat),
            transcendentals=rows * heads * length * length,
        ),
        compiler_params=pltpu.CompilerParams(vmem_limit_bytes=48 << 20),
    )(*flat)


def weight_grad_kernel(count, *refs):
    ins, outs = refs[: 4 * count], refs[4 * count :]
    left = 0
    for pair in range(2):
        base = 2 * pair * count
        out = outs[pair % len(outs)]
        left = left if len(outs) == 1 else 0
        rows = jnp.concatenate([ref[...] for ref in ins[base : base + count]], axis=0)
        cols = ins[base + count : base + 2 * count]
        width = cols[0].shape[1]
        step = width if width % 1152 else 1152
        for start in range(0, width, step):
            right = jnp.concatenate([ref[:, start : start + step] for ref in cols], axis=0)
            out[:, left + start : left + start + step] = dot_tn(rows, right).astype(bf16)
        left += width


def weight_grad(first, second, split):
    count, width = len(first[0]), first[0][0].shape[1]
    block = 384 if width % 384 == 0 else width
    ins, specs = [], []
    for rows, cols in (first, second):
        ins += rows + cols
        specs += [pl.BlockSpec((r.shape[0], block), lambda i: (0, i)) for r in rows]
        specs += [pl.BlockSpec(c.shape, lambda i: (0, 0)) for c in cols]
    wide = [first[1][0].shape[1], second[1][0].shape[1]]
    total = sum(wide)
    wide = wide if split else [total]
    tokens = count * first[0][0].shape[0]
    return pl.pallas_call(
        functools.partial(weight_grad_kernel, count),
        grid=(width // block,),
        in_specs=specs,
        out_specs=[pl.BlockSpec((block, w), lambda i: (i, 0)) for w in wide],
        out_shape=[jax.ShapeDtypeStruct((width, w), bf16) for w in wide],
        cost_estimate=pl.CostEstimate(
            flops=2 * tokens * width * total,
            bytes_accessed=2 * width * total + 2 * tokens * (2 * width + total),
            transcendentals=0,
        ),
        compiler_params=pltpu.CompilerParams(vmem_limit_bytes=48 << 20),
    )(*ins)


def tie(*values):
    return lax.optimization_barrier(values)


class AllSum:
    def __init__(self, value):
        self.value = value
        self.pairs = [
            (axis, 1 << bit)
            for axis in ("tensor", "dp")
            for bit in range(lax.axis_size(axis).bit_length() - 1)
        ]
        self.begin()

    def begin(self):
        axis, stride = self.pairs[0]
        self.wait = swap(self.value, axis, stride, lax.axis_size(axis))

    def step(self, value=None):
        if not self.pairs:
            return value
        if value is not None:
            value, self.wait = tie(value, self.wait)
        self.value = self.value + self.wait
        self.pairs.pop(0)
        if self.pairs:
            self.begin()
        return value

    def finish(self):
        while self.pairs:
            self.step()
        return self.value


def exchange_pairs():
    return [
        (axis, 1 << bit)
        for axis in ("tensor", "dp")
        for bit in range(lax.axis_size(axis).bit_length() - 1)
    ]


class Scatter:
    def __init__(self, grad, out, refs, flipped):
        self.grad, self.out, self.flipped = grad, out, flipped
        self.own, self.own_sem, self.core_in, self.y_in, self.ring_in, self.send_sem, self.recv_sem = refs
        self.ring = grad.shape[0]
        self.stages = self.ring + 2
        self.chunks = self.send_sem.shape[1]
        self.width = grad.shape[-1] // self.chunks
        me, size = lax.axis_index("dp"), 4 * self.ring
        self.me, self.at, self.y, self.core = me, me // 4, lax.rem(me // 2, 2), lax.rem(me, 2)
        self.after, self.before = lax.rem(me + 4, size), lax.rem(me + size - 4, size)
        self.pending = {}
        self.load = None

    @staticmethod
    def scratch(ring, rows, cols, flips=True):
        chunks = cols // 384 if cols % 384 == 0 else 1
        return [
            pltpu.VMEM((ring, 2, rows, cols), bf16),
            pltpu.SemaphoreType.DMA,
            pltpu.VMEM((ring, 2, rows, cols), bf16),
            pltpu.VMEM((ring, rows, cols), bf16),
            pltpu.VMEM((ring - 1, 2 if flips else 1, rows, cols), bf16),
            pltpu.SemaphoreType.DMA((ring + 1, chunks)),
            pltpu.SemaphoreType.DMA((ring + 1, chunks)),
        ]

    def neighbours(self):
        return [{"dp": partner} for partner in (self.after, self.before, self.me ^ 1, self.me ^ 2)]

    def begin(self):
        self.load = pltpu.make_async_copy(self.grad.at[:, :, self.core], self.own, self.own_sem)
        self.load.start()

    def send(self, s, j, source, target, partner):
        copy = pltpu.make_async_remote_copy(
            src_ref=source, dst_ref=target, send_sem=self.send_sem.at[s, j], recv_sem=self.recv_sem.at[s, j],
            device_id={"dp": partner}, device_id_type=MESH,
        )
        copy.start()
        self.pending[s, j] = copy

    def stage(self, s, j):
        cols = pl.ds(j * self.width, self.width)
        ring, y, at = self.ring, self.y, self.at
        if s == 0:
            source = self.grad.at[:, :, 1 - self.core, :, cols]
            return self.send(s, j, source, self.core_in.at[:, :, :, cols], self.me ^ 1)
        if self.load is not None:
            self.load.wait()
            self.load = None
        self.pending[s - 1, j].wait_recv()
        flipped = self.flipped(j)
        if s == 1:
            total = self.own[:, :, :, cols].astype(f32) + self.core_in[:, :, :, cols].astype(f32)
            self.own[:, :, :, cols] = total.astype(bf16)
        if not flipped:
            if s == 1:
                return self.send(s, j, self.own.at[:, 1 - y, :, cols], self.y_in.at[:, :, cols], self.me ^ 2)
            h = s - 2
            if h == 0:
                total = self.own[:, y, :, cols].astype(f32) + self.y_in[:, :, cols].astype(f32)
                self.y_in[:, :, cols] = total.astype(bf16)
                source = self.y_in.at[lax.rem(at + ring - 1, ring), :, cols]
            else:
                total = self.y_in[lax.rem(at + ring - 1 - h, ring), :, cols].astype(f32)
                total = total + self.ring_in[h - 1, 0, :, cols].astype(f32)
                if h == ring - 1:
                    self.out[:, cols] = total
                    return None
                self.ring_in[h - 1, 0, :, cols] = total.astype(bf16)
                source = self.ring_in.at[h - 1, 0, :, cols]
            return self.send(s, j, source, self.ring_in.at[h, 0, :, cols], self.after)
        h = s - 1
        if h == 0:
            source = self.own.at[lax.rem(at + ring - 1, ring), :, :, cols]
            return self.send(s, j, source, self.ring_in.at[h, :, :, cols], self.after)
        if h < ring:
            total = self.own[lax.rem(at + ring - 1 - h, ring), :, :, cols].astype(f32)
            total = total + self.ring_in[h - 1, :, :, cols].astype(f32)
            self.ring_in[h - 1, :, :, cols] = total.astype(bf16)
            if h < ring - 1:
                source = self.ring_in.at[h - 1, :, :, cols]
                return self.send(s, j, source, self.ring_in.at[h, :, :, cols], self.after)
            source = self.ring_in.at[h - 1, 1 - y, :, cols]
            return self.send(s, j, source, self.y_in.at[0, :, cols], self.me ^ 2)
        total = self.ring_in[ring - 2, y, :, cols].astype(f32)
        self.out[:, cols] = total + self.y_in[0, :, cols].astype(f32)
        return None

    def finish(self):
        for copy in self.pending.values():
            copy.wait_send()


class Pipeline:
    def __init__(self):
        self.jobs, self.queue, self.flight = [], [], []

    def add(self, jobs):
        self.jobs = self.jobs + jobs
        self.queue += [(job, j) for job in jobs for j in range(job.chunks)]
        for job in jobs:
            job.begin()

    def tick(self):
        for entry in self.flight:
            job, j, s, age = entry
            if age >= max(2 * s - 1, 1):
                job.stage(s, j)
                entry[2] += 1
            entry[3] += 1
        self.flight = [entry for entry in self.flight if entry[2] < entry[0].stages]
        if self.queue:
            job, j = self.queue.pop(0)
            job.stage(0, j)
            self.flight.append([job, j, 1, 1])
        return bool(self.queue or self.flight)

    def finish(self):
        while self.tick():
            pass
        for job in self.jobs:
            job.finish()


class SmallSum:
    def __init__(self, pairs, value, out, refs):
        self.slots, self.landed, self.send_sem, self.recv_sem = refs
        self.value, self.out, self.copies = value, out, []
        self.partners = [{axis: lax.axis_index(axis) ^ stride} for axis, stride in pairs]
        self.k = 0

    @staticmethod
    def scratch(count, shape):
        return [
            pltpu.VMEM((count + 1,) + shape, f32),
            pltpu.VMEM((count,) + shape, f32),
            pltpu.SemaphoreType.DMA((count,)),
            pltpu.SemaphoreType.DMA((count,)),
        ]

    def tick(self):
        k, self.k = self.k, self.k + 1
        if k > len(self.partners):
            return False
        if k == 0:
            self.slots[0] = self.value[...]
        else:
            self.copies[k - 1].wait_recv()
            self.slots[k] = self.slots[k - 1] + self.landed[k - 1]
        if k == len(self.partners):
            self.out[...] = self.slots[k]
            return False
        copy = pltpu.make_async_remote_copy(
            src_ref=self.slots.at[k], dst_ref=self.landed.at[k],
            send_sem=self.send_sem.at[k], recv_sem=self.recv_sem.at[k],
            device_id=self.partners[k], device_id_type=MESH,
        )
        copy.start()
        self.copies.append(copy)
        return True

    def finish(self):
        while self.tick():
            pass
        for copy in self.copies:
            copy.wait_send()


def greet(partners):
    barrier = pltpu.get_barrier_semaphore()
    for partner in partners:
        pl.semaphore_signal(barrier, inc=1, device_id=partner, device_id_type=MESH)
    pl.semaphore_wait(barrier, len(partners))


class Swap:
    def __init__(self, source, target, sems, k):
        self.copy = pltpu.make_async_remote_copy(
            src_ref=source, dst_ref=target, send_sem=sems.at[0, k], recv_sem=sems.at[1, k],
            device_id={"tensor": 1 - lax.axis_index("tensor")}, device_id_type=MESH,
        )
        self.copy.start()


class Exchange:
    def __init__(self, source, target, sems):
        self.source, self.target = source, target
        self.send_sem, self.recv_sem, self.own_sem = sems
        self.size, self.me = source.shape[0], lax.axis_index("dp")

    @staticmethod
    def scratch(size):
        return [pltpu.SemaphoreType.DMA((size - 1,))] * 2 + [pltpu.SemaphoreType.DMA]

    def others(self):
        return [{"dp": lax.rem(self.me + k, self.size)} for k in range(1, self.size)]

    def start(self):
        self.own = pltpu.make_async_copy(
            self.source.at[self.me], self.target.at[self.me], self.own_sem
        )
        self.own.start()
        self.copies = []
        for k, partner in enumerate(self.others()):
            copy = pltpu.make_async_remote_copy(
                src_ref=self.source.at[partner["dp"]], dst_ref=self.target.at[self.me],
                send_sem=self.send_sem.at[k], recv_sem=self.recv_sem.at[k],
                device_id=partner, device_id_type=MESH,
            )
            copy.start()
            self.copies.append(copy)

    def finish(self):
        self.own.wait()
        for copy in self.copies:
            copy.wait_recv()
        for copy in self.copies:
            copy.wait_send()


def spread(value, rows, clips):
    return value.reshape(rows // clips, clips, value.shape[0] // rows, value.shape[1])


def clip_rows(mods, clips, span):
    rows = [mods[6 * c + span : 6 * c + span + 1, :] for c in range(clips)]
    return jnp.stack(rows, axis=0)[None]


def clip_sums(value, rows, clips):
    return jnp.sum(spread(value, rows, clips), axis=(0, 2))


def norm_back_rows(grad, grad_hidden, stream, scale, rows, clips):
    stream = stream.astype(f32)
    centered = stream - jnp.mean(stream, axis=-1, keepdims=True)
    inverse = lax.rsqrt(jnp.mean(centered * centered, axis=-1, keepdims=True) + epsilon)
    normed = centered * inverse
    grad_normed = (spread(grad_hidden, rows, clips) * (1.0 + scale)).reshape(grad_hidden.shape)
    flat = grad_normed - jnp.mean(grad_normed, axis=-1, keepdims=True)
    slope = jnp.mean(grad_normed * normed, axis=-1, keepdims=True)
    grad_in = grad.astype(f32) + inverse * (flat - normed * slope)
    return grad_in, clip_sums(grad_hidden, rows, clips), clip_sums(grad_hidden * normed, rows, clips)


def gradient_blocks(target, value):
    ring, rows = target.shape[0], target.shape[3]
    for k in range(4 * ring):
        target[k // 4, (k // 2) % 2, k % 2] = value[k * rows : (k + 1) * rows].astype(bf16)


def attention_back_kernel(rows, clips, spatial, extra, tailing, pairs, *refs):
    grad, branch, stream, mods, hidden0, hidden1, qkv0, qkv1, att0, att1, weights, *refs = refs
    others, refs = refs[:extra], refs[extra:]
    if tailing:
        dmod_in, grad_out, *refs = refs
    other_outs, refs = refs[:extra], refs[extra:]
    if tailing:
        own_outs, small_out, early_out, refs = refs[:4], refs[4], refs[5], refs[6:]
    else:
        dmod_out, gw_out, landed, *refs = refs
    w, w_sem, db0, db1, part_out, part_in, keep, ga0, ga1, x_sems, *refs = refs
    dqkv, refs = (refs[:3], refs[3:6]), refs[6:]
    inner = att0.shape[1]
    count = grad.shape[0]
    jobs = []
    for i in range(extra):
        jobs.append(Scatter(others[i], other_outs[i], refs[7 * i : 7 * i + 7], lambda j: j % 6 == 5))
    refs = refs[7 * extra :]
    greeted = [{"tensor": 1 - lax.axis_index("tensor")}]
    if tailing:
        small, gw, refs = refs[0], refs[1:5], refs[5:]
        own_jobs = [
            Scatter(gw[i], own_outs[i], refs[7 * i : 7 * i + 7], lambda j: False) for i in range(4)
        ]
        total = SmallSum(pairs, small, small_out, refs[28:32])
        early = SmallSum(pairs, dmod_in, early_out, refs[32:])
        greeted = total.partners + [{"dp": jobs[0].after}, {"dp": jobs[0].before}]
    else:
        low, *refs = refs
        exchange = Exchange(low, landed, refs)
        greeted += exchange.others()
    greet(greeted)
    load = pltpu.make_async_copy(weights, w, w_sem)
    load.start()
    db0[...] = (
        (spread(grad[...].astype(f32), rows, clips) * clip_rows(mods, clips, 2)).reshape(grad.shape).astype(bf16)
    )
    first = Swap(db0, db1, x_sems, 0)
    pipeline = Pipeline()
    pipeline.add(jobs)

    def tick():
        pipeline.tick()
        if tailing:
            early.tick()

    dgate = clip_sums(grad[...].astype(f32) * branch[...], rows, clips)
    load.wait()
    w_proj = w[:, 3 * inner :]
    ga0[...] = dot(db0[...], w_proj).astype(bf16)
    tick()
    tick()

    def heads(pieces):
        take = lambda refs, cols: (
            refs[pieces[0][0]][pl.ds(*pieces[0][1:]), cols]
            if len(pieces) == 1
            else jnp.concatenate([refs[i][pl.ds(r, n), cols] for i, r, n in pieces], axis=0)
        )
        residue = 0 if spatial else count // FRAMES
        for h, start in enumerate(range(0, inner, HEAD_DIM)):
            q, k, v = (
                take((qkv0, qkv1), slice(p * inner + start, p * inner + start + HEAD_DIM)) for p in range(3)
            )
            cols = slice(start, start + HEAD_DIM)
            grad_out_h = take((ga0, ga1), cols)
            probs = softmax_scores(q, k, residue)
            grad_probs = dot_nt(grad_out_h, v)
            mean = jnp.sum(probs * grad_probs, axis=-1, keepdims=True)
            scaled = (probs * (grad_probs - mean) * HEAD_DIM ** (-0.5)).astype(bf16)
            results = (dot(scaled, k), dot_tn(scaled, q), dot_tn(probs.astype(bf16), grad_out_h))
            for p, value in enumerate(results):
                at = 0
                for i, r, n in pieces:
                    dqkv[i][p][pl.ds(r, n), cols] = value[at : at + n].astype(bf16)
                    at += n
            if h % 4 == 3:
                tick()

    def grad_hidden(i):
        value = dot_nt(dqkv[i][0][...], w[:, :inner])
        value += dot_nt(dqkv[i][1][...], w[:, inner : 2 * inner])
        return value + dot_nt(dqkv[i][2][...], w[:, 2 * inner : 3 * inner])

    if not spatial:
        heads([(0, 0, count)])
    first.copy.wait_recv()
    ga1[...] = dot(db1[...], w_proj).astype(bf16)
    tick()
    if spatial:
        tokens = count // rows
        for r in range(rows):
            heads([(0, r * tokens, tokens), (1, r * tokens, tokens)])
    else:
        heads([(1, 0, count)])
    part_out[...] = grad_hidden(1).astype(bf16)
    second = Swap(part_out, part_in, x_sems, 1)
    tick()
    keep[...] = grad_hidden(0)
    tick()
    both = lambda a, b: jnp.concatenate([a[...], b[...]], axis=0)
    for p in range(4):
        left = both(hidden0, hidden1) if p < 3 else both(db0, db1)
        right = both(dqkv[0][p], dqkv[1][p]) if p < 3 else both(att0, att1)
        value = dot_tn(left, right)
        cols = slice(p * inner, (p + 1) * inner)
        if tailing:
            gradient_blocks(gw[p], value)
        else:
            gw_out[:, cols] = value.astype(bf16)
        if p % 2:
            tick()
    if tailing:
        pipeline.add(own_jobs)
    second.copy.wait_recv()
    result, dshift, dscale = norm_back_rows(
        grad[...], keep[...] + part_in[...].astype(f32), stream[...], clip_rows(mods, clips, 1), rows, clips
    )
    if tailing:
        grad_out[...] = result
    else:
        low[...] = result.reshape(low.shape).astype(bf16)
        exchange.start()
    dmod = (dshift, dscale, dgate)
    if tailing:
        for k, value in enumerate(dmod):
            small[k * clips : (k + 1) * clips] = value
        more = total.tick()
        while more:
            pipeline.tick()
            more = total.tick()
        pipeline.finish()
        total.finish()
        early.finish()
    else:
        for k, value in enumerate(dmod):
            dmod_out[k * clips : (k + 1) * clips] = value
        pipeline.finish()
        exchange.finish()
    for exchange in (first, second):
        exchange.copy.wait_send()


def attention_back_call(layer, grad, mod, stored, others=(), dmod_in=None):
    stream, branch, hidden, qkv, attended, weights = stored
    rows, clips, count = layer.rows, layer.clips, layer.rows * layer.tokens
    width, inner, ring = weights.shape[0], attended[0].shape[1], lax.axis_size("dp") // 4
    share = width // (4 * ring)
    pairs = exchange_pairs()
    others = [g.reshape(ring, 2, 2, share, g.shape[1]) for g in others]
    vmem, anywhere = pl.BlockSpec(memory_space=pltpu.VMEM), pl.BlockSpec(memory_space=pl.ANY)
    args = [layer.flat(grad), layer.flat(branch), layer.flat(stream), mod.reshape(-1, width)]
    args += [*hidden, *qkv, *attended]
    specs = [vmem] * len(args) + [anywhere] * (1 + len(others))
    args += [weights, *others]
    shape = jax.ShapeDtypeStruct
    outs = [shape((count, width), f32)] if dmod_in is not None else []
    scratch = [pltpu.VMEM(weights.shape, bf16), pltpu.SemaphoreType.DMA]
    scratch += [pltpu.VMEM((count, width), bf16)] * 4 + [pltpu.VMEM((count, width), f32)]
    scratch += [pltpu.VMEM((count, inner), bf16)] * 2 + [pltpu.SemaphoreType.DMA((2, 2))]
    scratch += [pltpu.VMEM((count, inner), bf16)] * 6
    outs += [shape((share, g.shape[-1]), f32) for g in others]
    for g in others:
        scratch += Scatter.scratch(ring, share, g.shape[-1])
    tailing = dmod_in is not None
    if tailing:
        args.append(dmod_in)
        specs.append(vmem)
        outs += [shape((share, inner), f32)] * 4
        total = (3 * clips, width)
        outs += [shape(total, f32), shape(dmod_in.shape, f32)]
        scratch.append(pltpu.VMEM(total, f32))
        scratch += [pltpu.VMEM((ring, 2, 2, share, inner), bf16)] * 4
        for _ in range(4):
            scratch += Scatter.scratch(ring, share, inner, False)
        scratch += SmallSum.scratch(len(pairs), total) + SmallSum.scratch(len(pairs), dmod_in.shape)
    else:
        blocks = (4 * ring, count // (4 * ring), width)
        outs += [shape((3 * clips, width), f32), shape((width, 4 * inner), bf16), shape(blocks, bf16)]
        scratch += [pltpu.VMEM(blocks, bf16)] + Exchange.scratch(4 * ring)
    return pl.pallas_call(
        functools.partial(attention_back_kernel, rows, clips, layer.spatial, len(others), tailing, pairs),
        in_specs=specs,
        out_specs=[vmem] * len(outs),
        out_shape=outs,
        scratch_shapes=scratch,
        cost_estimate=pl.CostEstimate(flops=1 << 35, bytes_accessed=1 << 25, transcendentals=0),
        compiler_params=pltpu.CompilerParams(
            collective_id=2 + layer.spatial, has_side_effects=True, vmem_limit_bytes=62 << 20
        ),
    )(*args)


class Gather:
    def __init__(self, ring, shard, out, refs):
        self.ring, self.shard, self.out = ring, shard, out
        self.own_sem, self.send_sem, self.recv_sem = refs
        self.me, self.size, self.sent = lax.axis_index("dp"), 4 * ring, []
        self.k = 0

    @staticmethod
    def scratch(ring):
        return [pltpu.SemaphoreType.DMA] + [pltpu.SemaphoreType.DMA((4 * ring,))] * 2

    def neighbours(self):
        me, size = self.me, self.size
        around = (lax.rem(me + 4, size), lax.rem(me + size - 4, size), me ^ 1, me ^ 2)
        return [{"dp": partner} for partner in around]

    def back(self, device, k):
        return lax.rem(device + self.size - 4 * k, self.size)

    def send(self, source, place, slot, partner):
        copy = pltpu.make_async_remote_copy(
            src_ref=source, dst_ref=self.out.at[place],
            send_sem=self.send_sem.at[slot], recv_sem=self.recv_sem.at[slot],
            device_id={"dp": partner}, device_id_type=MESH,
        )
        copy.start()
        self.sent.append(copy)

    def landed(self, place, slot):
        pltpu.make_async_remote_copy(
            src_ref=self.out.at[place], dst_ref=self.out.at[place],
            send_sem=self.send_sem.at[slot], recv_sem=self.recv_sem.at[slot],
            device_id={"dp": self.me ^ 1}, device_id_type=MESH,
        ).wait_recv()

    def step(self):
        k, self.k = self.k, self.k + 1
        ring, me = self.ring, self.me
        if k == 0:
            self.keep = pltpu.make_async_copy(self.shard, self.out.at[me], self.own_sem)
            self.keep.start()
        if k < ring:
            place = self.back(me, k)
            if k:
                self.landed(place, k - 1)
            source = self.out.at[place] if k else self.shard
            if k < ring - 1:
                self.send(source, place, k, lax.rem(me + 4, self.size))
            self.send(source, place, ring + k, me ^ 2)
            self.send(source, place, 2 * ring + k, me ^ 1)
        if 0 < k <= ring:
            place = self.back(me ^ 2, k - 1)
            self.landed(place, ring + k - 1)
            self.send(self.out.at[place], place, 3 * ring + k - 1, me ^ 1)

    def finish(self):
        while self.k <= self.ring:
            self.step()
        for k in range(self.ring):
            self.landed(self.back(self.me ^ 1, k), 2 * self.ring + k)
            self.landed(self.back(self.me ^ 3, k), 3 * self.ring + k)
        self.keep.wait()
        for copy in self.sent:
            copy.wait_send()


class Pieces:
    def __init__(self, rows, clips, count, spatial):
        self.number = rows if spatial else 2
        self.rows, self.clips = rows // self.number, clips
        self.count = count // self.number

    def at(self, i):
        return pl.ds(i * self.count, self.count)

    def times(self, value, mods, span, i, one=0.0):
        if self.rows % self.clips == 0:
            rows = one + clip_rows(mods, self.clips, span)
            return (spread(value, self.rows, self.clips) * rows).reshape(value.shape)
        return value * (one + self.row(mods, span, i))

    def plus(self, value, mods, span, i):
        if self.rows % self.clips == 0:
            rows = clip_rows(mods, self.clips, span)
            return (spread(value, self.rows, self.clips) + rows).reshape(value.shape)
        return value + self.row(mods, span, i)

    def row(self, mods, span, i):
        at = 6 * (i * self.rows % self.clips) + span
        return mods[at : at + 1, :]

    def swap(self, source, target, sems, i, first):
        return Swap(source.at[self.at(i)], target.at[self.at(i)], sems, first + i).copy


def frame_sums(value, rows, clips):
    frames = rows // clips
    view = (value * value).reshape(frames, value.shape[0] // frames, value.shape[1])
    sums = jnp.sum(jnp.sum(view, axis=1), axis=-1, keepdims=True)
    return jnp.broadcast_to(sums, (frames, 128))


def sublayer_end(pieces, stream, mods, span, keep, part_in, swaps, outs, regroup=None):
    stream_out, stream_low, branch_out, squares, rows, clips = outs
    for i, swap_i in enumerate(swaps):
        at = pieces.at(i)
        swap_i.wait_recv()
        branch = keep[at, :] + part_in[at, :].astype(f32)
        branch_out[at, :] = branch
        gated = pieces.times(branch, mods, span, i)
        keep[at, :] = gated
        total = stream[at, :].astype(f32) + gated
        stream_out[at, :] = total
        stream_low[at, :] = total.astype(bf16)
        if regroup:
            size, some = regroup.size, total.shape[0] // regroup.size
            for d in range(size):
                regroup.source[d, i * some : (i + 1) * some, :] = total[
                    d * some : (d + 1) * some
                ].astype(bf16)
    if regroup:
        regroup.start()
    squares[0] = frame_sums(stream_out[...], rows, clips)
    squares[1] = frame_sums(keep[...], rows, clips)


def attention_kernel(rows, clips, spatial, given, ring, *refs):
    stream, mods, *refs = refs
    if given:
        hidden0, hidden1, *refs = refs
    weights, *refs = refs
    if ring:
        shard, *refs = refs
    stream_out, stream_low, branch_out, squares, qkv0, qkv1, att0, att1, *refs = refs
    if not given:
        hidden0, hidden1, *refs = refs
    if ring:
        gathered, *refs = refs
    w, w_sem, part_out, part_in, keep, x_sems, *refs = refs
    pieces = Pieces(rows, clips, stream.shape[0], spatial)
    inner, count = att0.shape[1], stream.shape[0]
    gather = Gather(ring, shard, gathered, refs) if ring else None
    step = gather.step if ring else (lambda: None)
    greeted = gather.neighbours() if ring else []
    greet([{"tensor": 1 - lax.axis_index("tensor")}] + greeted)
    load = pltpu.make_async_copy(weights, w, w_sem)
    load.start()
    step()
    arrivals = []
    for i in range(pieces.number if not given else 0):
        normed = norm_rows(stream[pieces.at(i), :].astype(f32))
        value = pieces.plus(pieces.times(normed, mods, 1, i, 1.0), mods, 0, i)
        hidden0[pieces.at(i), :] = value.astype(bf16)
        arrivals.append(pieces.swap(hidden0, hidden1, x_sems, i, 0))
    load.wait()
    w_qkv = w[:, : 3 * inner]
    qkv0[...] = dot(hidden0[...], w_qkv).astype(bf16)
    step()

    def heads(group):
        residue = 0 if spatial else count // FRAMES

        def take(refs, cols):
            values = [refs[i][pl.ds(r, n), cols] for i, r, n in group]
            return values[0] if len(values) == 1 else jnp.concatenate(values, axis=0)

        for start in range(0, inner, HEAD_DIM):
            q, k, v = (
                take((qkv0, qkv1), slice(p * inner + start, p * inner + start + HEAD_DIM)) for p in range(3)
            )
            value = dot(softmax_scores(q, k, residue).astype(bf16), v).astype(bf16)
            at = 0
            for i, r, n in group:
                (att0, att1)[i][pl.ds(r, n), start : start + HEAD_DIM] = value[at : at + n]
                at += n

    swaps = []
    w_proj = w[:, 3 * inner :]
    if spatial:
        tokens = pieces.count
        for r in range(pieces.number):
            if not given:
                arrivals[r].wait_recv()
            at = pieces.at(r)
            qkv1[at, :] = dot(hidden1[at, :], w_qkv).astype(bf16)
            heads([(0, r * tokens, tokens), (1, r * tokens, tokens)])
            part_out[at, :] = dot_nt(att1[at, :], w_proj).astype(bf16)
            swaps.append(pieces.swap(part_out, part_in, x_sems, r, pieces.number))
            step()
    else:
        heads([(0, 0, count)])
        for arrival in arrivals:
            arrival.wait_recv()
        qkv1[...] = dot(hidden1[...], w_qkv).astype(bf16)
        heads([(1, 0, count)])
        for i in range(pieces.number):
            at = pieces.at(i)
            part_out[at, :] = dot_nt(att1[at, :], w_proj).astype(bf16)
            swaps.append(pieces.swap(part_out, part_in, x_sems, i, pieces.number))
    keep[...] = dot_nt(att0[...], w_proj)
    step()
    sublayer_end(
        pieces, stream, mods, 2, keep, part_in, swaps,
        (stream_out, stream_low, branch_out, squares, rows, clips),
    )
    if ring:
        gather.finish()
    for copy in arrivals + swaps:
        copy.wait_send()


def mlp_kernel(rows, clips, spatial, *refs):
    stream, mods, weights, *refs = refs
    if not spatial:
        low, *refs = refs
    stream_out, stream_low, branch_out, squares, hidden0, hidden1, pre0, pre1, act0, act1, *refs = refs
    landed, *refs = refs
    w, w_sem, part_out, part_in, keep, x_sems, *refs = refs
    if spatial:
        low, *refs = refs
    regroup = Exchange(low, landed, refs)
    greeted = [{"tensor": 1 - lax.axis_index("tensor")}] + regroup.others()
    pieces = Pieces(rows, clips, stream.shape[0], spatial)
    inner = act0.shape[1]
    greet(greeted)
    load = pltpu.make_async_copy(weights, w, w_sem)
    load.start()
    arrivals, swaps = [], []
    for i in range(pieces.number):
        normed = norm_rows(stream[pieces.at(i), :].astype(f32))
        value = pieces.plus(pieces.times(normed, mods, 4, i, 1.0), mods, 3, i)
        hidden0[pieces.at(i), :] = value.astype(bf16)
        arrivals.append(pieces.swap(hidden0, hidden1, x_sems, i, 0))
    if not spatial:
        regroup.start()
    load.wait()
    block = 768 if inner % 768 == 0 else inner

    def through(hidden, pre, act, at):
        for start in range(0, inner, block):
            cols = slice(start, start + block)
            value = dot(hidden[at, :], w[:, cols])
            pre[at, cols] = value
            act[at, cols] = gelu_tanh(value).astype(bf16)

    w_down = w[:, inner:]
    everything = pl.ds(0, stream.shape[0])
    through(hidden0, pre0, act0, everything)
    for i, arrival in enumerate(arrivals):
        at = pieces.at(i)
        arrival.wait_recv()
        through(hidden1, pre1, act1, at)
        part_out[at, :] = dot_nt(act1[at, :], w_down).astype(bf16)
        swaps.append(pieces.swap(part_out, part_in, x_sems, i, pieces.number))
    keep[...] = dot_nt(act0[...], w_down)
    sublayer_end(
        pieces, stream, mods, 5, keep, part_in, swaps,
        (stream_out, stream_low, branch_out, squares, rows, clips), regroup if spatial else None,
    )
    regroup.finish()
    for copy in arrivals + swaps:
        copy.wait_send()


def forward_call(layer, attends, stream, mod, weights, hidden=None, shard=None, ride=None):
    rows, clips, count = layer.rows, layer.clips, layer.rows * layer.tokens
    width = weights.shape[0]
    inner = weights.shape[1] // (4 if attends else 2)
    number = rows if layer.spatial else 2
    ring = lax.axis_size("dp") // 4 if shard is not None else 0
    vmem, anywhere = pl.BlockSpec(memory_space=pltpu.VMEM), pl.BlockSpec(memory_space=pl.ANY)
    args, specs = [stream, mod.reshape(-1, width)], [vmem, vmem]
    if hidden:
        args, specs = args + list(hidden), specs + [vmem, vmem]
    args, specs = args + [weights], specs + [anywhere]
    shape = jax.ShapeDtypeStruct
    outs = [shape((count, width), kind) for kind in (f32, bf16, f32)]
    outs.append(shape((2, rows // clips, 128), f32))
    if attends:
        outs += [shape((count, 3 * inner), bf16)] * 2 + [shape((count, inner), bf16)] * 2
        if not hidden:
            outs += [shape((count, width), bf16)] * 2
    else:
        outs += [shape((count, width), bf16)] * 2
        outs += [shape((count, inner), f32)] * 2 + [shape((count, inner), bf16)] * 2
    out_specs = [vmem] * len(outs)
    scratch = [pltpu.VMEM(weights.shape, bf16), pltpu.SemaphoreType.DMA]
    scratch += [pltpu.VMEM((count, width), bf16)] * 2 + [pltpu.VMEM((count, width), f32)]
    scratch += [pltpu.SemaphoreType.DMA((2, 2 * number))]
    if ring:
        args, specs = args + [shard], specs + [anywhere]
        outs.append(shape((4 * ring,) + shard.shape, bf16))
        out_specs.append(anywhere)
        scratch += Gather.scratch(ring)
    size = lax.axis_size("dp")
    blocks = shape((size, count // size, width), bf16)
    if ride is not None:
        args, specs = args + [ride], specs + [vmem]
    if not attends:
        outs.append(blocks)
        out_specs.append(vmem)
        scratch += [pltpu.VMEM(blocks.shape, bf16)] if layer.spatial else []
        scratch += Exchange.scratch(size)
    if attends:
        kernel = functools.partial(attention_kernel, rows, clips, layer.spatial, bool(hidden), ring)
    else:
        kernel = functools.partial(mlp_kernel, rows, clips, layer.spatial)
    return pl.pallas_call(
        kernel,
        in_specs=specs,
        out_specs=out_specs,
        out_shape=outs,
        scratch_shapes=scratch,
        cost_estimate=pl.CostEstimate(flops=1 << 35, bytes_accessed=1 << 25, transcendentals=0),
        compiler_params=pltpu.CompilerParams(
            collective_id=6 + 2 * attends + layer.spatial, has_side_effects=True, vmem_limit_bytes=60 << 20
        ),
    )(*args)


def gelu_slope(value):
    root, cubic = 0.7978845608028654, 0.044715
    square = value * value
    bend = jnp.tanh(root * (value + cubic * square * value))
    return 0.5 * (1.0 + bend) + 0.5 * value * (1.0 - bend * bend) * root * (1.0 + 3.0 * cubic * square)


def mlp_back_kernel(rows, clips, extra, packed, rides, *refs):
    grad, branch, stream, mods, hidden0, hidden1, pre0, pre1, act0, act1, weights, *refs = refs
    others, refs = refs[:extra], refs[extra:]
    if rides:
        ride, *refs = refs
    grad_out, dmod_out, *refs = refs
    gw_outs, refs = refs[: 2 - packed], refs[2 - packed :]
    other_outs, refs = refs[:extra], refs[extra:]
    if rides:
        landed, *refs = refs
    w, w_sem, db0, db1, part_out, part_in, keep, dpre0, dpre1, gw, gw_sem, x_sems, *refs = refs
    inner = act0.shape[1]
    jobs = [
        Scatter(others[i], other_outs[i], refs[7 * i : 7 * i + 7], lambda j: j % 6 == 5) for i in range(extra)
    ]
    greeted = [{"tensor": 1 - lax.axis_index("tensor")}]
    if rides:
        exchange = Exchange(ride, landed, refs[7 * extra :])
        greeted += exchange.others()
    elif extra:
        greeted += jobs[0].neighbours()
    greet(greeted)
    load = pltpu.make_async_copy(weights, w, w_sem)
    load.start()
    db0[...] = (
        (spread(grad[...].astype(f32), rows, clips) * clip_rows(mods, clips, 5)).reshape(grad.shape).astype(bf16)
    )
    first = Swap(db0, db1, x_sems, 0)
    if rides:
        exchange.start()
    pipeline = Pipeline()
    pipeline.add(jobs)
    tick = pipeline.tick
    dgate = clip_sums(grad[...].astype(f32) * branch[...], rows, clips)
    load.wait()
    block = 768 if inner % 768 == 0 else inner

    def through(db, pre, dpre):
        for start in range(0, inner, block):
            cols = slice(start, start + block)
            dact = dot(db[...], w[:, inner + start : inner + start + block])
            dpre[:, cols] = (dact * gelu_slope(pre[:, cols])).astype(bf16)
        tick()

    tick()
    through(db0, pre0, dpre0)
    first.copy.wait_recv()
    through(db1, pre1, dpre1)
    part_out[...] = dot_nt(dpre1[...], w[:, :inner]).astype(bf16)
    second = Swap(part_out, part_in, x_sems, 1)
    tick()
    keep[...] = dot_nt(dpre0[...], w[:, :inner])
    tick()
    both = lambda a, b, cols: jnp.concatenate([a[:, cols], b[:, cols]], axis=0)
    whole = slice(0, grad.shape[1])
    stored = []
    for p, (left, right) in enumerate((((hidden0, hidden1), (dpre0, dpre1)), ((db0, db1), (act0, act1)))):
        tall = both(*left, whole)
        for start in range(0, inner, block):
            slot = len(stored) % 2
            if len(stored) > 1:
                stored[-2].wait()
            gw[slot] = dot_tn(tall, both(*right, slice(start, start + block))).astype(bf16)
            at = start + inner if packed and p else start
            out = gw_outs[0 if packed else p].at[:, pl.ds(at, block)]
            copy = pltpu.make_async_copy(gw.at[slot], out, gw_sem.at[slot])
            copy.start()
            stored.append(copy)
            if len(stored) % 2:
                tick()
    second.copy.wait_recv()
    result, dshift, dscale = norm_back_rows(
        grad[...], keep[...] + part_in[...].astype(f32), stream[...], clip_rows(mods, clips, 4), rows, clips
    )
    grad_out[...] = result
    for k, value in enumerate((dshift, dscale, dgate)):
        dmod_out[k * clips : (k + 1) * clips] = value
    pipeline.finish()
    if rides:
        exchange.finish()
    for copy in stored[-2:]:
        copy.wait()
    for exchange in (first, second):
        exchange.copy.wait_send()


def mlp_back_call(layer, grad, mod, stored, packed, others=(), ride=None):
    stream, branch, hidden, pre, active, weights = stored
    rows, clips, count = layer.rows, layer.clips, layer.rows * layer.tokens
    width, inner, ring = weights.shape[0], active[0].shape[1], lax.axis_size("dp") // 4
    share = width // (4 * ring)
    others = [g.reshape(ring, 2, 2, share, g.shape[1]) for g in others]
    vmem, anywhere = pl.BlockSpec(memory_space=pltpu.VMEM), pl.BlockSpec(memory_space=pl.ANY)
    args = [layer.flat(grad), layer.flat(branch), layer.flat(stream), mod.reshape(-1, width)]
    args += [*hidden, *pre, *active]
    specs = [vmem] * len(args) + [anywhere] * (1 + len(others))
    args += [weights, *others]
    shape = jax.ShapeDtypeStruct
    gw = [shape((width, 2 * inner), bf16)] if packed else [shape((width, inner), bf16)] * 2
    outs = [shape((count, width), f32), shape((3 * clips, width), f32)] + gw
    outs += [shape((share, g.shape[-1]), f32) for g in others]
    rides = ride is not None
    if rides:
        args, specs = args + [ride], specs + [vmem]
        outs.append(shape(ride.shape, bf16))
    block = 768 if inner % 768 == 0 else inner
    scratch = [pltpu.VMEM(weights.shape, bf16), pltpu.SemaphoreType.DMA]
    scratch += [pltpu.VMEM((count, width), bf16)] * 4 + [pltpu.VMEM((count, width), f32)]
    scratch += [pltpu.VMEM((count, inner), bf16)] * 2
    scratch += [pltpu.VMEM((2, width, block), bf16), pltpu.SemaphoreType.DMA((2,))]
    scratch += [pltpu.SemaphoreType.DMA((2, 2))]
    for g in others:
        scratch += Scatter.scratch(ring, share, g.shape[-1])
    if rides:
        scratch += Exchange.scratch(4 * ring)
    return pl.pallas_call(
        functools.partial(mlp_back_kernel, rows, clips, len(others), packed, rides),
        in_specs=specs,
        out_specs=[vmem, vmem] + [anywhere] * len(gw) + [vmem] * (len(others) + rides),
        out_shape=outs,
        scratch_shapes=scratch,
        cost_estimate=pl.CostEstimate(flops=1 << 35, bytes_accessed=1 << 25, transcendentals=0),
        compiler_params=pltpu.CompilerParams(
            collective_id=4 + layer.spatial, has_side_effects=True, vmem_limit_bytes=62 << 20
        ),
    )(*args)


def tail_kernel(count, pairs, *refs):
    grads, small = refs[:count], refs[count]
    outs, small_out = refs[count + 1 : 2 * count + 1], refs[2 * count + 1]
    scratch = refs[2 * count + 2 :]
    jobs = [
        Scatter(grads[i], outs[i], scratch[7 * i : 7 * i + 7], lambda j: j % 6 == 5)
        for i in range(count)
    ]
    total = SmallSum(pairs, small, small_out, scratch[7 * count :])
    greet(total.partners + [{"dp": jobs[0].after}, {"dp": jobs[0].before}])
    pipeline = Pipeline()
    total.tick()
    pipeline.add(jobs)
    for _ in range(len(pairs)):
        pipeline.tick()
        total.tick()
    pipeline.finish()
    total.finish()


def tail(grads, small):
    ring = lax.axis_size("dp") // 4
    grads = [grad.reshape(ring, 2, 2, -1, grad.shape[1]) for grad in grads]
    pairs = exchange_pairs()
    anywhere, vmem = pl.BlockSpec(memory_space=pl.ANY), pl.BlockSpec(memory_space=pltpu.VMEM)
    scratch = []
    for grad in grads:
        scratch += Scatter.scratch(ring, *grad.shape[3:])
    return pl.pallas_call(
        functools.partial(tail_kernel, len(grads), pairs),
        in_specs=[anywhere] * len(grads) + [vmem],
        out_specs=[vmem] * (len(grads) + 1),
        out_shape=[jax.ShapeDtypeStruct(grad.shape[3:], f32) for grad in grads]
        + [jax.ShapeDtypeStruct(small.shape, f32)],
        scratch_shapes=scratch + SmallSum.scratch(len(pairs), small.shape),
        compiler_params=pltpu.CompilerParams(
            collective_id=0, has_side_effects=True, vmem_limit_bytes=56 << 20
        ),
    )(*grads, small)


class Layer:
    def __init__(self, rows, tokens, clips, spatial, first_row):
        self.rows, self.tokens, self.clips, self.spatial = rows, tokens, clips, spatial
        self.first_row = first_row

    def by_row(self, table):
        if self.rows % self.clips == 0:
            width = table.shape[-1]
            spread = jnp.broadcast_to(table[None], (self.rows // self.clips, self.clips, width))
            return spread.reshape(self.rows, 1, width)
        start = lax.rem(self.first_row, self.clips)
        return lax.dynamic_slice_in_dim(table, start, self.rows, 0)[:, None, :]

    def by_clip(self, sums):
        width = sums.shape[-1]
        if self.rows % self.clips == 0:
            return jnp.sum(sums.reshape(self.rows // self.clips, self.clips, width), axis=0)
        start = lax.rem(self.first_row, self.clips)
        empty = jnp.zeros((self.clips, width), f32)
        return lax.dynamic_update_slice_in_dim(empty, sums, start, 0)

    def by_frame(self, entries):
        per_row = jnp.sum(entries * entries, axis=(1, 2))
        frames = max(self.rows // self.clips, 1)
        sums = jnp.sum(per_row.reshape(frames, -1), axis=1)
        if frames == FRAMES:
            return sums
        start = self.first_row // self.clips
        return lax.dynamic_update_slice_in_dim(jnp.zeros((FRAMES,), f32), sums, start, 0)

    def modulated(self, stream, mod, offset):
        normed = layer_norm(stream)[0]
        scale = 1.0 + self.by_row(mod[:, offset + 1])
        return (normed * scale + self.by_row(mod[:, offset])).astype(bf16)

    def flat(self, value):
        return value.reshape(self.rows * self.tokens, value.shape[-1])

    def full(self, value):
        return value.reshape(self.rows, self.tokens, value.shape[-1])

    def attend(self, kernel, operands, widths):
        if self.spatial:
            views = [[self.full(value) for value in group] for group in operands]
            return [self.flat(v) for v in attend_call(kernel, 0, views, widths)]
        count = self.rows * self.tokens
        out = []
        for i in range(len(operands[0])):
            views = [[group[i][None]] for group in operands]
            out.append(attend_call(kernel, count // FRAMES, views, widths)[0][0])
        return out

    def attention(self, stream, mod, weights, pump, hidden=None):
        inner = weights.shape[1] // 4
        if hidden is None:
            hidden = gather_tokens(self.modulated(stream, mod, 0))
        hidden = [self.flat(h) for h in hidden]
        w_qkv, w_proj = weights[:, : 3 * inner], weights[:, 3 * inner :]
        qkv = [dot(h, w_qkv).astype(bf16) for h in hidden]
        attended = self.attend(attend_kernel, [qkv], inner)
        attended[-1] = pump(attended[-1])
        partial = [self.full(dot_nt(a, w_proj)) for a in attended]
        branch = scatter_tokens(partial)
        branch = pump(branch)
        gated = self.by_row(mod[:, 2]) * branch
        return stream + gated, gated, (stream, branch, hidden, qkv, attended, w_qkv, w_proj)

    def mlp(self, stream, mod, weights, pump):
        inner = weights.shape[1] // 2
        hidden = [self.flat(h) for h in gather_tokens(self.modulated(stream, mod, 3))]
        hidden[-1] = pump(hidden[-1])
        w_up, w_down = weights[:, :inner], weights[:, inner:]
        pre = [dot(h, w_up) for h in hidden]
        active = [gelu_tanh(p).astype(bf16) for p in pre]
        branch = scatter_tokens([self.full(dot_nt(a, w_down)) for a in active])
        branch = pump(branch)
        gated = self.by_row(mod[:, 5]) * branch
        return stream + gated, gated, (stream, branch, hidden, pre, active, w_up, w_down)

    def branch_back(self, grad, mod, offset, branch):
        grad_branch = (grad * self.by_row(mod[:, offset + 2])).astype(bf16)
        grad_gate = self.by_clip(jnp.sum(grad * branch, axis=1))
        return [self.flat(g) for g in gather_tokens(grad_branch)], grad_gate

    def norm_back(self, grad, grad_hidden, stream, mod, offset):
        normed, inverse = layer_norm(stream)
        grad_normed = grad_hidden * (1.0 + self.by_row(mod[:, offset + 1]))
        centered = grad_normed - jnp.mean(grad_normed, axis=-1, keepdims=True)
        grad_in = inverse * (
            centered - normed * jnp.mean(grad_normed * normed, axis=-1, keepdims=True)
        )
        shift = self.by_clip(jnp.sum(grad_hidden, axis=1))
        scale = self.by_clip(jnp.sum(grad_hidden * normed, axis=1))
        return grad + grad_in, shift, scale

    def mlp_back(self, grad, mod, stored, split, pump):
        stream, branch, hidden, pre, active, w_up, w_down = stored
        grad_branch, gate = self.branch_back(grad, mod, 3, branch)
        grad_branch[-1] = pump(grad_branch[-1])
        grad_pre = [
            jax.vjp(gelu_tanh, p)[1](dot(g, w_down))[0].astype(bf16)
            for p, g in zip(pre, grad_branch)
        ]
        grad_pre[-1] = pump(grad_pre[-1])
        grad_hidden = scatter_tokens([self.full(dot_nt(g, w_up)) for g in grad_pre])
        grad_w = weight_grad((hidden, grad_pre), (grad_branch, active), split)
        grad_hidden, *grad_w = tie(grad_hidden, *grad_w)
        grad_hidden = pump(grad_hidden)
        grad, shift, scale = self.norm_back(grad, grad_hidden, stream, mod, 3)
        return grad, jnp.stack([shift, scale, gate], axis=1), grad_w

    def attention_back(self, grad, mod, stored, split, pump):
        stream, branch, hidden, qkv, attended, w_qkv, w_proj = stored
        grad_branch, gate = self.branch_back(grad, mod, 0, branch)
        grad_branch[-1] = pump(grad_branch[-1])
        grad_att = [dot(g, w_proj).astype(bf16) for g in grad_branch]
        grad_qkv = self.attend(attend_back_kernel, [qkv, grad_att], w_qkv.shape[1])
        grad_qkv[-1] = pump(grad_qkv[-1])
        grad_hidden = scatter_tokens([self.full(dot_nt(g, w_qkv)) for g in grad_qkv])
        grad_w = weight_grad((hidden, grad_qkv), (grad_branch, attended), split)
        grad_hidden, *grad_w = tie(grad_hidden, *grad_w)
        grad_hidden = pump(grad_hidden)
        grad, shift, scale = self.norm_back(grad, grad_hidden, stream, mod, 0)
        return grad, jnp.stack([shift, scale, gate], axis=1), grad_w


def to_places(stream, kind=f32):
    return lax.all_to_all(
        stream.astype(bf16), "dp", split_axis=1, concat_axis=0, tiled=True
    ).astype(kind)


def to_frames(stream):
    return lax.all_to_all(stream.astype(bf16), "dp", split_axis=0, concat_axis=1, tiled=True)


def pack(first, second):
    return jnp.concatenate([first.reshape(first.shape[0], -1), second.T], axis=1)


def gather_weights(first, second):
    return lax.all_gather(pack(first, second), "dp", axis=0, tiled=True)


def norm_rows(value):
    centered = value - jnp.mean(value, axis=-1, keepdims=True)
    return centered * lax.rsqrt(jnp.mean(centered * centered, axis=-1, keepdims=True) + epsilon)


def head_kernel(
    ring, clips, pairs, shard, small, video, out, small_out, hidden, other,
    slots, landed_small, own_sem, send_sem, recv_sem, pair_send, pair_recv, x_send, x_recv,
):
    size, me = 4 * ring, lax.axis_index("dp")
    tensor = lax.axis_index("tensor")
    after, before = lax.rem(me + 4, size), lax.rem(me + size - 4, size)
    beside, core = me ^ 2, me ^ 1
    exchange = lax.axis_size("tensor") == 2
    barrier = pltpu.get_barrier_semaphore()
    partners = [{"dp": me ^ stride} for stride in pairs]
    greeted = partners + [{"dp": after}, {"dp": before}]
    if exchange:
        greeted.append({"tensor": 1 - tensor})
    for partner in greeted:
        pl.semaphore_signal(barrier, inc=1, device_id=partner, device_id_type=MESH)
    pl.semaphore_wait(barrier, len(greeted))
    keep = pltpu.make_async_copy(shard, out.at[me], own_sem)
    keep.start()
    sent = []

    def send(source, target, out_sem, in_sem, partner):
        copy = pltpu.make_async_remote_copy(
            src_ref=source, dst_ref=target, send_sem=out_sem, recv_sem=in_sem,
            device_id=partner, device_id_type=MESH,
        )
        copy.start()
        sent.append(copy)
        return copy

    def pass_on(source, place, slot, partner):
        send(source, out.at[place], send_sem.at[slot], recv_sem.at[slot], {"dp": partner})

    def landed(place, slot):
        pltpu.make_async_remote_copy(
            src_ref=out.at[place], dst_ref=out.at[place],
            send_sem=send_sem.at[slot], recv_sem=recv_sem.at[slot],
            device_id={"dp": core}, device_id_type=MESH,
        ).wait_recv()

    flying = []

    def pair_step(k):
        if k == 0:
            slots[0] = small[...]
        else:
            flying[k - 1].wait_recv()
            slots[k] = slots[k - 1] + landed_small[k - 1]
        if k < len(partners):
            flying.append(
                send(slots.at[k], landed_small.at[k], pair_send.at[k], pair_recv.at[k], partners[k])
            )

    pair_step(0)
    step = 1
    for k in range(ring):
        place = lax.rem(me + size - 4 * k, size)
        if k:
            landed(place, k - 1)
        source = shard if k == 0 else out.at[place]
        if k < ring - 1:
            pass_on(source, place, k, after)
        pass_on(source, place, ring + k, beside)
        pass_on(source, place, 2 * ring + k, core)
        if k:
            place = lax.rem((me ^ 2) + size - 4 * (k - 1), size)
            landed(place, ring + k - 1)
            pass_on(out.at[place], place, 3 * ring + k - 1, core)
        if step <= len(partners):
            pair_step(step)
            step += 1
    while step <= len(partners):
        pair_step(step)
        step += 1
    small_out[...] = slots[len(partners)]
    if exchange:
        rows = video.shape[0]
        for r in range(rows):
            clip = r % clips if rows % clips == 0 else lax.rem(me * rows + r, clips)
            shift = slots[len(partners), pl.ds(6 * clip, 1), :]
            scale = slots[len(partners), pl.ds(6 * clip + 1, 1), :]
            normed = norm_rows(video[r].astype(f32))
            hidden[r] = (normed * (1.0 + scale) + shift).astype(bf16)
        swapped = send(hidden, other, x_send, x_recv, {"tensor": 1 - tensor})
    place = lax.rem((me ^ 2) + size - 4 * (ring - 1), size)
    landed(place, 2 * ring - 1)
    pass_on(out.at[place], place, 4 * ring - 1, core)
    for k in range(ring):
        landed(lax.rem(core + size - 4 * k, size), 2 * ring + k)
        landed(lax.rem((core ^ 2) + size - 4 * k, size), 3 * ring + k)
    keep.wait()
    if exchange:
        swapped.wait_recv()
    for copy in sent:
        copy.wait_send()


def head(shard, small, video, clips):
    ring = lax.axis_size("dp") // 4
    rows, cols = shard.shape
    pairs = [1 << bit for bit in range(lax.axis_size("dp").bit_length() - 1)]
    count = len(pairs)
    vmem, anywhere = pl.BlockSpec(memory_space=pltpu.VMEM), pl.BlockSpec(memory_space=pl.ANY)
    full, total, mine, other = pl.pallas_call(
        functools.partial(head_kernel, ring, clips, pairs),
        in_specs=[anywhere, vmem, vmem],
        out_specs=[anywhere, vmem, vmem, vmem],
        out_shape=[
            jax.ShapeDtypeStruct((4 * ring, rows, cols), bf16),
            jax.ShapeDtypeStruct(small.shape, f32),
            jax.ShapeDtypeStruct(video.shape, bf16),
            jax.ShapeDtypeStruct(video.shape, bf16),
        ],
        scratch_shapes=[
            pltpu.VMEM((count + 1,) + small.shape, f32),
            pltpu.VMEM((count,) + small.shape, f32),
            pltpu.SemaphoreType.DMA,
            pltpu.SemaphoreType.DMA((4 * ring,)),
            pltpu.SemaphoreType.DMA((4 * ring,)),
            pltpu.SemaphoreType.DMA((count,)),
            pltpu.SemaphoreType.DMA((count,)),
            pltpu.SemaphoreType.DMA,
            pltpu.SemaphoreType.DMA,
        ],
        cost_estimate=pl.CostEstimate(flops=1 << 35, bytes_accessed=8 * ring * rows * cols, transcendentals=0),
        compiler_params=pltpu.CompilerParams(
            collective_id=1, has_side_effects=True, vmem_limit_bytes=32 << 20
        ),
    )(shard, small, video)
    hidden = [mine, other] if lax.axis_size("tensor") == 2 else None
    return full.reshape(4 * ring * rows, cols), total, hidden


def assemble_kernel(ring, own, *refs):
    hops, beside, core, out, sems = refs[: ring - 1], *refs[ring - 1 :]
    size, me = 4 * ring, lax.axis_index("dp")
    copies = []

    def put(source, place):
        copy = pltpu.make_async_copy(source, out.at[place], sems.at[len(copies)])
        copy.start()
        copies.append(copy)

    for k in range(ring):
        back = lambda device: lax.rem(device + size - 4 * k, size)
        put(own if k == 0 else hops[k - 1], back(me))
        put(beside.at[k], back(me ^ 2))
        put(core.at[k], back(me ^ 1))
        put(core.at[ring + k], back(me ^ 3))
    for copy in copies:
        copy.wait()


class WeightGather:
    def __init__(self, shard):
        self.size = lax.axis_size("dp")
        self.ring = self.size // 4
        self.pieces, self.stage = [shard], 0
        self.begin()

    def begin(self):
        if self.stage < self.ring - 1:
            links = [(i, (i + 4) % self.size) for i in range(self.size)]
            self.wait = lax.ppermute(self.pieces[-1], "dp", links)
        elif self.stage == self.ring - 1:
            self.column = jnp.stack(self.pieces)
            self.wait = swap(self.column, "dp", 2, self.size)
        else:
            self.wait = swap(jnp.concatenate([self.column, self.pieces[-1]]), "dp", 1, self.size)

    def step(self, value=None):
        if self.stage > self.ring:
            return value
        if value is not None:
            value, self.wait = tie(value, self.wait)
        self.pieces.append(self.wait)
        self.stage += 1
        if self.stage <= self.ring:
            self.begin()
        return value

    def finish(self):
        while self.stage <= self.ring:
            self.step()
        rows, cols = self.pieces[0].shape
        anywhere = pl.BlockSpec(memory_space=pl.ANY)
        full = pl.pallas_call(
            functools.partial(assemble_kernel, self.ring),
            in_specs=[anywhere] * (self.ring + 2),
            out_specs=pl.BlockSpec(memory_space=pltpu.VMEM),
            out_shape=jax.ShapeDtypeStruct((self.size, rows, cols), bf16),
            scratch_shapes=[pltpu.SemaphoreType.DMA((self.size,))],
            compiler_params=pltpu.CompilerParams(vmem_limit_bytes=32 << 20),
        )(*self.pieces)
        return full.reshape(self.size * rows, cols)


def scatter_grads(grad_w):
    return lax.psum_scatter(grad_w, "dp", scatter_dimension=0, tiled=True)


def unpack(local, first, second):
    local = local.astype(f32)
    cut = local.shape[1] - second.shape[0]
    return local[:, :cut].reshape(first.shape), local[:, cut:].T


def finish_spatial(gw_mlp, gw_attn, dmod_attn, dmod_mlp):
    small = jnp.concatenate([dmod_attn.reshape(-1), dmod_mlp.reshape(-1)]).reshape(-1, 128)
    return tail([*gw_mlp, gw_attn], small)


def body(
    video_in,
    condition,
    adaln_spatial,
    qkv_spatial,
    proj_spatial,
    up_spatial,
    down_spatial,
    adaln_temporal,
    qkv_temporal,
    proj_temporal,
    up_temporal,
    down_temporal,
    grad_output,
):
    rows, tokens, width = video_in.shape
    clips = condition.shape[0]
    dp, me = lax.axis_size("dp"), lax.axis_index("dp")
    spatial = Layer(rows, tokens, clips, True, me * rows)
    temporal = Layer(rows * dp, tokens // dp, clips, False, 0)

    w_mlp_s = gather_weights(up_spatial, down_spatial)
    w_mlp_t = gather_weights(up_temporal, down_temporal)

    share = adaln_spatial.shape[0]
    cond_rows = lax.dynamic_slice_in_dim(condition, me * share, share, 1)
    silu_rows, silu_pull = jax.vjp(jax.nn.silu, cond_rows)
    silu_low = silu_rows.astype(bf16)
    flat_s = adaln_spatial.reshape(share, -1)
    flat_t = adaln_temporal.reshape(share, -1)
    mods = jnp.stack([dot(silu_low, flat_s), dot(silu_low, flat_t)]).reshape(-1, width)
    w_attn_s, mods, hidden = head(pack(qkv_spatial, proj_spatial), mods, video_in, clips)

    keep = lambda value: value
    mod_s, mod_t = mods.reshape(2, clips, 6, width)
    fused = lax.axis_size("tensor") == 2 and rows % clips == 0 and tokens % (8 * dp) == 0
    if fused:
        flat = video_in.reshape(rows * tokens, width)
        mine = [spatial.flat(h) for h in hidden]
        s1, _, b1, q1, *kept1, w_attn_t = forward_call(
            spatial, True, flat, mod_s, w_attn_s, mine, pack(qkv_temporal, proj_temporal)
        )
        w_attn_t = w_attn_t.reshape(width, -1)
        kept1 = (flat, b1, mine, kept1[:2], kept1[2:])
        s2, _, b2, q2, *kept2, placed = forward_call(spatial, False, s1, mod_s, w_mlp_s)
        kept2 = (s1, b2, kept2[:2], kept2[2:4], kept2[4:])
        placed = placed.reshape(-1, width)
        by_place = grad_output.astype(bf16).reshape(rows, dp, tokens // dp, width)
        by_place = jnp.moveaxis(by_place, 1, 0).reshape(dp, -1, width)
        s3, _, b3, q3, *kept3 = forward_call(temporal, True, placed, mod_t, w_attn_t)
        kept3 = (placed, b3, kept3[4:], kept3[:2], kept3[2:4])
        _, low4, b4, q4, *kept4, grad = forward_call(temporal, False, s3, mod_t, w_mlp_t, ride=by_place)
        grad = grad.reshape(-1, width)
        kept4 = (s3, b4, kept4[:2], kept4[2:4], kept4[4:])
        spots = []
        for layer, values in ((spatial, (q1, q2)), (temporal, (q3, q4))):
            for value in values:
                empty = jnp.zeros((2, FRAMES), f32)
                spots.append(
                    lax.dynamic_update_slice_in_dim(empty, value[:, :, 0], layer.first_row // clips, 1)
                )
        squares = jnp.concatenate([jnp.stack([v[i] for v in spots]) for i in range(2)])
    else:
        stream0 = video_in.astype(f32)
        shard, mods = tie(pack(qkv_temporal, proj_temporal), mods)
        mod_s, mod_t = mods.reshape(2, clips, 6, width)
        later = WeightGather(shard)
        s1, g1, kept1 = spatial.attention(stream0, mod_s, w_attn_s, later.step, hidden)
        s2, g2, kept2 = spatial.mlp(s1, mod_s, w_mlp_s, later.step)
        placed = later.step(to_places(s2))
        w_attn_t = later.finish()
        placed, grad_output = tie(placed, grad_output)
        grad = to_places(grad_output)
        s3, g3, kept3 = temporal.attention(placed, mod_t, w_attn_t, keep)
        s4, g4, kept4 = temporal.mlp(s3, mod_t, w_mlp_t, keep)
        video_out = to_frames(s4)
        squares = jnp.stack(
            [spatial.by_frame(v) for v in (s1, s2)]
            + [temporal.by_frame(v) for v in (s3, s4)]
            + [spatial.by_frame(v) for v in (g1, g2)]
            + [temporal.by_frame(v) for v in (g3, g4)]
        )
    by_span = lambda dmod: jnp.moveaxis(dmod.reshape(3, clips, width), 0, 1)
    if fused:
        grad, dmod4, gw4, by_frame = mlp_back_call(
            temporal, grad, mod_t, (*kept4[:5], w_mlp_t), True, ride=low4.reshape(dp, -1, width)
        )
        framed = lambda blocks: jnp.moveaxis(blocks.reshape(dp, rows, -1, width), 0, 1)
        video_out = framed(by_frame).reshape(video_in.shape)
        own4 = scatter_grads(gw4)
        dmod3, gw3, by_frame = attention_back_call(temporal, grad, mod_t, (*kept3[:5], w_attn_t))
        grad = framed(by_frame).reshape(-1, width)
    else:
        grad, dmod4, (gw4,) = temporal.mlp_back(grad, mod_t, kept4, False, keep)
        own4 = scatter_grads(gw4)
        grad, dmod3, (gw3,) = temporal.attention_back(grad, mod_t, kept3, False, keep)
        own3 = scatter_grads(gw3)
    if fused:
        grad, dmod2, up, down, own3 = mlp_back_call(
            spatial, grad, mod_s, (*kept2[:5], w_mlp_s), False, (gw3,)
        )
        line = jnp.pad(squares.reshape(1, -1), ((0, 0), (0, width - squares.size)))
        small = jnp.concatenate([dmod2, dmod3, dmod4, line], axis=0)
        grad, grad_up_s, down_s, *own1, late, early = attention_back_call(
            spatial, grad, mod_s, (*kept1[:5], w_attn_s), (up, down), small
        )
        grad = spatial.full(grad)
        own1 = jnp.concatenate(own1, axis=1)
        dmod1 = by_span(late)
        dmod2, dmod3, dmod4 = [by_span(early[3 * clips * i : 3 * clips * (i + 1)]) for i in range(3)]
        squares = early[9 * clips, : squares.size].reshape(8, FRAMES)
    else:
        early = AllSum(
            jnp.concatenate([dmod3.reshape(-1), dmod4.reshape(-1), squares.reshape(-1)]).reshape(-1, 128)
        )
        grad = early.step(to_frames(grad).astype(f32))
        grad, dmod2, gw2 = spatial.mlp_back(grad, mod_s, kept2, True, early.step)
        grad, own4 = tie(grad, own4)
        grad, dmod1, (gw1,) = spatial.attention_back(grad, mod_s, kept1, False, early.step)
        grad_up_s, down_s, own1, late = finish_spatial(gw2, gw1, dmod1, dmod2)
        late = late.reshape(2, clips, 3, width)
        dmod1, dmod2 = late[0], late[1]
        cut = clips * 3 * width
        flat_early = early.finish().reshape(-1)
        dmod3 = flat_early[:cut].reshape(clips, 3, width)
        dmod4 = flat_early[cut : 2 * cut].reshape(clips, 3, width)
        squares = flat_early[2 * cut :].reshape(8, FRAMES)
    grad_up_t, grad_down_t = unpack(own4, up_temporal, down_temporal)
    grad_qkv_t, grad_proj_t = unpack(own3, qkv_temporal, proj_temporal)
    grad_down_s = down_s.T
    grad_qkv_s, grad_proj_s = unpack(own1, qkv_spatial, proj_spatial)
    frame_rms = jnp.sqrt(squares / (clips * PATCHES * width))
    shift_grad = jnp.stack([d[:, 0] for d in (dmod1, dmod2, dmod3, dmod4)])
    silu_wide = silu_low.astype(f32)

    def adaln_back(flat, dmod_attn, dmod_mlp, shape):
        dmod = jnp.concatenate([dmod_attn, dmod_mlp], axis=1).reshape(clips, -1)
        grad_w = jnp.sum(silu_wide[:, :, None] * dmod[:, None, :], axis=0).reshape(shape)
        back = lax.dot_general(
            dmod, flat.astype(f32), (((1,), (1,)), ((), ())), precision=highest
        )
        return grad_w, back

    adaln_t_grad, back_t = adaln_back(flat_t, dmod3, dmod4, adaln_temporal.shape)
    adaln_s_grad, back_s = adaln_back(flat_s, dmod1, dmod2, adaln_spatial.shape)
    condition_grad = silu_pull(back_s + back_t)[0]
    return (
        video_out,
        grad,
        condition_grad,
        adaln_s_grad,
        grad_qkv_s,
        grad_proj_s,
        grad_up_s,
        grad_down_s,
        adaln_t_grad,
        grad_qkv_t,
        grad_proj_t,
        grad_up_t,
        grad_down_t,
        frame_rms,
        shift_grad,
    )


def solution(mesh):
    return jax.shard_map(
        body,
        mesh=mesh,
        in_specs=(
            P("dp", "tensor", None),
            P(),
            P("dp", None, None),
            P("dp", None, "tensor"),
            P("tensor", "dp"),
            P("dp", "tensor"),
            P("tensor", "dp"),
            P("dp", None, None),
            P("dp", None, "tensor"),
            P("tensor", "dp"),
            P("dp", "tensor"),
            P("tensor", "dp"),
            P("dp", "tensor", None),
        ),
        out_specs=(
            P("dp", "tensor", None),
            P("dp", "tensor", None),
            P(None, "dp"),
            P("dp", None, None),
            P("dp", None, "tensor"),
            P("tensor", "dp"),
            P("dp", "tensor"),
            P("tensor", "dp"),
            P("dp", None, None),
            P("dp", None, "tensor"),
            P("tensor", "dp"),
            P("dp", "tensor"),
            P("tensor", "dp"),
            P(),
            P(),
        ),
        check_vma=False,
    )
```
